512 devices in a mesh: gx: 32 (over x_hi, z, core), gy: 16 (over y, x_lo).
Axes of the slice: x: 4 (x_hi: 2, x_lo: 2; x = x_hi * 2 + x_lo), y: 8, z: 8, core: 2. Of those that a mesh axis runs over, the one named last changes fastest.
Arguments:
- coords: float32 [32, 16, 3, 1024], P('gx', 'gy'), may hold values from 0 to 1
- multipoles: float32 [32, 16, 10, 1024], P('gx', 'gy'), may hold values from -3 to 3
- face_atoms: int32 [32, 16, 3, 512], P('gx', 'gy'), may hold values from 0 to 1023, as said below
- tile_pairs: int32 [32, 16, 2, 32], P('gx', 'gy'), may hold values from 0 to 19, as said below
- tile_count: int32 [32, 16], P('gx', 'gy'), may hold values from 16 to 32
- frame_atoms: int32 [32, 16, 3, 1024], P('gx', 'gy'), may hold values from 0 to 2559, as said below
- send_list: int32 [32, 16, 3, 128], P('gx', 'gy'), may hold values from 0 to 511, as said below
- send_count: int32 [32, 16, 3], P('gx', 'gy'), may hold values from 42 to 128
Outputs:
- forces: float32 [32, 16, 3, 1024], P('gx', 'gy')
The draws below stay inside these ranges and needn't reach their ends.
Inputs may be any that keep to these rules, and one draw needn't show every extreme that they name: `face_atoms`: within one set of one domain the 512 atoms are distinct. `tile_pairs`: row 0 is below 8, row 1 is at least row 0; the tiles of one domain are distinct pairs of blocks; every block of imported atoms is the row 1 block of some live tile. `frame_atoms`: A frame atom differs from its own atom; a frame atom in an imported set is one of the live entries of that set's send list, and every live entry of a send list is the frame atom of some owned atom. `send_list`: the 128 entries of one list are distinct.
All inputs are finite; a program needn't handle non-finite values.
Results may differ from the reference program's by a relative error of at most 0.0003.
Values sent between devices are 32-bit elements; how exact they have to be, the bound alone decides.
A program may use at most 64 MiB of HBM per device.

```python
import jax
import jax.numpy as jnp
import numpy as np
from jax import lax

OWN = 1024
TILES = 32
MPOLE = 10
HALO = 512
SEND = 128
POOL = 2560
DOMX = 32
DOMY = 16


def own_table():
    leading = []
    trailing = []
    for near_id in range(OWN // 128):
        for far_id in range(near_id, OWN // 128):
            leading.append(near_id)
            trailing.append(far_id)
    return np.array([leading, trailing], dtype=np.int32)


def draw_face_atoms(key, part):
    subkeys = jax.random.split(key, DOMX * DOMY * 3)
    chosen = jax.vmap(lambda subkey: jax.random.permutation(subkey, OWN)[:HALO])(subkeys)
    return chosen.reshape(DOMX, DOMY, 3, HALO).astype(jnp.int32)


def device_tiles(subkey):
    own_blocks = OWN // 128
    halo_blocks = 3 * HALO // 128
    near_key, rest_key = jax.random.split(subkey, 2)
    near_halo = jax.random.randint(near_key, (halo_blocks,), 0, own_blocks)
    far_halo = own_blocks + jnp.arange(halo_blocks, dtype=jnp.int32)
    pair_table = jnp.asarray(own_table())
    rest = jax.random.permutation(rest_key, pair_table.shape[1])[:TILES - halo_blocks]
    picked = jnp.take(pair_table, rest, axis=1)
    leading = jnp.concatenate([near_halo.astype(jnp.int32), picked[0]])
    trailing = jnp.concatenate([far_halo, picked[1]])
    return jnp.stack([leading, trailing])


def draw_tile_pairs(key, part):
    subkeys = jax.random.split(key, DOMX * DOMY)
    tiles = jax.vmap(device_tiles)(subkeys)
    return tiles.reshape(DOMX, DOMY, 2, TILES).astype(jnp.int32)


def draw_tile_count(key, part):
    extra_key, forced_key = jax.random.split(key, 2)
    device_total = DOMX * DOMY
    counts = TILES // 2 + jax.random.randint(extra_key, (device_total,), 0, TILES - TILES // 2 + 1)
    forced_spot = jax.random.randint(forced_key, (), 0, device_total)
    counts = counts.at[forced_spot].set(TILES)
    counts = counts.at[(forced_spot + 1) % device_total].set(TILES // 2)
    return counts.reshape(DOMX, DOMY).astype(jnp.int32)


def device_frames(subkey, send_lists, counts):
    order_key, other_key, set_key, spot_key, halo_key = jax.random.split(subkey, 5)
    atom_order = jax.random.permutation(order_key, OWN)
    atom_ids = jnp.arange(OWN, dtype=jnp.int32)
    own_choice = (atom_ids[None, :] + 1 + jax.random.randint(other_key, (3, OWN), 0, OWN - 1)) % OWN
    set_ids = jax.random.randint(set_key, (3, OWN), 0, 3)
    position_ids = jax.random.randint(spot_key, (3, OWN), 0, 1048576) % counts[set_ids]
    halo_pick = OWN + set_ids * HALO + send_lists[set_ids, position_ids]
    use_halo = jax.random.randint(halo_key, (3, OWN), 0, 4) == 0
    frames = jnp.where(use_halo, halo_pick, own_choice)
    slot_ids = jnp.arange(3 * SEND, dtype=jnp.int32)
    cover_sets = slot_ids // SEND
    cover_spots = slot_ids % SEND
    target_atoms = atom_order[:3 * SEND]
    covering = OWN + cover_sets * HALO + send_lists[cover_sets, cover_spots]
    current = frames[0, target_atoms]
    frames = frames.at[0, target_atoms].set(jnp.where(cover_spots < counts[cover_sets], covering, current))
    return frames.astype(jnp.int32)


def frame_tables(key):
    device_total = DOMX * DOMY
    count_key, forced_key, list_key, frame_key = jax.random.split(jax.random.fold_in(key, 7), 4)
    ratios = jax.random.randint(count_key, (device_total * 3,), 0, 3)
    counts = jnp.maximum(SEND // (1 + ratios), 1)
    forced_spot = jax.random.randint(forced_key, (), 0, device_total * 3)
    counts = counts.at[forced_spot].set(SEND).reshape(device_total, 3).astype(jnp.int32)
    send_lists = jax.vmap(lambda subkey: jax.random.permutation(subkey, HALO)[:SEND])(jax.random.split(list_key, device_total * 3))
    send_lists = send_lists.reshape(device_total, 3, SEND).astype(jnp.int32)
    frames = jax.vmap(device_frames)(jax.random.split(frame_key, device_total), send_lists, counts)
    return (frames.reshape(DOMX, DOMY, 3, OWN), send_lists.reshape(DOMX, DOMY, 3, SEND), counts.reshape(DOMX, DOMY, 3))


def draw_frame_atoms(key, part):
    return frame_tables(key)[0]


def draw_send_list(key, part):
    return frame_tables(key)[1]


def draw_send_count(key, part):
    return frame_tables(key)[2]


def levels(rng, extent, cuts, smallest, high):
    gain, own = 1.0, jax.random.fold_in(rng, 6)
    for axis_at, shards_of in cuts:
        draws = jnp.exp(jax.random.uniform(jax.random.fold_in(own, axis_at), (shards_of,), jnp.float32, smallest / len(cuts), high / len(cuts)))
        gain = gain * jnp.repeat(draws, extent[axis_at] // shards_of).reshape([-1 if axis == axis_at else 1 for axis in range(len(extent))])
    return gain


def bell_draw(rng, extent, deviation, bound, pieces=(), kind=jnp.bfloat16):
    values = deviation * jax.random.normal(rng, extent, jnp.float32)
    if pieces:
        values = values * levels(rng, extent, pieces, -0.22, 0.18)
    return jnp.clip(values, -bound, bound).astype(kind)


def setup_inputs(seed: int = 0) -> dict:
    splits = jax.random.split(jax.random.key(seed), 9)
    return {
        "coords": jnp.clip(1.0 * jax.random.uniform(splits[0], (DOMX, DOMY, 3, OWN), jnp.float32) ** levels(splits[0], (DOMX, DOMY, 3, OWN), ((0, 32), (1, 16)), -0.2, 0.2), 0.0, 1.0),
        "multipoles": bell_draw(splits[1], (DOMX, DOMY, MPOLE, OWN), 0.2, 3.0, ((0, 32), (1, 16)), jnp.float32),
        "face_atoms": draw_face_atoms(jax.random.fold_in(splits[8], 71), 0),
        "tile_pairs": draw_tile_pairs(jax.random.fold_in(splits[8], 71), 0),
        "tile_count": draw_tile_count(jax.random.fold_in(splits[8], 71), 0),
        "frame_atoms": draw_frame_atoms(jax.random.fold_in(splits[8], 71), 0),
        "send_list": draw_send_list(jax.random.fold_in(splits[8], 71), 0),
        "send_count": draw_send_count(jax.random.fold_in(splits[8], 71), 0),
    }


SOFTENING = 0.5
LEVER_SOFT = 0.04
tile_group = 2

def cross_product(lhs_vec, rhs_vec):
    return (lhs_vec[1] * rhs_vec[2] - lhs_vec[2] * rhs_vec[1], lhs_vec[2] * rhs_vec[0] - lhs_vec[0] * rhs_vec[2], lhs_vec[0] * rhs_vec[1] - lhs_vec[1] * rhs_vec[0])

def inner_product(lhs_vec, rhs_vec):
    return lhs_vec[0] * rhs_vec[0] + lhs_vec[1] * rhs_vec[1] + lhs_vec[2] * rhs_vec[2]

def quad_matrix(entries):
    return ((entries[0], entries[3], entries[4]), (entries[3], entries[1], entries[5]), (entries[4], entries[5], entries[2]))

def apply_matrix(matrix, vector):
    return tuple((matrix[row_id][0] * vector[0] + matrix[row_id][1] * vector[1] + matrix[row_id][2] * vector[2] for row_id in range(3)))

def pair_energy(place_near, place_far, moment_near, moment_far, weight):
    between = tuple((place_far[row_id] - place_near[row_id] for row_id in range(3)))
    distance_sq = inner_product(between, between) + SOFTENING
    radial = [lax.rsqrt(distance_sq)]
    for order_id in range(4):
        radial.append((2 * order_id + 1) * radial[order_id] / distance_sq)
    charge_near = moment_near[0]
    charge_far = moment_far[0]
    dipole_near = (moment_near[1], moment_near[2], moment_near[3])
    dipole_far = (moment_far[1], moment_far[2], moment_far[3])
    quadrupole_near = quad_matrix(moment_near[4:10])
    quadrupole_far = quad_matrix(moment_far[4:10])
    turned_near = apply_matrix(quadrupole_near, between)
    turned_far = apply_matrix(quadrupole_far, between)
    along_near = inner_product(dipole_near, between)
    along_far = inner_product(dipole_far, between)
    double_near = inner_product(between, turned_near)
    double_far = inner_product(between, turned_far)
    quad_both = jnp.zeros_like(distance_sq)
    for row_id in range(3):
        for column_id in range(3):
            quad_both = quad_both + quadrupole_near[row_id][column_id] * quadrupole_far[row_id][column_id]
    energy = charge_near * charge_far * radial[0]
    energy = energy + (charge_far * along_near - charge_near * along_far + inner_product(dipole_near, dipole_far)) * radial[1]
    energy = energy + (charge_near * double_far + charge_far * double_near - along_near * along_far + 2.0 * (inner_product(dipole_far, turned_near) - inner_product(dipole_near, turned_far) + quad_both)) * radial[2]
    energy = energy + (along_near * double_far - along_far * double_near - 4.0 * inner_product(turned_near, turned_far)) * radial[3]
    energy = energy + double_near * double_far * radial[4]
    return jnp.sum(energy * weight)

def torque_from(moment, slope):
    from_dipole = cross_product((moment[1], moment[2], moment[3]), (slope[1], slope[2], slope[3]))
    quadrupole = quad_matrix(moment[4:10])
    quad_slope = quad_matrix((slope[4], slope[5], slope[6], 0.5 * slope[7], 0.5 * slope[8], 0.5 * slope[9]))

    def commutator(row_id, column_id):
        summed = quadrupole[row_id][0] * quad_slope[0][column_id] - quad_slope[row_id][0] * quadrupole[0][column_id]
        for inner_id in (1, 2):
            summed = summed + quadrupole[row_id][inner_id] * quad_slope[inner_id][column_id] - quad_slope[row_id][inner_id] * quadrupole[inner_id][column_id]
        return summed
    return jnp.stack([2.0 * commutator(2, 1) - from_dipole[0], 2.0 * commutator(0, 2) - from_dipole[1], 2.0 * commutator(1, 0) - from_dipole[2]])

def tile_terms(near_block, far_block, weight):
    slopes = jax.grad(pair_energy, argnums=(0, 1, 2, 3))(near_block[0:3, :, None], far_block[0:3, None, :], near_block[3:13, :, None], far_block[3:13, None, :], weight)
    return (-slopes[0][:, :, 0], torque_from(near_block[3:13], slopes[2][:, :, 0]), -slopes[1][:, 0, :], torque_from(far_block[3:13], slopes[3][:, 0, :]))

def group_terms(pooled, blocks_near, blocks_far, alive):
    lanes = jnp.arange(128, dtype=jnp.int32)
    rows_near = blocks_near[:, None] * 128 + lanes[None, :]
    rows_far = blocks_far[:, None] * 128 + lanes[None, :]
    near_block = jnp.take(pooled, rows_near, axis=1)
    far_block = jnp.take(pooled, rows_far, axis=1)
    upper_half = lanes[:, None] < lanes[None, :]
    keep_pair = alive[:, None, None] & ((blocks_near != blocks_far)[:, None, None] | upper_half[None])
    weight = jnp.where(keep_pair, 1.0, 0.0).astype(pooled.dtype)
    force_near, torque_near, force_far, torque_far = jax.vmap(tile_terms, in_axes=(1, 1, 0))(near_block, far_block, weight)
    values = jnp.concatenate([jnp.concatenate([force_near, torque_near], axis=1), jnp.concatenate([force_far, torque_far], axis=1)], axis=0)
    values = jnp.transpose(values, (1, 0, 2)).reshape(6, -1)
    targets = jnp.concatenate([rows_near, rows_far], axis=0).reshape(-1)
    return (targets, values)

def device_pairs(pooled, tile_rows, live_tiles, group_count):

    def accumulate(group_id, partials):
        offset_row = group_id.astype(jnp.int32) * tile_group
        blocks_near = lax.dynamic_slice_in_dim(tile_rows[0], offset_row, tile_group)
        blocks_far = lax.dynamic_slice_in_dim(tile_rows[1], offset_row, tile_group)
        alive = offset_row + jnp.arange(tile_group, dtype=jnp.int32) < live_tiles
        targets, values = group_terms(pooled, blocks_near, blocks_far, alive)
        return partials.at[:, targets].add(values)
    return lax.fori_loop(0, group_count, accumulate, jnp.zeros((6, pooled.shape[1]), pooled.dtype))

def frame_section(pool_place, torque, frames):
    own_count = frames.shape[1]
    own_place = pool_place[:, :own_count]
    frame_place = jnp.take(pool_place, frames, axis=1)
    lever = frame_place - own_place[:, None, :]
    scale = 1.0 / (3.0 * (inner_product(lever, lever) + LEVER_SOFT))
    push = jnp.stack(cross_product(torque[:, None, :], lever)) * scale[None]
    spread = jnp.zeros(pool_place.shape, pool_place.dtype).at[:, frames.reshape(-1)].add(push.reshape(3, -1))
    return spread.at[:, :own_count].add(-lax.optimization_barrier(jnp.sum(push, axis=1)))

def pick_listed(halo_values, chosen, live_count):
    alive = (jnp.arange(chosen.shape[0], dtype=jnp.int32) < live_count).astype(halo_values.dtype)
    return jnp.take(halo_values, chosen, axis=1) * alive[None, :]

def both_axes(function):
    return jax.vmap(jax.vmap(function))

def take_columns(source_rows, pick_rows):
    return jnp.take(source_rows, pick_rows, axis=1)

def add_returns(owned, pick_rows, return_x, return_y, return_c):
    return owned.at[:, pick_rows[0]].add(return_x).at[:, pick_rows[1]].add(return_y).at[:, pick_rows[2]].add(return_c)

def add_listed(owned_force, pick_rows, slot_ids, values):
    return owned_force.at[:, jnp.take(pick_rows, slot_ids)].add(values)

def reference(coords, multipoles, face_atoms, tile_pairs, tile_count, frame_atoms, send_list, send_count):
    stacked = jnp.concatenate([coords, multipoles], axis=2)
    exports = both_axes(take_columns)(stacked, face_atoms)
    unit_x = jnp.zeros((13, 1), jnp.float32).at[0, 0].set(1.0)
    unit_y = jnp.zeros((13, 1), jnp.float32).at[1, 0].set(1.0)
    import_x = jnp.roll(exports[:, :, :, 0], -1, axis=0) + unit_x
    import_y = jnp.roll(exports[:, :, :, 1], -1, axis=1) + unit_y
    import_c = jnp.roll(jnp.roll(exports[:, :, :, 2], -1, axis=0), -1, axis=1) + unit_x + unit_y
    pooled = jnp.concatenate([stacked, import_x, import_y, import_c], axis=3)
    device_total = DOMX * DOMY
    partials = lax.map(lambda entries: device_pairs(entries[0], entries[1], entries[2], TILES // tile_group), (pooled.reshape(device_total, 13, POOL), tile_pairs.reshape(device_total, 2, TILES), tile_count.reshape(device_total)))
    partials = partials.reshape(DOMX, DOMY, 6, POOL)
    halo_back = [partials[:, :, :, OWN + set_id * HALO:OWN + (set_id + 1) * HALO] for set_id in range(3)]
    return_x = jnp.roll(halo_back[0], 1, axis=0)
    return_y = jnp.roll(halo_back[1], 1, axis=1)
    return_c = jnp.roll(jnp.roll(halo_back[2], 1, axis=0), 1, axis=1)
    owned = both_axes(add_returns)(partials[:, :, :, :OWN], face_atoms, return_x, return_y, return_c)
    spread = both_axes(frame_section)(pooled[:, :, 0:3], owned[:, :, 3:6], frame_atoms)
    forces = owned[:, :, 0:3] + spread[:, :, :, :OWN]
    for set_id in range(3):
        sent = both_axes(pick_listed)(spread[:, :, :, OWN + set_id * HALO:OWN + (set_id + 1) * HALO], send_list[:, :, set_id], send_count[:, :, set_id])
        slots = send_list[:, :, set_id]
        if set_id != 1:
            sent = jnp.roll(sent, 1, axis=0)
            slots = jnp.roll(slots, 1, axis=0)
        if set_id != 0:
            sent = jnp.roll(sent, 1, axis=1)
            slots = jnp.roll(slots, 1, axis=1)
        forces = both_axes(add_listed)(forces, face_atoms[:, :, set_id], slots, sent)
    return forces
```

```python
import jax
import jax.numpy as jnp
from jax import lax
from jax.experimental import pallas as pl
from jax.experimental.pallas import tpu as pltpu
from jax.sharding import PartitionSpec as P

SOFTENING = 0.5
LEVER_SOFT = 0.04
OWN_BLOCKS = 8
POOL_BLOCKS = 20
ROWS = 24
ENTRIES = ((0, 0), (1, 1), (2, 2), (0, 1), (0, 2), (1, 2))
ENTRY_AT = {(0, 0): 0, (1, 1): 1, (2, 2): 2, (0, 1): 3, (1, 0): 3, (0, 2): 4, (2, 0): 4, (1, 2): 5, (2, 1): 5}
MULT = (1.0, 1.0, 1.0, 2.0, 2.0, 2.0)
F32 = jnp.float32
BF16 = jnp.bfloat16
ACC_GROUPS = 18
MESH = pl.DeviceIdType.MESH


def cross3(a, b):
    return (a[1] * b[2] - a[2] * b[1], a[2] * b[0] - a[0] * b[2], a[0] * b[1] - a[1] * b[0])


def dot3(a, b):
    return a[0] * b[0] + a[1] * b[1] + a[2] * b[2]


def mat_vec(m, v):
    return [sum_list([m[ENTRY_AT[(r, c)]] * v[c] for c in range(3)]) for r in range(3)]


def sum_list(items):
    total = items[0]
    for item in items[1:]:
        total = total + item
    return total


def sym_outer(a, b):
    out = []
    for r, c in ENTRIES:
        if r == c:
            out.append(a[r] * b[r])
        else:
            out.append(0.5 * (a[r] * b[c] + a[c] * b[r]))
    return out


def split2(value):
    hi = value.astype(BF16).astype(F32)
    lo = (value - hi).astype(BF16).astype(F32)
    return hi, lo


def nt_dot(a, b):
    return lax.dot_general(a, b, (((1,), (1,)), ((), ())), preferred_element_type=F32)


def mm(a, b):
    return lax.dot_general(a, b, (((1,), (0,)), ((), ())), preferred_element_type=F32)


def lane_gather(row, index):
    table = jnp.broadcast_to(row, (8, 128))
    return jnp.take_along_axis(table, index, axis=1)


def face_masks(face_rows):
    sub8 = lax.broadcasted_iota(jnp.int32, (8, 128), 0)
    sub128 = lax.broadcasted_iota(jnp.int32, (128, 128), 0)
    blocks, lanes = [], []
    for row in face_rows:
        blocks.append(jnp.broadcast_to(row >> 7, (8, 128)) == sub8)
        hit = jnp.broadcast_to(row & 127, (128, 128)) == sub128
        lanes.append(jnp.where(hit, 1.0, 0.0).astype(BF16))
    return blocks, lanes


def scatter_faces(values, blocks, lanes):
    comps = len(values)
    columns = []
    for j in range(len(blocks)):
        parts = []
        for c in range(comps):
            hi, lo = split2(values[c][j])
            parts.append(jnp.where(blocks[j], jnp.broadcast_to(hi, (8, 128)), 0.0))
            parts.append(jnp.where(blocks[j], jnp.broadcast_to(lo, (8, 128)), 0.0))
        columns.append(jnp.concatenate(parts, axis=0).astype(BF16))
    lhs = jnp.concatenate(columns, axis=1)
    rhs = jnp.concatenate(lanes, axis=1)
    out = nt_dot(lhs, rhs)
    return [out[16 * c : 16 * c + 8] + out[16 * c + 8 : 16 * c + 16] for c in range(comps)]


def export_body(coords_ref, mult_ref, face_ref, own_ref, out_ref):
    for c in range(13):
        src, row = (coords_ref, c) if c < 3 else (mult_ref, c - 3)
        for b in range(OWN_BLOCKS):
            own_ref[c, b : b + 1, :] = src[0, 0, row : row + 1, b * 128 : (b + 1) * 128]
    face = jnp.concatenate(
        [face_ref[0, 0, k : k + 1, j * 128 : (j + 1) * 128] for k in range(3) for j in range(4)]
        + [jnp.zeros((4, 128), jnp.int32)],
        axis=0,
    )
    shift = lax.broadcasted_iota(jnp.int32, (16, 128), 0)
    shift_x = jnp.where((shift < 4) | (shift >= 8), 1.0, 0.0).astype(F32)
    shift_y = jnp.where(shift >= 4, 1.0, 0.0).astype(F32)
    halves = [face[0:8], face[8:16]]
    lows = [h & 127 for h in halves]
    highs = [h >> 7 for h in halves]
    for c in range(13):
        got = []
        for part in range(2):
            total = jnp.zeros((8, 128), F32)
            for b in range(OWN_BLOCKS):
                picked = lane_gather(own_ref[c, b : b + 1, :], lows[part])
                total = jnp.where(highs[part] == b, picked, total)
            got.append(total)
        rows = jnp.concatenate(got, axis=0)
        if c == 0:
            rows = rows + shift_x
        if c == 1:
            rows = rows + shift_y
        for k in range(3):
            out_ref[k, 4 * c : 4 * c + 4, :] = rows[4 * k : 4 * k + 4]


def exchange_body(step, sizes, send_ref, recv_ref, send_sem, recv_sem):
    gx, gy = lax.axis_index("gx"), lax.axis_index("gy")
    nx, ny = sizes
    up = (lax.rem(gx + 1, nx), lax.rem(gy + 1, ny))
    down = (lax.rem(gx + nx - 1, nx), lax.rem(gy + ny - 1, ny))
    to = up if step > 0 else down
    barrier = pltpu.get_barrier_semaphore()
    for other in (up, down):
        for peer in ((other[0], gy), (gx, other[1]), (other[0], other[1])):
            pl.semaphore_signal(barrier, inc=1, device_id=peer, device_id_type=MESH)
    pl.semaphore_wait(barrier, 6)
    copies = []
    for k, peer in enumerate(((to[0], gy), (gx, to[1]), (to[0], to[1]))):
        copy = pltpu.make_async_remote_copy(
            src_ref=send_ref.at[k],
            dst_ref=recv_ref.at[k],
            send_sem=send_sem.at[k],
            recv_sem=recv_sem.at[k],
            device_id=peer,
            device_id_type=MESH,
        )
        copy.start()
        copies.append(copy)
    for copy in copies:
        copy.wait()


def pool_features(pool):
    x = [pool[0] - 1.0, pool[1] - 1.0, pool[2] - 0.5]
    q = pool[3]
    d = [pool[4], pool[5], pool[6]]
    quad = [pool[7], pool[8], pool[9], pool[10], pool[11], pool[12]]
    one = jnp.ones_like(q)
    xx = [x[r] * x[c] for r, c in ENTRIES]
    qx = [q * x[r] for r in range(3)]
    m = [qx[r] + d[r] for r in range(3)]
    turned = mat_vec(quad, x)
    dx = dot3(d, x)
    xqx = dot3(x, turned)
    sdx = sym_outer(d, x)
    h = [q * xx[e] + 2.0 * sdx[e] for e in range(6)]
    tx = sym_outer(turned, x)
    outer = [[quad[e] * x[c] for c in range(3)] for e in range(6)]
    return dict(one=one, x=x, q=q, d=d, quad=quad, xx=xx, qx=qx, m=m, turned=turned, dx=dx, xqx=xqx, h=h, tx=tx, outer=outer)


def sum_rows(f):
    zero = jnp.zeros_like(f["one"])
    rows = [f["one"], *f["x"], f["q"], *f["d"]]
    rows += [*f["qx"], *f["m"], zero, zero]
    rows += [*f["quad"], *f["turned"], *f["h"], zero]
    rows += [*f["tx"]] + [f["outer"][e][c] for e in range(6) for c in range(3)]
    rows += [*f["xx"], zero, zero]
    return rows


def near_rows(f):
    zero = jnp.zeros_like(f["one"])
    first = [*f["d"], f["dx"], *f["quad"], *f["turned"], f["xqx"], f["one"], *f["x"], *f["xx"]]
    second = [*f["d"], f["dx"], f["q"], *f["qx"], *f["quad"], *f["turned"], f["xqx"], *f["h"]]
    third = [*f["quad"], *f["turned"], *f["tx"]] + [f["outer"][e][c] for e in range(6) for c in range(3)]
    return first + second + third + [zero] * 7


def far_rows(f):
    zero = jnp.zeros_like(f["one"])
    one = f["one"]
    x, d, q, xx = f["x"], f["d"], f["q"], f["xx"]
    quad, turned = f["quad"], f["turned"]
    z = lambda n: [zero] * n
    u = [3.0 * x[r] for r in range(3)] + [-3.0 * one] + z(20)
    v = z(14) + [3.0 * f["dx"]] + [-3.0 * d[r] for r in range(3)] + z(6)
    p = z(4) + [15.0 * MULT[e] * xx[e] for e in range(6)] + [-30.0 * x[r] for r in range(3)] + [15.0 * one] + z(10)
    r_ = (
        z(14)
        + [15.0 * f["xqx"]]
        + [-30.0 * turned[r] for r in range(3)]
        + [15.0 * MULT[e] * quad[e] for e in range(6)]
    )
    l1 = [1.8 * f["m"][r] for r in range(3)] + [-1.8 * q, -1.8 * f["dx"]] + [1.8 * d[r] for r in range(3)]
    l1 += z(16)
    l2 = (
        [-18.0 * turned[r] for r in range(3)]
        + z(1)
        + [9.0 * f["xqx"]]
        + [-18.0 * turned[r] for r in range(3)]
        + [9.0 * MULT[e] * (f["h"][e] + 2.0 * quad[e]) for e in range(6)]
        + [-18.0 * f["m"][r] for r in range(3)]
        + [9.0 * q]
        + [9.0 * MULT[e] * quad[e] for e in range(6)]
    )
    l3 = [-180.0 * MULT[e] * f["tx"][e] for e in range(6)] + [180.0 * turned[r] for r in range(3)]
    l3 += [-180.0 * MULT[e] * quad[e] for e in range(6)]
    for a, b in ENTRIES:
        for c in range(3):
            term = quad[ENTRY_AT[(a, c)]] * x[b]
            if a != b:
                term = term + quad[ENTRY_AT[(b, c)]] * x[a]
            l3.append(180.0 * term)
    l3 += z(7)
    return [u, v, p, r_, l1, l2, l3]


def tile_setup(pool_ref, sum_scr, near_scr, far_scr, feat_ref, lhs_ref, rhs_ref, place_ref, wide_ref):
    f = pool_features([pool_ref[c] for c in range(13)])
    for n, row in enumerate(sum_rows(f)):
        sum_scr[n * ROWS : (n + 1) * ROWS, :] = row
    for n, row in enumerate(near_rows(f)):
        near_scr[n * 8 : n * 8 + 8, :] = row[0:8]
    at = 0
    for group in far_rows(f):
        for row in group:
            far_scr[at * ROWS : (at + 1) * ROWS, :] = row
            at += 1

    def per_block(b, _):
        sums = sum_scr[pl.ds(b, 64, stride=ROWS), :]
        place_ref[b] = sums[0:8]
        hi, lo = split2(sums)
        parts = []
        for g in range(8):
            parts += [hi[8 * g : 8 * g + 8], lo[8 * g : 8 * g + 8]]
        feat_ref[b] = jnp.concatenate(parts, axis=0).astype(BF16)
        start = 0
        for out_id, count in enumerate((24, 24, 24, 24, 24, 24, 40)):
            rows = far_scr[pl.ds(b + start * ROWS, count, stride=ROWS), :]
            start += count
            hi, lo = split2(rows)
            pad = [jnp.zeros((128 - 3 * count, 128), F32)]
            stacked = jnp.concatenate([hi, lo, hi] + pad, axis=0).astype(BF16)
            rhs_ref[b, :, out_id * 128 : (out_id + 1) * 128] = stacked
        return 0

    lax.fori_loop(0, POOL_BLOCKS, per_block, 0)

    def per_near(b, _):
        start = 0
        for group, count in enumerate((24, 24, 40)):
            rows = near_scr[pl.ds(b + start * 8, count, stride=8), :]
            start += count
            hi, lo = split2(rows)
            stacked = jnp.concatenate([hi, hi, lo, jnp.zeros((128 - 3 * count, 128), F32)], axis=0)
            lhs_ref[b, :, group * 128 : (group + 1) * 128] = stacked.T.astype(BF16)
        place = jnp.concatenate([place_ref[b], jnp.zeros((120, 128), F32)], axis=0).T
        for r in range(3):
            wide_ref[b, r] = jnp.broadcast_to(place[:, r + 1 : r + 2], (128, 128))
        return 0

    lax.fori_loop(0, OWN_BLOCKS, per_near, 0)


def tile_work(near, far, feat_ref, lhs_ref, rhs_ref, place_ref, wide_ref, keep_ref, keep):
    first = mm(lhs_ref[near, :, 0:128], rhs_ref[far, :, 0:512])
    second = mm(lhs_ref[near, :, 128:256], rhs_ref[far, :, 512:768])
    third = mm(lhs_ref[near, :, 256:384], rhs_ref[far, :, 768:896])
    chunk = 32
    names = ("b1", "b2", "b3", "al", "be", "ga", "de", "e1")
    pieces = {name: ([], []) for name in names}
    place = [jnp.broadcast_to(place_ref[far, r + 1 : r + 2, :], (chunk, 128)) for r in range(3)]
    for row in range(0, 128, chunk):
        rows = slice(row, row + chunk)
        diff = [place[r] - wide_ref[near, r, rows, :] for r in range(3)]
        dist = diff[0] * diff[0] + (diff[1] * diff[1] + (diff[2] * diff[2] + SOFTENING))
        root = lax.rsqrt(dist)
        t = root * root
        b0 = root * keep_ref[keep, rows, :]
        b1 = b0 * t
        b2 = b1 * t
        b3 = b2 * t
        b4 = b3 * (1.4 * t)
        b5 = b4 * (1.8 * t)
        u, v = first[rows, 0:128], first[rows, 128:256]
        p, r_ = first[rows, 256:384], first[rows, 384:512]
        l1, l2, l3 = second[rows, 0:128], second[rows, 128:256], third[rows, :]
        al = r_ * b3 - v * b2
        be = p * b3 + u * b2
        ga = r_ * b4 - v * b3
        de = p * b4 + u * b3
        e1 = l1 * b2 + (l2 - u * v) * b3 + (u * r_ - v * p + l3) * b4 + (p * r_) * b5
        for name, value in zip(names, (b1, b2, b3, al, be, ga, de, e1)):
            hi = value.astype(BF16)
            pieces[name][0].append(hi)
            pieces[name][1].append((value - hi.astype(F32)).astype(BF16))
    return {name: (jnp.concatenate(h, axis=0), jnp.concatenate(l, axis=0)) for name, (h, l) in pieces.items()}


def tile_sums(w, near, far, feat_ref, add):
    near_pairs = (
        ("al", "be", 16, ((0, 0),), ((1, 0),)),
        ("e1", "b1", 32, ((2, 0),), ((3, 0), (4, 1))),
        ("b2", "de", 64, ((5, 0), (6, 1), (7, 2), (8, 3)), ((9, 2), (10, 3))),
        ("ga", "b3", 128, ((11, 0), (12, 7)), ((13, 2), (14, 3), (15, 4), (16, 5), (17, 6))),
    )
    far_pairs = (
        ("be", "al", 16, ((0, 0),), ((1, 0),)),
        ("e1", "b1", 32, ((2, 0),), ((3, 0), (4, 1))),
        ("b2", "ga", 64, ((5, 0), (6, 1), (7, 2), (8, 3)), ((9, 2), (10, 3))),
        ("de", "b3", 128, ((11, 0), (12, 7)), ((13, 2), (14, 3), (15, 4), (16, 5), (17, 6))),
    )
    for pairs, source, target, transposed in ((near_pairs, far, near, True), (far_pairs, near, far, False)):
        for one, two, rows, slots_one, slots_two in pairs:
            feats = feat_ref[source, 0:rows, :]
            lhs = jnp.concatenate([feats, feats], axis=1)
            if transposed:
                rhs = jnp.concatenate(
                    [jnp.concatenate(w[one], axis=1), jnp.concatenate(w[two], axis=1)], axis=0
                )
                out = nt_dot(lhs, rhs)
            else:
                rhs = jnp.concatenate(
                    [jnp.concatenate([w[one][s], w[two][s]], axis=1) for s in range(2)], axis=0
                )
                out = mm(lhs, rhs)
            for half, slots in enumerate((slots_one, slots_two)):
                lanes = slice(128 * half, 128 * half + 128)
                for slot, group in slots:
                    at = 16 * group
                    add(target, slot, out[at : at + 8, lanes] + out[at + 8 : at + 16, lanes])


def finish_sums(load, f):
    x, q, d, quad = f["x"], f["q"], f["d"], f["quad"]
    turned = f["turned"]
    a_one, a_x = load(0, 0), [load(0, 1 + r) for r in range(3)]
    ap_d = [load(1, 5 + r) for r in range(3)]
    e_one, e_x = load(2, 0), [load(2, 1 + r) for r in range(3)]
    b1_q, b1_d = load(3, 4), [load(3, 5 + r) for r in range(3)]
    b1_qx = [load(4, r) for r in range(3)]
    b2_q, b2_m = load(5, 4), [load(6, 3 + r) for r in range(3)]

    def wide(slot):
        flat = lambda n: load(slot + n // 8, n % 8)
        return [flat(e) for e in range(6)], [flat(6 + r) for r in range(3)]

    b2_quad, b2_t = wide(7)
    b2_h = [load(7 + (9 + e) // 8, (9 + e) % 8) for e in range(6)]
    cp_quad, cp_t = wide(9)
    c_one, c_x = load(11, 0), [load(11, 1 + r) for r in range(3)]
    c_xx = [load(12, e) for e in range(6)]
    b3_quad, b3_t = wide(13)
    b3_tx = [load(15, e) for e in range(6)]
    b3_outer = [[load(15 + (6 + 3 * e + c) // 8, (6 + 3 * e + c) % 8) for c in range(3)] for e in range(6)]

    b2_quad_x = mat_vec(b2_quad, x)
    b3_quad_x = mat_vec(b3_quad, x)
    cp_quad_x = mat_vec(cp_quad, x)
    b2_turn = [b2_t[r] - b2_quad_x[r] for r in range(3)]
    b3_turn = [b3_t[r] - b3_quad_x[r] for r in range(3)]
    cp_turn = [cp_t[r] - cp_quad_x[r] for r in range(3)]
    b1_r = [b1_qx[r] - x[r] * b1_q for r in range(3)]
    a_r = [a_x[r] - x[r] * a_one for r in range(3)]
    e_r = [e_x[r] - x[r] * e_one for r in range(3)]
    c_r = [c_x[r] - x[r] * c_one for r in range(3)]
    b2_r = [b2_m[r] - x[r] * b2_q for r in range(3)]

    slope_d = [a_r[r] + b1_r[r] + b1_d[r] - 6.0 * b2_turn[r] for r in range(3)]

    sx_c = sym_outer(c_x, x)
    sx_m = sym_outer(b2_m, x)
    sx_t = sym_outer(b3_t, x)
    sx_q = sym_outer(b3_quad_x, x)
    mixed = [
        [sum_list([b3_outer[ENTRY_AT[(a, c)]][b] * x[c] for c in range(3)]) for b in range(3)] for a in range(3)
    ]
    slope_q = []
    for e, (a, b) in enumerate(ENTRIES):
        ym = mixed[a][b] if a == b else 0.5 * (mixed[a][b] + mixed[b][a])
        slope_q.append(
            5.0 * (c_xx[e] - 2.0 * sx_c[e] + c_one * f["xx"][e])
            + 3.0 * (b2_h[e] - 2.0 * sx_m[e] + b2_q * f["xx"][e])
            + 6.0 * b2_quad[e]
            - 60.0 * (b3_tx[e] - sx_t[e] - ym + sx_q[e])
        )

    inner = [10.0 * c_r[r] + 6.0 * b2_r[r] - 60.0 * b3_turn[r] for r in range(3)]
    inner = mat_vec(quad, inner)
    b2_quad_d = mat_vec(b2_quad, d)
    b3_quad_t = mat_vec(b3_quad, turned)
    force = []
    for a in range(3):
        spun = sum_list(
            [
                b3_outer[ENTRY_AT[(a, b)]][c] * quad[ENTRY_AT[(b, c)]]
                for b in range(3)
                for c in range(3)
            ]
        )
        force.append(
            -q * (b1_r[a] + b1_d[a])
            - (5.0 / 3.0) * e_r[a]
            + d[a] * (a_one + b1_q)
            - ap_d[a]
            + inner[a]
            + 10.0 * cp_turn[a]
            + 6.0 * q * b2_turn[a]
            - 6.0 * b2_quad_d[a]
            - 60.0 * (spun - b3_quad_t[a])
        )

    full = lambda m, r, c: m[ENTRY_AT[(r, c)]]

    def commutator(r, c):
        return sum_list(
            [full(quad, r, k) * full(slope_q, k, c) - full(slope_q, r, k) * full(quad, k, c) for k in range(3)]
        )

    twist = cross3(d, slope_d)
    torque = [
        2.0 * commutator(2, 1) - twist[0],
        2.0 * commutator(0, 2) - twist[1],
        2.0 * commutator(1, 0) - twist[2],
    ]
    return force, torque


def tiles_body(
    own_ref, import_ref, pairs_ref, count_ref, own_out, halo_out,
    pool_ref, sum_scr, near_scr, far_scr, feat_ref, lhs_ref, rhs_ref, place_ref, wide_ref, keep_ref, acc_ref,
):
    for c in range(13):
        pool_ref[c, 0:8, :] = own_ref[c]
        for k in range(3):
            pool_ref[c, 8 + 4 * k : 12 + 4 * k, :] = import_ref[k, 4 * c : 4 * c + 4, :]
        pool_ref[c, 20:24, :] = jnp.zeros((4, 128), F32)
    above = lax.broadcasted_iota(jnp.int32, (128, 128), 0) < lax.broadcasted_iota(jnp.int32, (128, 128), 1)
    keep_ref[0] = jnp.ones((128, 128), F32)
    keep_ref[1] = jnp.where(above, 1.0, 0.0).astype(F32)
    acc_ref[...] = jnp.zeros_like(acc_ref)
    tile_setup(pool_ref, sum_scr, near_scr, far_scr, feat_ref, lhs_ref, rhs_ref, place_ref, wide_ref)

    def add(block, slot, value):
        at = pl.multiple_of(block * (8 * ACC_GROUPS) + 8 * slot, 8)
        acc_ref[pl.ds(at, 8), :] += value

    def step(t, _):
        near, far = pairs_ref[0, 0, 0, t], pairs_ref[0, 0, 1, t]
        keep = jnp.where(near == far, 1, 0)
        w = tile_work(near, far, feat_ref, lhs_ref, rhs_ref, place_ref, wide_ref, keep_ref, keep)
        tile_sums(w, near, far, feat_ref, add)
        return 0

    lax.fori_loop(0, count_ref[0, 0], step, 0)

    def load(slot, row):
        return acc_ref[pl.ds(8 * slot + row, ROWS, stride=8 * ACC_GROUPS), :]

    force, torque = finish_sums(load, pool_features([pool_ref[c] for c in range(13)]))
    for c, rows in enumerate(force + torque):
        own_out[c] = rows[0:8]
        for k in range(3):
            halo_out[k, 4 * c : 4 * c + 4, :] = rows[8 + 4 * k : 12 + 4 * k]


def face_rows_of(face_ref):
    return [face_ref[0, 0, k : k + 1, j * 128 : (j + 1) * 128] for k in range(3) for j in range(4)]


def returned_rows(back_ref, comps):
    return [[back_ref[k, 4 * c + j : 4 * c + j + 1, :] for k in range(3) for j in range(4)] for c in range(comps)]


def frame_body(own_ref, back_ref, pool_x_ref, import_ref, face_ref, frame_ref, force_out, halo_out):
    blocks, lanes = face_masks(face_rows_of(face_ref))
    added = scatter_faces(returned_rows(back_ref, 6), blocks, lanes)
    owned = [own_ref[c] + added[c] for c in range(6)]
    torque = owned[3:6]
    index = [
        jnp.concatenate([frame_ref[0, 0, m : m + 1, b * 128 : (b + 1) * 128] for b in range(OWN_BLOCKS)], axis=0)
        for m in range(3)
    ]
    low = [i & 127 for i in index]
    high = [i >> 7 for i in index]
    spots = [[jnp.zeros((8, 128), F32) for _ in range(3)] for _ in range(3)]
    for b in range(POOL_BLOCKS):
        rows = []
        for c in range(3):
            if b < OWN_BLOCKS:
                rows.append(pool_x_ref[c, b : b + 1, :])
            else:
                k, j = divmod(b - OWN_BLOCKS, 4)
                rows.append(import_ref[k, 4 * c + j : 4 * c + j + 1, :])
        for m in range(3):
            hit = high[m] == b
            for c in range(3):
                spots[m][c] = jnp.where(hit, lane_gather(rows[c], low[m]), spots[m][c])
    place = [pool_x_ref[c] for c in range(3)]
    sub24 = lax.broadcasted_iota(jnp.int32, (ROWS, 128), 0)
    sub128 = lax.broadcasted_iota(jnp.int32, (128, 128), 0)
    kept = [jnp.zeros((8, 128), F32) for _ in range(3)]
    columns, hot = [], []
    for m in range(3):
        lever = [spots[m][c] - place[c] for c in range(3)]
        scale = 1.0 / (3.0 * (dot3(lever, lever) + LEVER_SOFT))
        push = [w * scale for w in cross3(torque, lever)]
        kept = [kept[c] + push[c] for c in range(3)]
        halves = [split2(w) for w in push]
        for b in range(OWN_BLOCKS):
            hit = jnp.broadcast_to(high[m][b : b + 1], (ROWS, 128)) == sub24
            parts = []
            for c in range(3):
                for half in halves[c]:
                    parts.append(jnp.where(hit, jnp.broadcast_to(half[b : b + 1], (ROWS, 128)), 0.0))
            columns.append(jnp.concatenate(parts, axis=0).astype(BF16))
            lane = jnp.broadcast_to(low[m][b : b + 1], (128, 128)) == sub128
            hot.append(jnp.where(lane, 1.0, 0.0).astype(BF16))
    out = nt_dot(jnp.concatenate(columns, axis=1), jnp.concatenate(hot, axis=1))
    for c in range(3):
        rows = out[48 * c : 48 * c + 24] + out[48 * c + 24 : 48 * c + 48]
        force_out[c] = owned[c] + rows[0:8] - kept[c]
        for k in range(3):
            halo_out[k, 4 * c : 4 * c + 4, :] = rows[8 + 4 * k : 12 + 4 * k]
        halo_out[:, 12:16, :] = jnp.zeros((3, 4, 128), F32)


def final_body(force_ref, back_ref, face_ref, out_ref):
    blocks, lanes = face_masks(face_rows_of(face_ref))
    added = scatter_faces(returned_rows(back_ref, 3), blocks, lanes)
    for c in range(3):
        total = force_ref[c] + added[c]
        for b in range(OWN_BLOCKS):
            out_ref[0, 0, c : c + 1, b * 128 : (b + 1) * 128] = total[b : b + 1]


def vmem(count):
    return [pl.BlockSpec(memory_space=pltpu.VMEM)] * count


def shape(*dims):
    return jax.ShapeDtypeStruct(dims, F32)


def exchange(array, step, sizes, collective):
    def body(send_ref, recv_ref, send_sem, recv_sem):
        exchange_body(step, sizes, send_ref, recv_ref, send_sem, recv_sem)

    return pl.pallas_call(
        body,
        out_shape=jax.ShapeDtypeStruct(array.shape, array.dtype),
        in_specs=vmem(1),
        out_specs=pl.BlockSpec(memory_space=pltpu.VMEM),
        scratch_shapes=[pltpu.SemaphoreType.DMA((3,)), pltpu.SemaphoreType.DMA((3,))],
        compiler_params=pltpu.CompilerParams(collective_id=collective, has_side_effects=True),
    )(array)


def gather_exports(coords, multipoles, face_atoms):
    return pl.pallas_call(
        export_body,
        out_shape=(shape(13, 8, 128), shape(3, 56, 128)),
        in_specs=vmem(3),
        out_specs=vmem(2),
    )(coords, multipoles, face_atoms)


def pair_tiles(own, imports, tile_pairs, tile_count):
    return pl.pallas_call(
        tiles_body,
        out_shape=(shape(6, 8, 128), shape(3, 24, 128)),
        in_specs=vmem(2) + [pl.BlockSpec(memory_space=pltpu.SMEM)] * 2,
        out_specs=vmem(2),
        scratch_shapes=[
            pltpu.VMEM((13, ROWS, 128), F32),
            pltpu.VMEM((64 * ROWS, 128), F32),
            pltpu.VMEM((88 * 8, 128), F32),
            pltpu.VMEM((184 * ROWS, 128), F32),
            pltpu.VMEM((POOL_BLOCKS, 128, 128), BF16),
            pltpu.VMEM((OWN_BLOCKS, 128, 384), BF16),
            pltpu.VMEM((POOL_BLOCKS, 128, 896), BF16),
            pltpu.VMEM((POOL_BLOCKS, 8, 128), F32),
            pltpu.VMEM((OWN_BLOCKS, 3, 128, 128), F32),
            pltpu.VMEM((2, 128, 128), F32),
            pltpu.VMEM((ROWS * 8 * ACC_GROUPS, 128), F32),
        ],
        compiler_params=pltpu.CompilerParams(vmem_limit_bytes=48 << 20),
    )(own, imports, tile_pairs, tile_count)


def frame_forces(owned, back, own, imports, face_atoms, frame_atoms):
    return pl.pallas_call(
        frame_body,
        out_shape=(shape(3, 8, 128), shape(3, 16, 128)),
        in_specs=vmem(6),
        out_specs=vmem(2),
    )(owned, back, own, imports, face_atoms, frame_atoms)


def final_forces(force, back, face_atoms):
    return pl.pallas_call(
        final_body,
        out_shape=shape(1, 1, 3, 1024),
        in_specs=vmem(3),
        out_specs=pl.BlockSpec(memory_space=pltpu.VMEM),
    )(force, back, face_atoms)


def solution(mesh):
    sizes = (mesh.shape["gx"], mesh.shape["gy"])

    def shards(coords, multipoles, face_atoms, tile_pairs, tile_count, frame_atoms, send_list, send_count):
        own, exports = gather_exports(coords, multipoles, face_atoms)
        imports = exchange(exports, -1, sizes, 0)
        owned, halo = pair_tiles(own, imports, tile_pairs, tile_count)
        back = exchange(halo, 1, sizes, 1)
        force, spread = frame_forces(owned, back, own, imports, face_atoms, frame_atoms)
        frame_back = exchange(spread, 1, sizes, 2)
        return final_forces(force, frame_back, face_atoms)

    four = P("gx", "gy", None, None)
    placed = (four, four, four, four, P("gx", "gy"), four, four, P("gx", "gy", None))
    return jax.shard_map(shards, mesh=mesh, in_specs=placed, out_specs=four, check_vma=False)
```

```python
import functools

import jax
import jax.numpy as jnp
from jax import lax
from jax.experimental import pallas as pl
from jax.experimental.pallas import tpu as pltpu
from jax.sharding import PartitionSpec as P

SOFTENING = 0.5
LEVER_SOFT = 0.04
OWN_BLOCKS = 8
POOL_BLOCKS = 20
ROWS = 24
ENTRIES = ((0, 0), (1, 1), (2, 2), (0, 1), (0, 2), (1, 2))
ENTRY_AT = {(0, 0): 0, (1, 1): 1, (2, 2): 2, (0, 1): 3, (1, 0): 3, (0, 2): 4, (2, 0): 4, (1, 2): 5, (2, 1): 5}
MULT = (1.0, 1.0, 1.0, 2.0, 2.0, 2.0)
F32 = jnp.float32
BF16 = jnp.bfloat16
ACC_GROUPS = 18
MESH = pl.DeviceIdType.MESH


def cross3(a, b):
    return (a[1] * b[2] - a[2] * b[1], a[2] * b[0] - a[0] * b[2], a[0] * b[1] - a[1] * b[0])


def dot3(a, b):
    return a[0] * b[0] + a[1] * b[1] + a[2] * b[2]


def mat_vec(m, v):
    return [sum_list([m[ENTRY_AT[(r, c)]] * v[c] for c in range(3)]) for r in range(3)]


def sum_list(items):
    total = items[0]
    for item in items[1:]:
        total = total + item
    return total


def sym_outer(a, b):
    out = []
    for r, c in ENTRIES:
        if r == c:
            out.append(a[r] * b[r])
        else:
            out.append(0.5 * (a[r] * b[c] + a[c] * b[r]))
    return out


def split2(value):
    hi = value.astype(BF16).astype(F32)
    lo = (value - hi).astype(BF16).astype(F32)
    return hi, lo


def nt_dot(a, b):
    return lax.dot_general(a, b, (((1,), (1,)), ((), ())), preferred_element_type=F32)


def mm(a, b):
    return lax.dot_general(a, b, (((1,), (0,)), ((), ())), preferred_element_type=F32)


def lane_gather(row, index):
    table = jnp.broadcast_to(row, (8, 128))
    return jnp.take_along_axis(table, index, axis=1)


def face_masks(face_rows):
    sub8 = lax.broadcasted_iota(jnp.int32, (8, 128), 0)
    sub128 = lax.broadcasted_iota(jnp.int32, (128, 128), 0)
    blocks, lanes = [], []
    for row in face_rows:
        blocks.append(jnp.broadcast_to(row >> 7, (8, 128)) == sub8)
        hit = jnp.broadcast_to(row & 127, (128, 128)) == sub128
        lanes.append(jnp.where(hit, 1.0, 0.0).astype(BF16))
    return blocks, lanes


def scatter_faces(values, blocks, lanes):
    comps = len(values)
    columns = []
    for j in range(len(blocks)):
        parts = []
        for c in range(comps):
            hi, lo = split2(values[c][j])
            parts.append(jnp.where(blocks[j], jnp.broadcast_to(hi, (8, 128)), 0.0))
            parts.append(jnp.where(blocks[j], jnp.broadcast_to(lo, (8, 128)), 0.0))
        columns.append(jnp.concatenate(parts, axis=0).astype(BF16))
    lhs = jnp.concatenate(columns, axis=1)
    rhs = jnp.concatenate(lanes, axis=1)
    out = nt_dot(lhs, rhs)
    return [out[16 * c : 16 * c + 8] + out[16 * c + 8 : 16 * c + 16] for c in range(comps)]


def neighbours(sizes):
    gx, gy = lax.axis_index("gx"), lax.axis_index("gy")
    nx, ny = sizes
    up = (lax.rem(gx + 1, nx), lax.rem(gy + 1, ny))
    down = (lax.rem(gx + nx - 1, nx), lax.rem(gy + ny - 1, ny))
    return [[(to[0], gy), (gx, to[1]), (to[0], to[1])] for to in (up, down)]


def greet(senders):
    for peer in senders:
        pl.semaphore_signal(pltpu.get_barrier_semaphore(), inc=1, device_id=peer, device_id_type=MESH)


def send_sets(send_ref, recv_ref, send_sem, recv_sem, targets):
    copies = []
    for k, peer in enumerate(targets):
        copy = pltpu.make_async_remote_copy(
            src_ref=send_ref.at[k],
            dst_ref=recv_ref.at[k],
            send_sem=send_sem.at[k],
            recv_sem=recv_sem.at[k],
            device_id=peer,
            device_id_type=MESH,
        )
        copy.start()
        copies.append(copy)
    return copies


def import_body(sizes, coords_ref, mult_ref, face_ref, recv_ref, send_ref, send_sem, recv_sem):
    up, down = neighbours(sizes)
    greet(up)
    face = jnp.concatenate([face_ref[k] for k in range(3)] + [jnp.zeros((4, 128), jnp.int32)], axis=0)
    shift = lax.broadcasted_iota(jnp.int32, (16, 128), 0)
    shift_x = jnp.where((shift < 4) | (shift >= 8), 1.0, 0.0).astype(F32)
    shift_y = jnp.where(shift >= 4, 1.0, 0.0).astype(F32)
    halves = [face[0:8], face[8:16]]
    lows = [h & 127 for h in halves]
    highs = [h >> 7 for h in halves]
    for c in range(13):
        src, at = (coords_ref, 8 * c) if c < 3 else (mult_ref, 8 * (c - 3))
        got = []
        for part in range(2):
            total = jnp.zeros((8, 128), F32)
            for b in range(OWN_BLOCKS):
                picked = lane_gather(src[at + b : at + b + 1, :], lows[part])
                total = jnp.where(highs[part] == b, picked, total)
            got.append(total)
        rows = jnp.concatenate(got, axis=0)
        if c == 0:
            rows = rows + shift_x
        if c == 1:
            rows = rows + shift_y
        for k in range(3):
            send_ref[k, 4 * c : 4 * c + 4, :] = rows[4 * k : 4 * k + 4]
    for k in range(3):
        send_ref[k, 52:56, :] = jnp.zeros((4, 128), F32)
    pl.semaphore_wait(pltpu.get_barrier_semaphore(), 3)
    for copy in send_sets(send_ref, recv_ref, send_sem, recv_sem, down):
        copy.wait()


def pool_features(pool):
    x = [pool[0] - 1.0, pool[1] - 1.0, pool[2] - 0.5]
    q = pool[3]
    d = [pool[4], pool[5], pool[6]]
    quad = [pool[7], pool[8], pool[9], pool[10], pool[11], pool[12]]
    one = jnp.ones_like(q)
    xx = [x[r] * x[c] for r, c in ENTRIES]
    qx = [q * x[r] for r in range(3)]
    m = [qx[r] + d[r] for r in range(3)]
    turned = mat_vec(quad, x)
    dx = dot3(d, x)
    xqx = dot3(x, turned)
    sdx = sym_outer(d, x)
    h = [q * xx[e] + 2.0 * sdx[e] for e in range(6)]
    tx = sym_outer(turned, x)
    outer = [[quad[e] * x[c] for c in range(3)] for e in range(6)]
    return dict(one=one, x=x, q=q, d=d, quad=quad, xx=xx, qx=qx, m=m, turned=turned, dx=dx, xqx=xqx, h=h, tx=tx, outer=outer)


def sum_rows(f):
    zero = jnp.zeros_like(f["one"])
    rows = [f["one"], *f["x"], f["q"], *f["d"]]
    rows += [*f["qx"], *f["m"], zero, zero]
    rows += [*f["quad"], *f["turned"], *f["h"], zero]
    rows += [*f["tx"]] + [f["outer"][e][c] for e in range(6) for c in range(3)]
    rows += [*f["xx"], zero, zero]
    return rows


def near_rows(f):
    zero = jnp.zeros_like(f["one"])
    first = [*f["d"], f["dx"], *f["quad"], *f["turned"], f["xqx"], f["one"], *f["x"], *f["xx"]]
    second = [*f["d"], f["dx"], f["q"], *f["qx"], *f["quad"], *f["turned"], f["xqx"], *f["h"]]
    third = [*f["quad"], *f["turned"], *f["tx"]] + [f["outer"][e][c] for e in range(6) for c in range(3)]
    return first + second + third + [zero] * 7


def far_rows(f):
    zero = jnp.zeros_like(f["one"])
    one = f["one"]
    x, d, q, xx = f["x"], f["d"], f["q"], f["xx"]
    quad, turned = f["quad"], f["turned"]
    z = lambda n: [zero] * n
    u = [3.0 * x[r] for r in range(3)] + [-3.0 * one] + z(20)
    v = z(14) + [3.0 * f["dx"]] + [-3.0 * d[r] for r in range(3)] + z(6)
    p = z(4) + [15.0 * MULT[e] * xx[e] for e in range(6)] + [-30.0 * x[r] for r in range(3)] + [15.0 * one] + z(10)
    r_ = (
        z(14)
        + [15.0 * f["xqx"]]
        + [-30.0 * turned[r] for r in range(3)]
        + [15.0 * MULT[e] * quad[e] for e in range(6)]
    )
    l1 = [1.8 * f["m"][r] for r in range(3)] + [-1.8 * q, -1.8 * f["dx"]] + [1.8 * d[r] for r in range(3)]
    l1 += z(16)
    l2 = (
        [-18.0 * turned[r] for r in range(3)]
        + z(1)
        + [9.0 * f["xqx"]]
        + [-18.0 * turned[r] for r in range(3)]
        + [9.0 * MULT[e] * (f["h"][e] + 2.0 * quad[e]) for e in range(6)]
        + [-18.0 * f["m"][r] for r in range(3)]
        + [9.0 * q]
        + [9.0 * MULT[e] * quad[e] for e in range(6)]
    )
    l3 = [-180.0 * MULT[e] * f["tx"][e] for e in range(6)] + [180.0 * turned[r] for r in range(3)]
    l3 += [-180.0 * MULT[e] * quad[e] for e in range(6)]
    for a, b in ENTRIES:
        for c in range(3):
            term = quad[ENTRY_AT[(a, c)]] * x[b]
            if a != b:
                term = term + quad[ENTRY_AT[(b, c)]] * x[a]
            l3.append(180.0 * term)
    l3 += z(7)
    return [u, v, p, r_, l1, l2, l3]


def tile_setup(pool_ref, sum_scr, near_scr, far_scr, feat_ref, lhs_ref, rhs_ref, place_ref, wide_ref):
    f = pool_features([pool_ref[c] for c in range(13)])
    for n, row in enumerate(sum_rows(f)):
        sum_scr[n * ROWS : (n + 1) * ROWS, :] = row
    for n, row in enumerate(near_rows(f)):
        near_scr[n * 8 : n * 8 + 8, :] = row[0:8]
    at = 0
    for group in far_rows(f):
        for row in group:
            far_scr[at * ROWS : (at + 1) * ROWS, :] = row
            at += 1

    def per_block(b, _):
        sums = sum_scr[pl.ds(b, 64, stride=ROWS), :]
        place_ref[b] = sums[0:8]
        hi, lo = split2(sums)
        parts = []
        for g in range(8):
            parts += [hi[8 * g : 8 * g + 8], lo[8 * g : 8 * g + 8]]
        feat_ref[b] = jnp.concatenate(parts, axis=0).astype(BF16)
        start = 0
        for out_id, count in enumerate((24, 24, 24, 24, 24, 24, 40)):
            rows = far_scr[pl.ds(b + start * ROWS, count, stride=ROWS), :]
            start += count
            hi, lo = split2(rows)
            pad = [jnp.zeros((128 - 3 * count, 128), F32)]
            stacked = jnp.concatenate([hi, lo, hi] + pad, axis=0).astype(BF16)
            rhs_ref[b, :, out_id * 128 : (out_id + 1) * 128] = stacked
        return 0

    lax.fori_loop(0, POOL_BLOCKS, per_block, 0)

    def per_near(b, _):
        start = 0
        for group, count in enumerate((24, 24, 40)):
            rows = near_scr[pl.ds(b + start * 8, count, stride=8), :]
            start += count
            hi, lo = split2(rows)
            stacked = jnp.concatenate([hi, hi, lo, jnp.zeros((128 - 3 * count, 128), F32)], axis=0)
            lhs_ref[b, :, group * 128 : (group + 1) * 128] = stacked.T.astype(BF16)
        place = jnp.concatenate([place_ref[b], jnp.zeros((120, 128), F32)], axis=0).T
        for r in range(3):
            wide_ref[b, r] = jnp.broadcast_to(place[:, r + 1 : r + 2], (128, 128))
        return 0

    lax.fori_loop(0, OWN_BLOCKS, per_near, 0)


def tile_work(near, far, feat_ref, lhs_ref, rhs_ref, place_ref, wide_ref, keep_ref, keep):
    first = mm(lhs_ref[near, :, 0:128], rhs_ref[far, :, 0:512])
    second = mm(lhs_ref[near, :, 128:256], rhs_ref[far, :, 512:768])
    third = mm(lhs_ref[near, :, 256:384], rhs_ref[far, :, 768:896])
    chunk = 32
    names = ("b1", "b2", "b3", "al", "be", "ga", "de", "e1")
    pieces = {name: ([], []) for name in names}
    place = [jnp.broadcast_to(place_ref[far, r + 1 : r + 2, :], (chunk, 128)) for r in range(3)]
    for row in range(0, 128, chunk):
        rows = slice(row, row + chunk)
        diff = [place[r] - wide_ref[near, r, rows, :] for r in range(3)]
        dist = diff[0] * diff[0] + (diff[1] * diff[1] + (diff[2] * diff[2] + SOFTENING))
        root = lax.rsqrt(dist)
        t = root * root
        b0 = root * keep_ref[keep, rows, :]
        b1 = b0 * t
        b2 = b1 * t
        b3 = b2 * t
        b4 = b3 * (1.4 * t)
        b5 = b4 * (1.8 * t)
        u, v = first[rows, 0:128], first[rows, 128:256]
        p, r_ = first[rows, 256:384], first[rows, 384:512]
        l1, l2, l3 = second[rows, 0:128], second[rows, 128:256], third[rows, :]
        al = r_ * b3 - v * b2
        be = p * b3 + u * b2
        ga = r_ * b4 - v * b3
        de = p * b4 + u * b3
        e1 = l1 * b2 + (l2 - u * v) * b3 + (u * r_ - v * p + l3) * b4 + (p * r_) * b5
        for name, value in zip(names, (b1, b2, b3, al, be, ga, de, e1)):
            hi = value.astype(BF16)
            pieces[name][0].append(hi)
            pieces[name][1].append((value - hi.astype(F32)).astype(BF16))
    return {name: (jnp.concatenate(h, axis=0), jnp.concatenate(l, axis=0)) for name, (h, l) in pieces.items()}


def tile_sums(w, near, far, feat_ref, add):
    near_pairs = (
        ("al", "be", 16, ((0, 0),), ((1, 0),)),
        ("e1", "b1", 32, ((2, 0),), ((3, 0), (4, 1))),
        ("b2", "de", 64, ((5, 0), (6, 1), (7, 2), (8, 3)), ((9, 2), (10, 3))),
        ("ga", "b3", 128, ((11, 0), (12, 7)), ((13, 2), (14, 3), (15, 4), (16, 5), (17, 6))),
    )
    far_pairs = (
        ("be", "al", 16, ((0, 0),), ((1, 0),)),
        ("e1", "b1", 32, ((2, 0),), ((3, 0), (4, 1))),
        ("b2", "ga", 64, ((5, 0), (6, 1), (7, 2), (8, 3)), ((9, 2), (10, 3))),
        ("de", "b3", 128, ((11, 0), (12, 7)), ((13, 2), (14, 3), (15, 4), (16, 5), (17, 6))),
    )
    for pairs, source, target, transposed in ((near_pairs, far, near, True), (far_pairs, near, far, False)):
        for one, two, rows, slots_one, slots_two in pairs:
            feats = feat_ref[source, 0:rows, :]
            lhs = jnp.concatenate([feats, feats], axis=1)
            if transposed:
                rhs = jnp.concatenate(
                    [jnp.concatenate(w[one], axis=1), jnp.concatenate(w[two], axis=1)], axis=0
                )
                out = nt_dot(lhs, rhs)
            else:
                rhs = jnp.concatenate(
                    [jnp.concatenate([w[one][s], w[two][s]], axis=1) for s in range(2)], axis=0
                )
                out = mm(lhs, rhs)
            for half, slots in enumerate((slots_one, slots_two)):
                lanes = slice(128 * half, 128 * half + 128)
                for slot, group in slots:
                    at = 16 * group
                    add(target, slot, out[at : at + 8, lanes] + out[at + 8 : at + 16, lanes])


def finish_sums(load, f):
    x, q, d, quad = f["x"], f["q"], f["d"], f["quad"]
    turned = f["turned"]
    a_one, a_x = load(0, 0), [load(0, 1 + r) for r in range(3)]
    ap_d = [load(1, 5 + r) for r in range(3)]
    e_one, e_x = load(2, 0), [load(2, 1 + r) for r in range(3)]
    b1_q, b1_d = load(3, 4), [load(3, 5 + r) for r in range(3)]
    b1_qx = [load(4, r) for r in range(3)]
    b2_q, b2_m = load(5, 4), [load(6, 3 + r) for r in range(3)]

    def wide(slot):
        flat = lambda n: load(slot + n // 8, n % 8)
        return [flat(e) for e in range(6)], [flat(6 + r) for r in range(3)]

    b2_quad, b2_t = wide(7)
    b2_h = [load(7 + (9 + e) // 8, (9 + e) % 8) for e in range(6)]
    cp_quad, cp_t = wide(9)
    c_one, c_x = load(11, 0), [load(11, 1 + r) for r in range(3)]
    c_xx = [load(12, e) for e in range(6)]
    b3_quad, b3_t = wide(13)
    b3_tx = [load(15, e) for e in range(6)]
    b3_outer = [[load(15 + (6 + 3 * e + c) // 8, (6 + 3 * e + c) % 8) for c in range(3)] for e in range(6)]

    b2_quad_x = mat_vec(b2_quad, x)
    b3_quad_x = mat_vec(b3_quad, x)
    cp_quad_x = mat_vec(cp_quad, x)
    b2_turn = [b2_t[r] - b2_quad_x[r] for r in range(3)]
    b3_turn = [b3_t[r] - b3_quad_x[r] for r in range(3)]
    cp_turn = [cp_t[r] - cp_quad_x[r] for r in range(3)]
    b1_r = [b1_qx[r] - x[r] * b1_q for r in range(3)]
    a_r = [a_x[r] - x[r] * a_one for r in range(3)]
    e_r = [e_x[r] - x[r] * e_one for r in range(3)]
    c_r = [c_x[r] - x[r] * c_one for r in range(3)]
    b2_r = [b2_m[r] - x[r] * b2_q for r in range(3)]

    slope_d = [a_r[r] + b1_r[r] + b1_d[r] - 6.0 * b2_turn[r] for r in range(3)]

    sx_c = sym_outer(c_x, x)
    sx_m = sym_outer(b2_m, x)
    sx_t = sym_outer(b3_t, x)
    sx_q = sym_outer(b3_quad_x, x)
    mixed = [
        [sum_list([b3_outer[ENTRY_AT[(a, c)]][b] * x[c] for c in range(3)]) for b in range(3)] for a in range(3)
    ]
    slope_q = []
    for e, (a, b) in enumerate(ENTRIES):
        ym = mixed[a][b] if a == b else 0.5 * (mixed[a][b] + mixed[b][a])
        slope_q.append(
            5.0 * (c_xx[e] - 2.0 * sx_c[e] + c_one * f["xx"][e])
            + 3.0 * (b2_h[e] - 2.0 * sx_m[e] + b2_q * f["xx"][e])
            + 6.0 * b2_quad[e]
            - 60.0 * (b3_tx[e] - sx_t[e] - ym + sx_q[e])
        )

    inner = [10.0 * c_r[r] + 6.0 * b2_r[r] - 60.0 * b3_turn[r] for r in range(3)]
    inner = mat_vec(quad, inner)
    b2_quad_d = mat_vec(b2_quad, d)
    b3_quad_t = mat_vec(b3_quad, turned)
    force = []
    for a in range(3):
        spun = sum_list(
            [
                b3_outer[ENTRY_AT[(a, b)]][c] * quad[ENTRY_AT[(b, c)]]
                for b in range(3)
                for c in range(3)
            ]
        )
        force.append(
            -q * (b1_r[a] + b1_d[a])
            - (5.0 / 3.0) * e_r[a]
            + d[a] * (a_one + b1_q)
            - ap_d[a]
            + inner[a]
            + 10.0 * cp_turn[a]
            + 6.0 * q * b2_turn[a]
            - 6.0 * b2_quad_d[a]
            - 60.0 * (spun - b3_quad_t[a])
        )

    full = lambda m, r, c: m[ENTRY_AT[(r, c)]]

    def commutator(r, c):
        return sum_list(
            [full(quad, r, k) * full(slope_q, k, c) - full(slope_q, r, k) * full(quad, k, c) for k in range(3)]
        )

    twist = cross3(d, slope_d)
    torque = [
        2.0 * commutator(2, 1) - twist[0],
        2.0 * commutator(0, 2) - twist[1],
        2.0 * commutator(1, 0) - twist[2],
    ]
    return force, torque


def tiles_body(
    coords_ref, mult_ref, import_ref, pairs_ref, count_ref, own_out, halo_out,
    pool_ref, sum_scr, near_scr, far_scr, feat_ref, lhs_ref, rhs_ref, place_ref, wide_ref, keep_ref, acc_ref,
):
    for c in range(13):
        src, at = (coords_ref, 8 * c) if c < 3 else (mult_ref, 8 * (c - 3))
        pool_ref[c, 0:8, :] = src[at : at + 8, :]
        for k in range(3):
            pool_ref[c, 8 + 4 * k : 12 + 4 * k, :] = import_ref[k, 4 * c : 4 * c + 4, :]
        pool_ref[c, 20:24, :] = jnp.zeros((4, 128), F32)
    above = lax.broadcasted_iota(jnp.int32, (128, 128), 0) < lax.broadcasted_iota(jnp.int32, (128, 128), 1)
    keep_ref[0] = jnp.ones((128, 128), F32)
    keep_ref[1] = jnp.where(above, 1.0, 0.0).astype(F32)
    acc_ref[...] = jnp.zeros_like(acc_ref)
    tile_setup(pool_ref, sum_scr, near_scr, far_scr, feat_ref, lhs_ref, rhs_ref, place_ref, wide_ref)

    def add(block, slot, value):
        at = pl.multiple_of(block * (8 * ACC_GROUPS) + 8 * slot, 8)
        acc_ref[pl.ds(at, 8), :] += value

    def step(t, _):
        near, far = pairs_ref[0, 0, 0, t], pairs_ref[0, 0, 1, t]
        keep = jnp.where(near == far, 1, 0)
        w = tile_work(near, far, feat_ref, lhs_ref, rhs_ref, place_ref, wide_ref, keep_ref, keep)
        tile_sums(w, near, far, feat_ref, add)
        return 0

    lax.fori_loop(0, count_ref[0, 0], step, 0)

    def load(slot, row):
        return acc_ref[pl.ds(8 * slot + row, ROWS, stride=8 * ACC_GROUPS), :]

    force, torque = finish_sums(load, pool_features([pool_ref[c] for c in range(13)]))
    for c, rows in enumerate(force + torque):
        own_out[c] = rows[0:8]
        for k in range(3):
            halo_out[k, 4 * c : 4 * c + 4, :] = rows[8 + 4 * k : 12 + 4 * k]


def returned_rows(back_ref, comps):
    return [[back_ref[k, 4 * c + j : 4 * c + j + 1, :] for k in range(3) for j in range(4)] for c in range(comps)]


def frame_body(
    sizes, own_ref, halo_ref, coords_ref, import_ref, face_ref, frame_ref, out_ref,
    back_ref, spread_ref, last_ref, send_sem, recv_sem,
):
    up, down = neighbours(sizes)
    greet(down)
    pl.semaphore_wait(pltpu.get_barrier_semaphore(), 3)
    copies = send_sets(halo_ref, back_ref, send_sem.at[0], recv_sem.at[0], up)

    blocks, lanes = face_masks([face_ref[k, j : j + 1, :] for k in range(3) for j in range(4)])
    index = [frame_ref[8 * m : 8 * m + 8, :] for m in range(3)]
    low = [i & 127 for i in index]
    high = [i >> 7 for i in index]
    spots = [[jnp.zeros((8, 128), F32) for _ in range(3)] for _ in range(3)]
    for b in range(POOL_BLOCKS):
        rows = []
        for c in range(3):
            if b < OWN_BLOCKS:
                rows.append(coords_ref[8 * c + b : 8 * c + b + 1, :])
            else:
                k, j = divmod(b - OWN_BLOCKS, 4)
                rows.append(import_ref[k, 4 * c + j : 4 * c + j + 1, :])
        for m in range(3):
            hit = high[m] == b
            for c in range(3):
                spots[m][c] = jnp.where(hit, lane_gather(rows[c], low[m]), spots[m][c])
    place = [coords_ref[8 * c : 8 * c + 8, :] for c in range(3)]
    levers, scales = [], []
    for m in range(3):
        lever = [spots[m][c] - place[c] for c in range(3)]
        levers.append(lever)
        scales.append(1.0 / (3.0 * (dot3(lever, lever) + LEVER_SOFT)))
    sub24 = lax.broadcasted_iota(jnp.int32, (ROWS, 128), 0)
    sub128 = lax.broadcasted_iota(jnp.int32, (128, 128), 0)
    hits, hot = [], []
    for m in range(3):
        for b in range(OWN_BLOCKS):
            hits.append(jnp.broadcast_to(high[m][b : b + 1], (ROWS, 128)) == sub24)
            lane = jnp.broadcast_to(low[m][b : b + 1], (128, 128)) == sub128
            hot.append(jnp.where(lane, 1.0, 0.0).astype(BF16))

    for copy in copies:
        copy.wait()
    added = scatter_faces(returned_rows(back_ref, 6), blocks, lanes)
    owned = [own_ref[c] + added[c] for c in range(6)]
    torque = owned[3:6]
    kept = [jnp.zeros((8, 128), F32) for _ in range(3)]
    columns = []
    for m in range(3):
        push = [w * scales[m] for w in cross3(torque, levers[m])]
        kept = [kept[c] + push[c] for c in range(3)]
        halves = [split2(w) for w in push]
        for b in range(OWN_BLOCKS):
            hit = hits[8 * m + b]
            parts = []
            for c in range(3):
                for half in halves[c]:
                    parts.append(jnp.where(hit, jnp.broadcast_to(half[b : b + 1], (ROWS, 128)), 0.0))
            columns.append(jnp.concatenate(parts, axis=0).astype(BF16))
    out = nt_dot(jnp.concatenate(columns, axis=1), jnp.concatenate(hot, axis=1))
    forces = []
    for c in range(3):
        rows = out[48 * c : 48 * c + 24] + out[48 * c + 24 : 48 * c + 48]
        forces.append(owned[c] + rows[0:8] - kept[c])
        for k in range(3):
            spread_ref[k, 4 * c : 4 * c + 4, :] = rows[8 + 4 * k : 12 + 4 * k]
    spread_ref[:, 12:16, :] = jnp.zeros((3, 4, 128), F32)
    for copy in send_sets(spread_ref, last_ref, send_sem.at[1], recv_sem.at[1], up):
        copy.wait()
    added = scatter_faces(returned_rows(last_ref, 3), blocks, lanes)
    for c in range(3):
        out_ref[8 * c : 8 * c + 8, :] = forces[c] + added[c]


def vmem(count):
    return [pl.BlockSpec(memory_space=pltpu.VMEM)] * count


def shape(*dims):
    return jax.ShapeDtypeStruct(dims, F32)


def import_halo(sizes, coords, multipoles, face_atoms):
    return pl.pallas_call(
        functools.partial(import_body, sizes),
        out_shape=shape(3, 56, 128),
        in_specs=vmem(3),
        out_specs=pl.BlockSpec(memory_space=pltpu.VMEM),
        scratch_shapes=[
            pltpu.VMEM((3, 56, 128), F32),
            pltpu.SemaphoreType.DMA((3,)),
            pltpu.SemaphoreType.DMA((3,)),
        ],
        compiler_params=pltpu.CompilerParams(collective_id=0, has_side_effects=True),
    )(coords, multipoles, face_atoms)


def pair_tiles(coords, multipoles, imports, tile_pairs, tile_count):
    return pl.pallas_call(
        tiles_body,
        out_shape=(shape(6, 8, 128), shape(3, 24, 128)),
        in_specs=vmem(3) + [pl.BlockSpec(memory_space=pltpu.SMEM)] * 2,
        out_specs=vmem(2),
        scratch_shapes=[
            pltpu.VMEM((13, ROWS, 128), F32),
            pltpu.VMEM((64 * ROWS, 128), F32),
            pltpu.VMEM((88 * 8, 128), F32),
            pltpu.VMEM((184 * ROWS, 128), F32),
            pltpu.VMEM((POOL_BLOCKS, 128, 128), BF16),
            pltpu.VMEM((OWN_BLOCKS, 128, 384), BF16),
            pltpu.VMEM((POOL_BLOCKS, 128, 896), BF16),
            pltpu.VMEM((POOL_BLOCKS, 8, 128), F32),
            pltpu.VMEM((OWN_BLOCKS, 3, 128, 128), F32),
            pltpu.VMEM((2, 128, 128), F32),
            pltpu.VMEM((ROWS * 8 * ACC_GROUPS, 128), F32),
        ],
        compiler_params=pltpu.CompilerParams(vmem_limit_bytes=48 << 20),
    )(coords, multipoles, imports, tile_pairs, tile_count)


def frame_forces(sizes, owned, halo, coords, imports, face_atoms, frame_atoms):
    return pl.pallas_call(
        functools.partial(frame_body, sizes),
        out_shape=shape(24, 128),
        in_specs=vmem(6),
        out_specs=pl.BlockSpec(memory_space=pltpu.VMEM),
        scratch_shapes=[
            pltpu.VMEM((3, 24, 128), F32),
            pltpu.VMEM((3, 16, 128), F32),
            pltpu.VMEM((3, 16, 128), F32),
            pltpu.SemaphoreType.DMA((2, 3)),
            pltpu.SemaphoreType.DMA((2, 3)),
        ],
        compiler_params=pltpu.CompilerParams(collective_id=1, has_side_effects=True),
    )(owned, halo, coords, imports, face_atoms, frame_atoms)


def solution(mesh):
    sizes = (mesh.shape["gx"], mesh.shape["gy"])

    def shards(coords, multipoles, face_atoms, tile_pairs, tile_count, frame_atoms, send_list, send_count):
        coords = coords.reshape(24, 128)
        multipoles = multipoles.reshape(80, 128)
        face_atoms = face_atoms.reshape(3, 4, 128)
        frame_atoms = frame_atoms.reshape(24, 128)
        imports = import_halo(sizes, coords, multipoles, face_atoms)
        owned, halo = pair_tiles(coords, multipoles, imports, tile_pairs, tile_count)
        forces = frame_forces(sizes, owned, halo, coords, imports, face_atoms, frame_atoms)
        return forces.reshape(1, 1, 3, 1024)

    four = P("gx", "gy", None, None)
    placed = (four, four, four, four, P("gx", "gy"), four, four, P("gx", "gy", None))
    return jax.shard_map(shards, mesh=mesh, in_specs=placed, out_specs=four, check_vma=False)
```

```python
import functools

import jax
import jax.numpy as jnp
from jax import lax
from jax.experimental import pallas as pl
from jax.experimental.pallas import tpu as pltpu
from jax.sharding import PartitionSpec as P

SOFTENING = 0.5
LEVER_SOFT = 0.04
OWN_BLOCKS = 8
POOL_BLOCKS = 20
ROWS = 24
ENTRIES = ((0, 0), (1, 1), (2, 2), (0, 1), (0, 2), (1, 2))
ENTRY_AT = {(0, 0): 0, (1, 1): 1, (2, 2): 2, (0, 1): 3, (1, 0): 3, (0, 2): 4, (2, 0): 4, (1, 2): 5, (2, 1): 5}
MULT = (1.0, 1.0, 1.0, 2.0, 2.0, 2.0)
F32 = jnp.float32
BF16 = jnp.bfloat16
ACC_GROUPS = 18
MESH = pl.DeviceIdType.MESH


def cross3(a, b):
    return (a[1] * b[2] - a[2] * b[1], a[2] * b[0] - a[0] * b[2], a[0] * b[1] - a[1] * b[0])


def dot3(a, b):
    return a[0] * b[0] + a[1] * b[1] + a[2] * b[2]


def mat_vec(m, v):
    return [sum_list([m[ENTRY_AT[(r, c)]] * v[c] for c in range(3)]) for r in range(3)]


def sum_list(items):
    total = items[0]
    for item in items[1:]:
        total = total + item
    return total


def sym_outer(a, b):
    out = []
    for r, c in ENTRIES:
        if r == c:
            out.append(a[r] * b[r])
        else:
            out.append(0.5 * (a[r] * b[c] + a[c] * b[r]))
    return out


def split2(value):
    hi = value.astype(BF16).astype(F32)
    lo = (value - hi).astype(BF16).astype(F32)
    return hi, lo


def nt_dot(a, b):
    return lax.dot_general(a, b, (((1,), (1,)), ((), ())), preferred_element_type=F32)


def mm(a, b):
    return lax.dot_general(a, b, (((1,), (0,)), ((), ())), preferred_element_type=F32)


def lane_gather(row, index):
    table = jnp.broadcast_to(row, (8, 128))
    return jnp.take_along_axis(table, index, axis=1)


def face_masks(face_rows):
    sub8 = lax.broadcasted_iota(jnp.int32, (8, 128), 0)
    sub128 = lax.broadcasted_iota(jnp.int32, (128, 128), 0)
    blocks, lanes = [], []
    for row in face_rows:
        blocks.append(jnp.broadcast_to(row >> 7, (8, 128)) == sub8)
        hit = jnp.broadcast_to(row & 127, (128, 128)) == sub128
        lanes.append(jnp.where(hit, 1.0, 0.0).astype(BF16))
    return blocks, lanes


def scatter_faces(values, blocks, lanes):
    comps = len(values)
    columns = []
    for j in range(len(blocks)):
        parts = []
        for c in range(comps):
            hi, lo = split2(values[c][j])
            parts.append(jnp.where(blocks[j], jnp.broadcast_to(hi, (8, 128)), 0.0))
            parts.append(jnp.where(blocks[j], jnp.broadcast_to(lo, (8, 128)), 0.0))
        columns.append(jnp.concatenate(parts, axis=0).astype(BF16))
    lhs = jnp.concatenate(columns, axis=1)
    rhs = jnp.concatenate(lanes, axis=1)
    out = nt_dot(lhs, rhs)
    return [out[16 * c : 16 * c + 8] + out[16 * c + 8 : 16 * c + 16] for c in range(comps)]


def neighbours(sizes):
    gx, gy = lax.axis_index("gx"), lax.axis_index("gy")
    nx, ny = sizes
    up = (lax.rem(gx + 1, nx), lax.rem(gy + 1, ny))
    down = (lax.rem(gx + nx - 1, nx), lax.rem(gy + ny - 1, ny))
    return [[(to[0], gy), (gx, to[1]), (to[0], to[1])] for to in (up, down)]


def greet(senders):
    for peer in senders:
        pl.semaphore_signal(pltpu.get_barrier_semaphore(), inc=1, device_id=peer, device_id_type=MESH)


def send_sets(send_ref, recv_ref, send_sem, recv_sem, targets):
    copies = []
    for k, peer in enumerate(targets):
        copy = pltpu.make_async_remote_copy(
            src_ref=send_ref.at[k],
            dst_ref=recv_ref.at[k],
            send_sem=send_sem.at[k],
            recv_sem=recv_sem.at[k],
            device_id=peer,
            device_id_type=MESH,
        )
        copy.start()
        copies.append(copy)
    return copies


def import_body(sizes, coords_ref, mult_ref, face_ref, recv_ref, send_ref, send_sem, recv_sem):
    up, down = neighbours(sizes)
    greet(up)
    face = jnp.concatenate([face_ref[k] for k in range(3)] + [jnp.zeros((4, 128), jnp.int32)], axis=0)
    shift = lax.broadcasted_iota(jnp.int32, (16, 128), 0)
    shift_x = jnp.where((shift < 4) | (shift >= 8), 1.0, 0.0).astype(F32)
    shift_y = jnp.where(shift >= 4, 1.0, 0.0).astype(F32)
    halves = [face[0:8], face[8:16]]
    lows = [h & 127 for h in halves]
    highs = [h >> 7 for h in halves]
    for c in range(13):
        src, at = (coords_ref, 8 * c) if c < 3 else (mult_ref, 8 * (c - 3))
        got = []
        for part in range(2):
            total = jnp.zeros((8, 128), F32)
            for b in range(OWN_BLOCKS):
                picked = lane_gather(src[at + b : at + b + 1, :], lows[part])
                total = jnp.where(highs[part] == b, picked, total)
            got.append(total)
        rows = jnp.concatenate(got, axis=0)
        if c == 0:
            rows = rows + shift_x
        if c == 1:
            rows = rows + shift_y
        for k in range(3):
            send_ref[k, 4 * c : 4 * c + 4, :] = rows[4 * k : 4 * k + 4]
    for k in range(3):
        send_ref[k, 52:56, :] = jnp.zeros((4, 128), F32)
    pl.semaphore_wait(pltpu.get_barrier_semaphore(), 3)
    for copy in send_sets(send_ref, recv_ref, send_sem, recv_sem, down):
        copy.wait()


def pool_features(pool):
    x = [pool[0] - 1.0, pool[1] - 1.0, pool[2] - 0.5]
    q = pool[3]
    d = [pool[4], pool[5], pool[6]]
    quad = [pool[7], pool[8], pool[9], pool[10], pool[11], pool[12]]
    one = jnp.ones_like(q)
    xx = [x[r] * x[c] for r, c in ENTRIES]
    qx = [q * x[r] for r in range(3)]
    m = [qx[r] + d[r] for r in range(3)]
    turned = mat_vec(quad, x)
    dx = dot3(d, x)
    xqx = dot3(x, turned)
    sdx = sym_outer(d, x)
    h = [q * xx[e] + 2.0 * sdx[e] for e in range(6)]
    tx = sym_outer(turned, x)
    outer = [[quad[e] * x[c] for c in range(3)] for e in range(6)]
    return dict(one=one, x=x, q=q, d=d, quad=quad, xx=xx, qx=qx, m=m, turned=turned, dx=dx, xqx=xqx, h=h, tx=tx, outer=outer)


def sum_rows(f):
    zero = jnp.zeros_like(f["one"])
    rows = [f["one"], *f["x"], f["q"], *f["d"]]
    rows += [*f["qx"], *f["m"], zero, zero]
    rows += [*f["quad"], *f["turned"], *f["h"], zero]
    rows += [*f["tx"]] + [f["outer"][e][c] for e in range(6) for c in range(3)]
    rows += [*f["xx"], zero, zero]
    return rows


def near_rows(f):
    zero = jnp.zeros_like(f["one"])
    first = [*f["d"], f["dx"], *f["quad"], *f["turned"], f["xqx"], f["one"], *f["x"], *f["xx"]]
    second = [*f["d"], f["dx"], f["q"], *f["qx"], *f["quad"], *f["turned"], f["xqx"], *f["h"]]
    third = [*f["quad"], *f["turned"], *f["tx"]] + [f["outer"][e][c] for e in range(6) for c in range(3)]
    return first + second + third + [zero] * 7


def far_rows(f):
    zero = jnp.zeros_like(f["one"])
    one = f["one"]
    x, d, q, xx = f["x"], f["d"], f["q"], f["xx"]
    quad, turned = f["quad"], f["turned"]
    z = lambda n: [zero] * n
    u = [3.0 * x[r] for r in range(3)] + [-3.0 * one] + z(20)
    v = z(14) + [3.0 * f["dx"]] + [-3.0 * d[r] for r in range(3)] + z(6)
    p = z(4) + [15.0 * MULT[e] * xx[e] for e in range(6)] + [-30.0 * x[r] for r in range(3)] + [15.0 * one] + z(10)
    r_ = (
        z(14)
        + [15.0 * f["xqx"]]
        + [-30.0 * turned[r] for r in range(3)]
        + [15.0 * MULT[e] * quad[e] for e in range(6)]
    )
    l1 = [1.8 * f["m"][r] for r in range(3)] + [-1.8 * q, -1.8 * f["dx"]] + [1.8 * d[r] for r in range(3)]
    l1 += z(16)
    l2 = (
        [-18.0 * turned[r] for r in range(3)]
        + z(1)
        + [9.0 * f["xqx"]]
        + [-18.0 * turned[r] for r in range(3)]
        + [9.0 * MULT[e] * (f["h"][e] + 2.0 * quad[e]) for e in range(6)]
        + [-18.0 * f["m"][r] for r in range(3)]
        + [9.0 * q]
        + [9.0 * MULT[e] * quad[e] for e in range(6)]
    )
    l3 = [-252.0 * MULT[e] * f["tx"][e] for e in range(6)] + [252.0 * turned[r] for r in range(3)]
    l3 += [-252.0 * MULT[e] * quad[e] for e in range(6)]
    for a, b in ENTRIES:
        for c in range(3):
            term = quad[ENTRY_AT[(a, c)]] * x[b]
            if a != b:
                term = term + quad[ENTRY_AT[(b, c)]] * x[a]
            l3.append(252.0 * term)
    l3 += z(7)
    return [u, v, p, r_, l1, l2, l3]


def tile_setup(pool_ref, sum_scr, near_scr, far_scr, feat_ref, lhs_ref, rhs_ref, place_ref, wide_ref):
    f = pool_features([pool_ref[c] for c in range(13)])
    for n, row in enumerate(sum_rows(f)):
        sum_scr[n * ROWS : (n + 1) * ROWS, :] = row
    for n, row in enumerate(near_rows(f)):
        near_scr[n * 8 : n * 8 + 8, :] = row[0:8]
    at = 0
    for group in far_rows(f):
        for row in group:
            far_scr[at * ROWS : (at + 1) * ROWS, :] = row
            at += 1

    def per_block(b, _):
        sums = sum_scr[pl.ds(b, 64, stride=ROWS), :]
        place_ref[b] = sums[0:8]
        hi, lo = split2(sums)
        parts = []
        for g in range(8):
            parts += [hi[8 * g : 8 * g + 8], lo[8 * g : 8 * g + 8]]
        feat_ref[b] = jnp.concatenate(parts, axis=0).astype(BF16)
        start = 0
        for out_id, count in enumerate((24, 24, 24, 24, 24, 24, 40)):
            rows = far_scr[pl.ds(b + start * ROWS, count, stride=ROWS), :]
            start += count
            hi, lo = split2(rows)
            pad = [jnp.zeros((128 - 3 * count, 128), F32)]
            stacked = jnp.concatenate([hi, lo, hi] + pad, axis=0).astype(BF16)
            rhs_ref[b, :, out_id * 128 : (out_id + 1) * 128] = stacked
        return 0

    lax.fori_loop(0, POOL_BLOCKS, per_block, 0, unroll=4)

    def per_near(b, _):
        start = 0
        for group, count in enumerate((24, 24, 40)):
            rows = near_scr[pl.ds(b + start * 8, count, stride=8), :]
            start += count
            hi, lo = split2(rows)
            stacked = jnp.concatenate([hi, hi, lo, jnp.zeros((128 - 3 * count, 128), F32)], axis=0)
            lhs_ref[b, :, group * 128 : (group + 1) * 128] = stacked.T.astype(BF16)
        place = jnp.concatenate([place_ref[b], jnp.zeros((120, 128), F32)], axis=0).T
        for r in range(3):
            wide_ref[b, r] = jnp.broadcast_to(place[:, r + 1 : r + 2], (128, 128))
        return 0

    lax.fori_loop(0, OWN_BLOCKS, per_near, 0, unroll=4)


def tile_work(near, far, feat_ref, lhs_ref, rhs_ref, place_ref, wide_ref, keep_ref, keep):
    first = mm(lhs_ref[near, :, 0:128], rhs_ref[far, :, 0:512])
    second = mm(lhs_ref[near, :, 128:256], rhs_ref[far, :, 512:768])
    third = mm(lhs_ref[near, :, 256:384], rhs_ref[far, :, 768:896])
    chunk = 32
    names = ("b1", "b2", "b3", "al", "be", "ga", "de", "e1")
    pieces = {name: ([], []) for name in names}
    place = [jnp.broadcast_to(place_ref[far, r + 1 : r + 2, :], (chunk, 128)) for r in range(3)]
    for row in range(0, 128, chunk):
        rows = slice(row, row + chunk)
        diff = [place[r] - wide_ref[near, r, rows, :] for r in range(3)]
        dist = diff[0] * diff[0] + (diff[1] * diff[1] + (diff[2] * diff[2] + SOFTENING))
        root = lax.rsqrt(dist)
        t = root * root
        b0 = root * keep_ref[keep, rows, :]
        b1 = b0 * t
        b2 = b1 * t
        b3 = b2 * t
        u, v = first[rows, 0:128], first[rows, 128:256]
        pt, rt = first[rows, 256:384] * t, first[rows, 384:512] * t
        l1, l2, l3 = second[rows, 0:128], second[rows, 128:256], third[rows, :]
        gr, gp = 1.4 * rt - v, 1.4 * pt + u
        al = b2 * (rt - v)
        be = b2 * (pt + u)
        ga = b3 * gr
        de = b3 * gp
        e1 = b2 * (l1 + t * (l2 + gr * gp + 0.56 * (rt * pt) + t * l3))
        for name, value in zip(names, (b1, b2, b3, al, be, ga, de, e1)):
            hi = value.astype(BF16)
            pieces[name][0].append(hi)
            pieces[name][1].append((value - hi.astype(F32)).astype(BF16))
    return {name: (jnp.concatenate(h, axis=0), jnp.concatenate(l, axis=0)) for name, (h, l) in pieces.items()}


def tile_sums(w, near, far, feat_ref, add):
    near_pairs = (
        ("al", "be", 16, ((0, 0),), ((1, 0),)),
        ("e1", "b1", 32, ((2, 0),), ((3, 0), (4, 1))),
        ("b2", "de", 64, ((5, 0), (6, 1), (7, 2), (8, 3)), ((9, 2), (10, 3))),
        ("ga", "b3", 128, ((11, 0), (12, 7)), ((13, 2), (14, 3), (15, 4), (16, 5), (17, 6))),
    )
    far_pairs = (
        ("be", "al", 16, ((0, 0),), ((1, 0),)),
        ("e1", "b1", 32, ((2, 0),), ((3, 0), (4, 1))),
        ("b2", "ga", 64, ((5, 0), (6, 1), (7, 2), (8, 3)), ((9, 2), (10, 3))),
        ("de", "b3", 128, ((11, 0), (12, 7)), ((13, 2), (14, 3), (15, 4), (16, 5), (17, 6))),
    )
    for pairs, source, target, transposed in ((near_pairs, far, near, True), (far_pairs, near, far, False)):
        for one, two, rows, slots_one, slots_two in pairs:
            feats = feat_ref[source, 0:rows, :]
            lhs = jnp.concatenate([feats, feats], axis=1)
            if transposed:
                rhs = jnp.concatenate(
                    [jnp.concatenate([w[one][s].T, w[two][s].T], axis=1) for s in range(2)], axis=0
                )
                out = mm(lhs, rhs)
            else:
                rhs = jnp.concatenate(
                    [jnp.concatenate([w[one][s], w[two][s]], axis=1) for s in range(2)], axis=0
                )
                out = mm(lhs, rhs)
            for half, slots in enumerate((slots_one, slots_two)):
                lanes = slice(128 * half, 128 * half + 128)
                for slot, group in slots:
                    at = 16 * group
                    add(target, slot, out[at : at + 8, lanes] + out[at + 8 : at + 16, lanes])


def finish_sums(load, f):
    x, q, d, quad = f["x"], f["q"], f["d"], f["quad"]
    turned = f["turned"]
    a_one, a_x = load(0, 0), [load(0, 1 + r) for r in range(3)]
    ap_d = [load(1, 5 + r) for r in range(3)]
    e_one, e_x = load(2, 0), [load(2, 1 + r) for r in range(3)]
    b1_q, b1_d = load(3, 4), [load(3, 5 + r) for r in range(3)]
    b1_qx = [load(4, r) for r in range(3)]
    b2_q, b2_m = load(5, 4), [load(6, 3 + r) for r in range(3)]

    def wide(slot):
        flat = lambda n: load(slot + n // 8, n % 8)
        return [flat(e) for e in range(6)], [flat(6 + r) for r in range(3)]

    b2_quad, b2_t = wide(7)
    b2_h = [load(7 + (9 + e) // 8, (9 + e) % 8) for e in range(6)]
    cp_quad, cp_t = wide(9)
    c_one, c_x = load(11, 0), [load(11, 1 + r) for r in range(3)]
    c_xx = [load(12, e) for e in range(6)]
    b3_quad, b3_t = wide(13)
    b3_tx = [load(15, e) for e in range(6)]
    b3_outer = [[load(15 + (6 + 3 * e + c) // 8, (6 + 3 * e + c) % 8) for c in range(3)] for e in range(6)]

    b2_quad_x = mat_vec(b2_quad, x)
    b3_quad_x = mat_vec(b3_quad, x)
    cp_quad_x = mat_vec(cp_quad, x)
    b2_turn = [b2_t[r] - b2_quad_x[r] for r in range(3)]
    b3_turn = [b3_t[r] - b3_quad_x[r] for r in range(3)]
    cp_turn = [cp_t[r] - cp_quad_x[r] for r in range(3)]
    b1_r = [b1_qx[r] - x[r] * b1_q for r in range(3)]
    a_r = [a_x[r] - x[r] * a_one for r in range(3)]
    e_r = [e_x[r] - x[r] * e_one for r in range(3)]
    c_r = [c_x[r] - x[r] * c_one for r in range(3)]
    b2_r = [b2_m[r] - x[r] * b2_q for r in range(3)]

    slope_d = [a_r[r] + b1_r[r] + b1_d[r] - 6.0 * b2_turn[r] for r in range(3)]

    sx_c = sym_outer(c_x, x)
    sx_m = sym_outer(b2_m, x)
    sx_t = sym_outer(b3_t, x)
    sx_q = sym_outer(b3_quad_x, x)
    mixed = [
        [sum_list([b3_outer[ENTRY_AT[(a, c)]][b] * x[c] for c in range(3)]) for b in range(3)] for a in range(3)
    ]
    slope_q = []
    for e, (a, b) in enumerate(ENTRIES):
        ym = mixed[a][b] if a == b else 0.5 * (mixed[a][b] + mixed[b][a])
        slope_q.append(
            5.0 * (c_xx[e] - 2.0 * sx_c[e] + c_one * f["xx"][e])
            + 3.0 * (b2_h[e] - 2.0 * sx_m[e] + b2_q * f["xx"][e])
            + 6.0 * b2_quad[e]
            - 60.0 * (b3_tx[e] - sx_t[e] - ym + sx_q[e])
        )

    inner = [10.0 * c_r[r] + 6.0 * b2_r[r] - 60.0 * b3_turn[r] for r in range(3)]
    inner = mat_vec(quad, inner)
    b2_quad_d = mat_vec(b2_quad, d)
    b3_quad_t = mat_vec(b3_quad, turned)
    force = []
    for a in range(3):
        spun = sum_list(
            [
                b3_outer[ENTRY_AT[(a, b)]][c] * quad[ENTRY_AT[(b, c)]]
                for b in range(3)
                for c in range(3)
            ]
        )
        force.append(
            -q * (b1_r[a] + b1_d[a])
            - (5.0 / 3.0) * e_r[a]
            + d[a] * (a_one + b1_q)
            - ap_d[a]
            + inner[a]
            + 10.0 * cp_turn[a]
            + 6.0 * q * b2_turn[a]
            - 6.0 * b2_quad_d[a]
            - 60.0 * (spun - b3_quad_t[a])
        )

    full = lambda m, r, c: m[ENTRY_AT[(r, c)]]

    def commutator(r, c):
        return sum_list(
            [full(quad, r, k) * full(slope_q, k, c) - full(slope_q, r, k) * full(quad, k, c) for k in range(3)]
        )

    twist = cross3(d, slope_d)
    torque = [
        2.0 * commutator(2, 1) - twist[0],
        2.0 * commutator(0, 2) - twist[1],
        2.0 * commutator(1, 0) - twist[2],
    ]
    return force, torque


def tiles_body(
    coords_ref, mult_ref, import_ref, pairs_ref, count_ref, own_out, halo_out,
    pool_ref, sum_scr, near_scr, far_scr, feat_ref, lhs_ref, rhs_ref, place_ref, wide_ref, keep_ref, acc_ref,
):
    for c in range(13):
        src, at = (coords_ref, 8 * c) if c < 3 else (mult_ref, 8 * (c - 3))
        pool_ref[c, 0:8, :] = src[at : at + 8, :]
        for k in range(3):
            pool_ref[c, 8 + 4 * k : 12 + 4 * k, :] = import_ref[k, 4 * c : 4 * c + 4, :]
        pool_ref[c, 20:24, :] = jnp.zeros((4, 128), F32)
    above = lax.broadcasted_iota(jnp.int32, (128, 128), 0) < lax.broadcasted_iota(jnp.int32, (128, 128), 1)
    keep_ref[0] = jnp.ones((128, 128), F32)
    keep_ref[1] = jnp.where(above, 1.0, 0.0).astype(F32)
    keep_ref[2] = jnp.zeros((128, 128), F32)
    acc_ref[...] = jnp.zeros_like(acc_ref)
    tile_setup(pool_ref, sum_scr, near_scr, far_scr, feat_ref, lhs_ref, rhs_ref, place_ref, wide_ref)

    def add(block, slot, value):
        at = pl.multiple_of(block * (8 * ACC_GROUPS) + 8 * slot, 8)
        acc_ref[pl.ds(at, 8), :] += value

    def one(t):
        near, far = pairs_ref[0, 0, 0, t], pairs_ref[0, 0, 1, t]
        keep = jnp.where(t < count_ref[0, 0], jnp.where(near == far, 1, 0), 2)
        w = tile_work(near, far, feat_ref, lhs_ref, rhs_ref, place_ref, wide_ref, keep_ref, keep)
        return near, far, w

    def step(g, _):
        prev = None
        for n in range(8):
            cur = one(8 * g + n)
            if prev is not None:
                tile_sums(prev[2], prev[0], prev[1], feat_ref, add)
            prev = cur
        tile_sums(prev[2], prev[0], prev[1], feat_ref, add)
        return 0

    lax.fori_loop(0, (count_ref[0, 0] + 7) // 8, step, 0)

    def load(slot, row):
        return acc_ref[pl.ds(8 * slot + row, ROWS, stride=8 * ACC_GROUPS), :]

    force, torque = finish_sums(load, pool_features([pool_ref[c] for c in range(13)]))
    for c, rows in enumerate(force + torque):
        own_out[c] = rows[0:8]
        for k in range(3):
            halo_out[k, 4 * c : 4 * c + 4, :] = rows[8 + 4 * k : 12 + 4 * k]


def returned_rows(back_ref, comps):
    return [[back_ref[k, 4 * c + j : 4 * c + j + 1, :] for k in range(3) for j in range(4)] for c in range(comps)]


def frame_body(
    sizes, own_ref, halo_ref, coords_ref, import_ref, face_ref, frame_ref, out_ref,
    back_ref, spread_ref, last_ref, send_sem, recv_sem,
):
    up, down = neighbours(sizes)
    greet(down)
    pl.semaphore_wait(pltpu.get_barrier_semaphore(), 3)
    copies = send_sets(halo_ref, back_ref, send_sem.at[0], recv_sem.at[0], up)

    blocks, lanes = face_masks([face_ref[k, j : j + 1, :] for k in range(3) for j in range(4)])
    index = [frame_ref[8 * m : 8 * m + 8, :] for m in range(3)]
    low = [i & 127 for i in index]
    high = [i >> 7 for i in index]
    spots = [[jnp.zeros((8, 128), F32) for _ in range(3)] for _ in range(3)]
    for b in range(POOL_BLOCKS):
        rows = []
        for c in range(3):
            if b < OWN_BLOCKS:
                rows.append(coords_ref[8 * c + b : 8 * c + b + 1, :])
            else:
                k, j = divmod(b - OWN_BLOCKS, 4)
                rows.append(import_ref[k, 4 * c + j : 4 * c + j + 1, :])
        for m in range(3):
            hit = high[m] == b
            for c in range(3):
                spots[m][c] = jnp.where(hit, lane_gather(rows[c], low[m]), spots[m][c])
    place = [coords_ref[8 * c : 8 * c + 8, :] for c in range(3)]
    levers, scales = [], []
    for m in range(3):
        lever = [spots[m][c] - place[c] for c in range(3)]
        levers.append(lever)
        scales.append(1.0 / (3.0 * (dot3(lever, lever) + LEVER_SOFT)))
    sub24 = lax.broadcasted_iota(jnp.int32, (ROWS, 128), 0)
    sub128 = lax.broadcasted_iota(jnp.int32, (128, 128), 0)
    hits, hot = [], []
    for m in range(3):
        for b in range(OWN_BLOCKS):
            hits.append(jnp.broadcast_to(high[m][b : b + 1], (ROWS, 128)) == sub24)
            lane = jnp.broadcast_to(low[m][b : b + 1], (128, 128)) == sub128
            hot.append(jnp.where(lane, 1.0, 0.0).astype(BF16))

    for copy in copies:
        copy.wait()
    added = scatter_faces(returned_rows(back_ref, 6), blocks, lanes)
    owned = [own_ref[c] + added[c] for c in range(6)]
    torque = owned[3:6]
    kept = [jnp.zeros((8, 128), F32) for _ in range(3)]
    columns = []
    for m in range(3):
        push = [w * scales[m] for w in cross3(torque, levers[m])]
        kept = [kept[c] + push[c] for c in range(3)]
        halves = [split2(w) for w in push]
        for b in range(OWN_BLOCKS):
            hit = hits[8 * m + b]
            parts = []
            for c in range(3):
                for half in halves[c]:
                    parts.append(jnp.where(hit, jnp.broadcast_to(half[b : b + 1], (ROWS, 128)), 0.0))
            columns.append(jnp.concatenate(parts, axis=0).astype(BF16))
    out = nt_dot(jnp.concatenate(columns, axis=1), jnp.concatenate(hot, axis=1))
    forces = []
    for c in range(3):
        rows = out[48 * c : 48 * c + 24] + out[48 * c + 24 : 48 * c + 48]
        forces.append(owned[c] + rows[0:8] - kept[c])
        for k in range(3):
            spread_ref[k, 4 * c : 4 * c + 4, :] = rows[8 + 4 * k : 12 + 4 * k]
    spread_ref[:, 12:16, :] = jnp.zeros((3, 4, 128), F32)
    for copy in send_sets(spread_ref, last_ref, send_sem.at[1], recv_sem.at[1], up):
        copy.wait()
    added = scatter_faces(returned_rows(last_ref, 3), blocks, lanes)
    for c in range(3):
        out_ref[8 * c : 8 * c + 8, :] = forces[c] + added[c]


def vmem(count):
    return [pl.BlockSpec(memory_space=pltpu.VMEM)] * count


def shape(*dims):
    return jax.ShapeDtypeStruct(dims, F32)


def import_halo(sizes, coords, multipoles, face_atoms):
    return pl.pallas_call(
        functools.partial(import_body, sizes),
        out_shape=shape(3, 56, 128),
        in_specs=vmem(3),
        out_specs=pl.BlockSpec(memory_space=pltpu.VMEM),
        scratch_shapes=[
            pltpu.VMEM((3, 56, 128), F32),
            pltpu.SemaphoreType.DMA((3,)),
            pltpu.SemaphoreType.DMA((3,)),
        ],
        compiler_params=pltpu.CompilerParams(collective_id=0, has_side_effects=True),
    )(coords, multipoles, face_atoms)


def pair_tiles(coords, multipoles, imports, tile_pairs, tile_count):
    return pl.pallas_call(
        tiles_body,
        out_shape=(shape(6, 8, 128), shape(3, 24, 128)),
        in_specs=vmem(3) + [pl.BlockSpec(memory_space=pltpu.SMEM)] * 2,
        out_specs=vmem(2),
        scratch_shapes=[
            pltpu.VMEM((13, ROWS, 128), F32),
            pltpu.VMEM((64 * ROWS, 128), F32),
            pltpu.VMEM((88 * 8, 128), F32),
            pltpu.VMEM((184 * ROWS, 128), F32),
            pltpu.VMEM((POOL_BLOCKS, 128, 128), BF16),
            pltpu.VMEM((OWN_BLOCKS, 128, 384), BF16),
            pltpu.VMEM((POOL_BLOCKS, 128, 896), BF16),
            pltpu.VMEM((POOL_BLOCKS, 8, 128), F32),
            pltpu.VMEM((OWN_BLOCKS, 3, 128, 128), F32),
            pltpu.VMEM((3, 128, 128), F32),
            pltpu.VMEM((ROWS * 8 * ACC_GROUPS, 128), F32),
        ],
        compiler_params=pltpu.CompilerParams(vmem_limit_bytes=48 << 20),
    )(coords, multipoles, imports, tile_pairs, tile_count)


def frame_forces(sizes, owned, halo, coords, imports, face_atoms, frame_atoms):
    return pl.pallas_call(
        functools.partial(frame_body, sizes),
        out_shape=shape(24, 128),
        in_specs=vmem(6),
        out_specs=pl.BlockSpec(memory_space=pltpu.VMEM),
        scratch_shapes=[
            pltpu.VMEM((3, 24, 128), F32),
            pltpu.VMEM((3, 16, 128), F32),
            pltpu.VMEM((3, 16, 128), F32),
            pltpu.SemaphoreType.DMA((2, 3)),
            pltpu.SemaphoreType.DMA((2, 3)),
        ],
        compiler_params=pltpu.CompilerParams(collective_id=1, has_side_effects=True),
    )(owned, halo, coords, imports, face_atoms, frame_atoms)


def solution(mesh):
    sizes = (mesh.shape["gx"], mesh.shape["gy"])

    def shards(coords, multipoles, face_atoms, tile_pairs, tile_count, frame_atoms, send_list, send_count):
        coords = coords.reshape(24, 128)
        multipoles = multipoles.reshape(80, 128)
        face_atoms = face_atoms.reshape(3, 4, 128)
        frame_atoms = frame_atoms.reshape(24, 128)
        imports = import_halo(sizes, coords, multipoles, face_atoms)
        owned, halo = pair_tiles(coords, multipoles, imports, tile_pairs, tile_count)
        forces = frame_forces(sizes, owned, halo, coords, imports, face_atoms, frame_atoms)
        return forces.reshape(1, 1, 3, 1024)

    four = P("gx", "gy", None, None)
    placed = (four, four, four, four, P("gx", "gy"), four, four, P("gx", "gy", None))
    return jax.shard_map(shards, mesh=mesh, in_specs=placed, out_specs=four, check_vma=False)
```

```python
import functools

import jax
import jax.numpy as jnp
from jax import lax
from jax.experimental import pallas as pl
from jax.experimental.pallas import tpu as pltpu
from jax.sharding import PartitionSpec as P

SOFTENING = 0.5
LEVER_SOFT = 0.04
OWN_BLOCKS = 8
POOL_BLOCKS = 20
ROWS = 24
ENTRIES = ((0, 0), (1, 1), (2, 2), (0, 1), (0, 2), (1, 2))
ENTRY_AT = {(0, 0): 0, (1, 1): 1, (2, 2): 2, (0, 1): 3, (1, 0): 3, (0, 2): 4, (2, 0): 4, (1, 2): 5, (2, 1): 5}
MULT = (1.0, 1.0, 1.0, 2.0, 2.0, 2.0)
F32 = jnp.float32
BF16 = jnp.bfloat16
ACC_GROUPS = 18
EVENTS = 64
TILE_STEP = 8
MESH = pl.DeviceIdType.MESH


def cross3(a, b):
    return (a[1] * b[2] - a[2] * b[1], a[2] * b[0] - a[0] * b[2], a[0] * b[1] - a[1] * b[0])


def dot3(a, b):
    return a[0] * b[0] + a[1] * b[1] + a[2] * b[2]


def mat_vec(m, v):
    return [sum_list([m[ENTRY_AT[(r, c)]] * v[c] for c in range(3)]) for r in range(3)]


def sum_list(items):
    total = items[0]
    for item in items[1:]:
        total = total + item
    return total


def sym_outer(a, b):
    out = []
    for r, c in ENTRIES:
        if r == c:
            out.append(a[r] * b[r])
        else:
            out.append(0.5 * (a[r] * b[c] + a[c] * b[r]))
    return out


def split2(value):
    hi = value.astype(BF16).astype(F32)
    lo = (value - hi).astype(BF16).astype(F32)
    return hi, lo


def nt_dot(a, b):
    return lax.dot_general(a, b, (((1,), (1,)), ((), ())), preferred_element_type=F32)


def mm(a, b):
    return lax.dot_general(a, b, (((1,), (0,)), ((), ())), preferred_element_type=F32)


def lane_gather(row, index):
    table = jnp.broadcast_to(row, (8, 128))
    return jnp.take_along_axis(table, index, axis=1)


def face_masks(face_rows):
    sub8 = lax.broadcasted_iota(jnp.int32, (8, 128), 0)
    sub128 = lax.broadcasted_iota(jnp.int32, (128, 128), 0)
    blocks, lanes = [], []
    for row in face_rows:
        blocks.append(jnp.broadcast_to(row >> 7, (8, 128)) == sub8)
        hit = jnp.broadcast_to(row & 127, (128, 128)) == sub128
        lanes.append(jnp.where(hit, 1.0, 0.0).astype(BF16))
    return blocks, lanes


def scatter_faces(values, blocks, lanes):
    comps = len(values)
    columns = []
    for j in range(len(blocks)):
        parts = []
        for c in range(comps):
            hi, lo = split2(values[c][j])
            parts.append(jnp.where(blocks[j], jnp.broadcast_to(hi, (8, 128)), 0.0))
            parts.append(jnp.where(blocks[j], jnp.broadcast_to(lo, (8, 128)), 0.0))
        columns.append(jnp.concatenate(parts, axis=0).astype(BF16))
    lhs = jnp.concatenate(columns, axis=1)
    rhs = jnp.concatenate(lanes, axis=1)
    out = nt_dot(lhs, rhs)
    return [out[16 * c : 16 * c + 8] + out[16 * c + 8 : 16 * c + 16] for c in range(comps)]


def neighbours(sizes):
    gx, gy = lax.axis_index("gx"), lax.axis_index("gy")
    nx, ny = sizes
    up = (lax.rem(gx + 1, nx), lax.rem(gy + 1, ny))
    down = (lax.rem(gx + nx - 1, nx), lax.rem(gy + ny - 1, ny))
    return [[(to[0], gy), (gx, to[1]), (to[0], to[1])] for to in (up, down)]


def greet(senders):
    for peer in senders:
        pl.semaphore_signal(pltpu.get_barrier_semaphore(), inc=1, device_id=peer, device_id_type=MESH)


def send_sets(send_ref, recv_ref, send_sem, recv_sem, targets):
    copies = []
    for k, peer in enumerate(targets):
        copy = pltpu.make_async_remote_copy(
            src_ref=send_ref.at[k],
            dst_ref=recv_ref.at[k],
            send_sem=send_sem.at[k],
            recv_sem=recv_sem.at[k],
            device_id=peer,
            device_id_type=MESH,
        )
        copy.start()
        copies.append(copy)
    return copies


def pool_features(pool):
    x = [pool[0] - 1.0, pool[1] - 1.0, pool[2] - 0.5]
    q = pool[3]
    d = [pool[4], pool[5], pool[6]]
    quad = [pool[7], pool[8], pool[9], pool[10], pool[11], pool[12]]
    one = jnp.ones_like(q)
    xx = [x[r] * x[c] for r, c in ENTRIES]
    qx = [q * x[r] for r in range(3)]
    m = [qx[r] + d[r] for r in range(3)]
    turned = mat_vec(quad, x)
    dx = dot3(d, x)
    xqx = dot3(x, turned)
    sdx = sym_outer(d, x)
    h = [q * xx[e] + 2.0 * sdx[e] for e in range(6)]
    tx = sym_outer(turned, x)
    outer = [[quad[e] * x[c] for c in range(3)] for e in range(6)]
    return dict(one=one, x=x, q=q, d=d, quad=quad, xx=xx, qx=qx, m=m, turned=turned, dx=dx, xqx=xqx, h=h, tx=tx, outer=outer)


def sum_rows(f):
    zero = jnp.zeros_like(f["one"])
    rows = [f["one"], *f["x"], f["q"], *f["d"]]
    rows += [*f["qx"], *f["m"], zero, zero]
    rows += [*f["quad"], *f["turned"], *f["h"], zero]
    rows += [*f["tx"]] + [f["outer"][e][c] for e in range(6) for c in range(3)]
    rows += [*f["xx"], zero, zero]
    return rows


def near_rows(f):
    zero = jnp.zeros_like(f["one"])
    first = [*f["d"], f["dx"], *f["quad"], *f["turned"], f["xqx"], f["one"], *f["x"], *f["xx"]]
    second = [*f["d"], f["dx"], f["q"], *f["qx"], *f["quad"], *f["turned"], f["xqx"], *f["h"]]
    third = [*f["quad"], *f["turned"], *f["tx"]] + [f["outer"][e][c] for e in range(6) for c in range(3)]
    return first + second + third + [zero] * 7


def far_rows(f):
    zero = jnp.zeros_like(f["one"])
    one = f["one"]
    x, d, q, xx = f["x"], f["d"], f["q"], f["xx"]
    quad, turned = f["quad"], f["turned"]
    z = lambda n: [zero] * n
    u = [3.0 * x[r] for r in range(3)] + [-3.0 * one] + z(20)
    v = z(14) + [3.0 * f["dx"]] + [-3.0 * d[r] for r in range(3)] + z(6)
    p = z(4) + [15.0 * MULT[e] * xx[e] for e in range(6)] + [-30.0 * x[r] for r in range(3)] + [15.0 * one] + z(10)
    r_ = (
        z(14)
        + [15.0 * f["xqx"]]
        + [-30.0 * turned[r] for r in range(3)]
        + [15.0 * MULT[e] * quad[e] for e in range(6)]
    )
    l1 = [1.8 * f["m"][r] for r in range(3)] + [-1.8 * q, -1.8 * f["dx"]] + [1.8 * d[r] for r in range(3)]
    l1 += z(16)
    l2 = (
        [-18.0 * turned[r] for r in range(3)]
        + z(1)
        + [9.0 * f["xqx"]]
        + [-18.0 * turned[r] for r in range(3)]
        + [9.0 * MULT[e] * (f["h"][e] + 2.0 * quad[e]) for e in range(6)]
        + [-18.0 * f["m"][r] for r in range(3)]
        + [9.0 * q]
        + [9.0 * MULT[e] * quad[e] for e in range(6)]
    )
    l3 = [-252.0 * MULT[e] * f["tx"][e] for e in range(6)] + [252.0 * turned[r] for r in range(3)]
    l3 += [-252.0 * MULT[e] * quad[e] for e in range(6)]
    for a, b in ENTRIES:
        for c in range(3):
            term = quad[ENTRY_AT[(a, c)]] * x[b]
            if a != b:
                term = term + quad[ENTRY_AT[(b, c)]] * x[a]
            l3.append(252.0 * term)
    l3 += z(7)
    return [u, v, p, r_, l1, l2, l3]


def far_block(b, sum_scr, far_scr, feat_ref, rhs_ref, place_ref):
    sums = sum_scr[pl.ds(b, 64, stride=ROWS), :]
    place_ref[b] = sums[0:8]
    hi, lo = split2(sums)
    parts = []
    for g in range(8):
        parts += [hi[8 * g : 8 * g + 8], lo[8 * g : 8 * g + 8]]
    feat_ref[b] = jnp.concatenate(parts, axis=0).astype(BF16)
    start = 0
    for out_id, count in enumerate((24, 24, 24, 24, 24, 24, 40)):
        rows = far_scr[pl.ds(b + start * ROWS, count, stride=ROWS), :]
        start += count
        hi, lo = split2(rows)
        pad = [jnp.zeros((128 - 3 * count, 128), F32)]
        stacked = jnp.concatenate([hi, lo, hi] + pad, axis=0).astype(BF16)
        rhs_ref[b, :, out_id * 128 : (out_id + 1) * 128] = stacked


def near_block(b, near_scr, lhs_ref, place_ref, wide_ref):
    start = 0
    for group, count in enumerate((24, 24, 40)):
        rows = near_scr[pl.ds(b + start * 8, count, stride=8), :]
        start += count
        hi, lo = split2(rows)
        stacked = jnp.concatenate([hi, hi, lo, jnp.zeros((128 - 3 * count, 128), F32)], axis=0)
        lhs_ref[b, :, group * 128 : (group + 1) * 128] = stacked.T.astype(BF16)
    place = jnp.concatenate([place_ref[b], jnp.zeros((120, 128), F32)], axis=0).T
    for r in range(3):
        wide_ref[b, r] = jnp.broadcast_to(place[:, r + 1 : r + 2], (128, 128))


def store_rows(pool, low, high, sum_scr, far_scr):
    f = pool_features([pool[c][low:high] for c in range(13)])
    for n, row in enumerate(sum_rows(f)):
        sum_scr[n * ROWS + low : n * ROWS + high, :] = row
    at = 0
    for group in far_rows(f):
        for row in group:
            far_scr[at * ROWS + low : at * ROWS + high, :] = row
            at += 1
    return f


def tile_work(near, far, feat_ref, lhs_ref, rhs_ref, place_ref, wide_ref, keep_ref, keep):
    first = mm(lhs_ref[near, :, 0:128], rhs_ref[far, :, 0:512])
    second = mm(lhs_ref[near, :, 128:256], rhs_ref[far, :, 512:768])
    third = mm(lhs_ref[near, :, 256:384], rhs_ref[far, :, 768:896])
    chunk = 32
    names = ("b1", "b2", "b3", "al", "be", "ga", "de", "e1")
    pieces = {name: ([], []) for name in names}
    place = [jnp.broadcast_to(place_ref[far, r + 1 : r + 2, :], (chunk, 128)) for r in range(3)]
    for row in range(0, 128, chunk):
        rows = slice(row, row + chunk)
        diff = [place[r] - wide_ref[near, r, rows, :] for r in range(3)]
        dist = diff[0] * diff[0] + (diff[1] * diff[1] + (diff[2] * diff[2] + SOFTENING))
        root = lax.rsqrt(dist)
        t = root * root
        b0 = root * keep_ref[keep, rows, :]
        b1 = b0 * t
        b2 = b1 * t
        b3 = b2 * t
        u, v = first[rows, 0:128], first[rows, 128:256]
        pt, rt = first[rows, 256:384] * t, first[rows, 384:512] * t
        l1, l2, l3 = second[rows, 0:128], second[rows, 128:256], third[rows, :]
        gr, gp = 1.4 * rt - v, 1.4 * pt + u
        al = b2 * (rt - v)
        be = b2 * (pt + u)
        ga = b3 * gr
        de = b3 * gp
        e1 = b2 * (l1 + t * (l2 + gr * gp + 0.56 * (rt * pt) + t * l3))
        for name, value in zip(names, (b1, b2, b3, al, be, ga, de, e1)):
            hi = value.astype(BF16)
            pieces[name][0].append(hi)
            pieces[name][1].append((value - hi.astype(F32)).astype(BF16))
    return {name: (jnp.concatenate(h, axis=0), jnp.concatenate(l, axis=0)) for name, (h, l) in pieces.items()}


def tile_sums(w, near, far, feat_ref, add):
    near_pairs = (
        ("al", "be", 16, ((0, 0),), ((1, 0),)),
        ("e1", "b1", 32, ((2, 0),), ((3, 0), (4, 1))),
        ("b2", "de", 64, ((5, 0), (6, 1), (7, 2), (8, 3)), ((9, 2), (10, 3))),
        ("ga", "b3", 128, ((11, 0), (12, 7)), ((13, 2), (14, 3), (15, 4), (16, 5), (17, 6))),
    )
    far_pairs = (
        ("be", "al", 16, ((0, 0),), ((1, 0),)),
        ("e1", "b1", 32, ((2, 0),), ((3, 0), (4, 1))),
        ("b2", "ga", 64, ((5, 0), (6, 1), (7, 2), (8, 3)), ((9, 2), (10, 3))),
        ("de", "b3", 128, ((11, 0), (12, 7)), ((13, 2), (14, 3), (15, 4), (16, 5), (17, 6))),
    )
    for pairs, source, side, transposed in ((near_pairs, far, 0, True), (far_pairs, near, 1, False)):
        for one, two, rows, slots_one, slots_two in pairs:
            feats = feat_ref[source, 0:rows, :]
            lhs = jnp.concatenate([feats, feats], axis=1)
            if transposed:
                rhs = jnp.concatenate(
                    [jnp.concatenate([w[one][s].T, w[two][s].T], axis=1) for s in range(2)], axis=0
                )
                out = mm(lhs, rhs)
            else:
                rhs = jnp.concatenate(
                    [jnp.concatenate([w[one][s], w[two][s]], axis=1) for s in range(2)], axis=0
                )
                out = mm(lhs, rhs)
            for half, slots in enumerate((slots_one, slots_two)):
                lanes = slice(128 * half, 128 * half + 128)
                for slot, group in slots:
                    at = 16 * group
                    add(side, slot, out[at : at + 8, lanes] + out[at + 8 : at + 16, lanes])


def finish_sums(load, f):
    x, q, d, quad = f["x"], f["q"], f["d"], f["quad"]
    turned = f["turned"]
    a_one, a_x = load(0, 0), [load(0, 1 + r) for r in range(3)]
    ap_d = [load(1, 5 + r) for r in range(3)]
    e_one, e_x = load(2, 0), [load(2, 1 + r) for r in range(3)]
    b1_q, b1_d = load(3, 4), [load(3, 5 + r) for r in range(3)]
    b1_qx = [load(4, r) for r in range(3)]
    b2_q, b2_m = load(5, 4), [load(6, 3 + r) for r in range(3)]

    def wide(slot):
        flat = lambda n: load(slot + n // 8, n % 8)
        return [flat(e) for e in range(6)], [flat(6 + r) for r in range(3)]

    b2_quad, b2_t = wide(7)
    b2_h = [load(7 + (9 + e) // 8, (9 + e) % 8) for e in range(6)]
    cp_quad, cp_t = wide(9)
    c_one, c_x = load(11, 0), [load(11, 1 + r) for r in range(3)]
    c_xx = [load(12, e) for e in range(6)]
    b3_quad, b3_t = wide(13)
    b3_tx = [load(15, e) for e in range(6)]
    b3_outer = [[load(15 + (6 + 3 * e + c) // 8, (6 + 3 * e + c) % 8) for c in range(3)] for e in range(6)]

    b2_quad_x = mat_vec(b2_quad, x)
    b3_quad_x = mat_vec(b3_quad, x)
    cp_quad_x = mat_vec(cp_quad, x)
    b2_turn = [b2_t[r] - b2_quad_x[r] for r in range(3)]
    b3_turn = [b3_t[r] - b3_quad_x[r] for r in range(3)]
    cp_turn = [cp_t[r] - cp_quad_x[r] for r in range(3)]
    b1_r = [b1_qx[r] - x[r] * b1_q for r in range(3)]
    a_r = [a_x[r] - x[r] * a_one for r in range(3)]
    e_r = [e_x[r] - x[r] * e_one for r in range(3)]
    c_r = [c_x[r] - x[r] * c_one for r in range(3)]
    b2_r = [b2_m[r] - x[r] * b2_q for r in range(3)]

    slope_d = [a_r[r] + b1_r[r] + b1_d[r] - 6.0 * b2_turn[r] for r in range(3)]

    sx_c = sym_outer(c_x, x)
    sx_m = sym_outer(b2_m, x)
    sx_t = sym_outer(b3_t, x)
    sx_q = sym_outer(b3_quad_x, x)
    mixed = [
        [sum_list([b3_outer[ENTRY_AT[(a, c)]][b] * x[c] for c in range(3)]) for b in range(3)] for a in range(3)
    ]
    slope_q = []
    for e, (a, b) in enumerate(ENTRIES):
        ym = mixed[a][b] if a == b else 0.5 * (mixed[a][b] + mixed[b][a])
        slope_q.append(
            5.0 * (c_xx[e] - 2.0 * sx_c[e] + c_one * f["xx"][e])
            + 3.0 * (b2_h[e] - 2.0 * sx_m[e] + b2_q * f["xx"][e])
            + 6.0 * b2_quad[e]
            - 60.0 * (b3_tx[e] - sx_t[e] - ym + sx_q[e])
        )

    inner = [10.0 * c_r[r] + 6.0 * b2_r[r] - 60.0 * b3_turn[r] for r in range(3)]
    inner = mat_vec(quad, inner)
    b2_quad_d = mat_vec(b2_quad, d)
    b3_quad_t = mat_vec(b3_quad, turned)
    force = []
    for a in range(3):
        spun = sum_list(
            [
                b3_outer[ENTRY_AT[(a, b)]][c] * quad[ENTRY_AT[(b, c)]]
                for b in range(3)
                for c in range(3)
            ]
        )
        force.append(
            -q * (b1_r[a] + b1_d[a])
            - (5.0 / 3.0) * e_r[a]
            + d[a] * (a_one + b1_q)
            - ap_d[a]
            + inner[a]
            + 10.0 * cp_turn[a]
            + 6.0 * q * b2_turn[a]
            - 6.0 * b2_quad_d[a]
            - 60.0 * (spun - b3_quad_t[a])
        )

    full = lambda m, r, c: m[ENTRY_AT[(r, c)]]

    def commutator(r, c):
        return sum_list(
            [full(quad, r, k) * full(slope_q, k, c) - full(slope_q, r, k) * full(quad, k, c) for k in range(3)]
        )

    twist = cross3(d, slope_d)
    torque = [
        2.0 * commutator(2, 1) - twist[0],
        2.0 * commutator(0, 2) - twist[1],
        2.0 * commutator(1, 0) - twist[2],
    ]
    return force, torque


def gather_exports(coords_ref, mult_ref, face_ref, send_ref):
    face = jnp.concatenate([face_ref[k] for k in range(3)] + [jnp.zeros((4, 128), jnp.int32)], axis=0)
    shift = lax.broadcasted_iota(jnp.int32, (16, 128), 0)
    shift_x = jnp.where((shift < 4) | (shift >= 8), 1.0, 0.0).astype(F32)
    shift_y = jnp.where(shift >= 4, 1.0, 0.0).astype(F32)
    halves = [face[0:8], face[8:16]]
    lows = [h & 127 for h in halves]
    highs = [h >> 7 for h in halves]
    for c in range(13):
        src, at = (coords_ref, 8 * c) if c < 3 else (mult_ref, 8 * (c - 3))
        got = []
        for part in range(2):
            total = jnp.zeros((8, 128), F32)
            for b in range(OWN_BLOCKS):
                picked = lane_gather(src[at + b : at + b + 1, :], lows[part])
                total = jnp.where(highs[part] == b, picked, total)
            got.append(total)
        rows = jnp.concatenate(got, axis=0)
        if c == 0:
            rows = rows + shift_x
        if c == 1:
            rows = rows + shift_y
        for k in range(3):
            send_ref[k, 4 * c : 4 * c + 4, :] = rows[4 * k : 4 * k + 4]
    for k in range(3):
        send_ref[k, 52:56, :] = jnp.zeros((4, 128), F32)


def event_tables(pairs_ref, table_ref):
    lane = lax.broadcasted_iota(jnp.int32, (8, 128), 1)
    blocks = [pairs_ref[0, 0, e % 2, e // 2] for e in range(EVENTS)]
    row = jnp.zeros((8, 128), jnp.int32)
    for e, block in enumerate(blocks):
        row = jnp.where(lane == e, block, row)
    before = jnp.full((8, 128), EVENTS, jnp.int32)
    last = jnp.full((8, 128), EVENTS, jnp.int32)
    for e, block in enumerate(blocks):
        before = jnp.where((row == block) & (lane > e), e, before)
        last = jnp.where(lane == block, e, last)
    sub = lax.broadcasted_iota(jnp.int32, (8, 128), 0)
    table_ref[...] = jnp.where(sub == 0, before, last)


def returned_rows(back_ref, comps):
    return [[back_ref[k, 4 * c + j : 4 * c + j + 1, :] for k in range(3) for j in range(4)] for c in range(comps)]


def kernel_body(
    sizes, coords_hbm, mult_hbm, face_hbm, frame_hbm, pairs_hbm, count_hbm, out_ref,
    coords_ref, mult_ref, face_ref, frame_ref, pairs_ref, count_ref, load_sem, send_ref, import_ref, halo_ref, back_ref, spread_ref, last_ref, table_ref, smem_ref,
    pool_ref, sum_scr, near_scr, far_scr, feat_ref, lhs_ref, rhs_ref, place_ref, wide_ref, keep_ref, runs_ref, acc_ref,
    send_sem, recv_sem, back_send, back_recv, last_send, last_recv, local_sem,
):
    up, down = neighbours(sizes)
    greet(up)
    loads = [
        pltpu.make_async_copy(source, target, load_sem.at[n])
        for n, (source, target) in enumerate(
            (
                (coords_hbm, coords_ref),
                (mult_hbm, mult_ref),
                (face_hbm, face_ref),
                (frame_hbm, frame_ref),
                (pairs_hbm, pairs_ref),
                (count_hbm, count_ref),
            )
        )
    ]
    for copy in loads:
        copy.start()
    for copy in loads:
        copy.wait()
    gather_exports(coords_ref, mult_ref, face_ref, send_ref)
    pl.semaphore_wait(pltpu.get_barrier_semaphore(), 3)
    copies = send_sets(send_ref, import_ref, send_sem, recv_sem, down)

    event_tables(pairs_ref, table_ref)
    table_copy = pltpu.make_async_copy(table_ref, smem_ref, local_sem)
    table_copy.start()
    own = [coords_ref[8 * c : 8 * c + 8, :] for c in range(3)] + [mult_ref[8 * c : 8 * c + 8, :] for c in range(10)]
    for c in range(13):
        pool_ref[c, 0:8, :] = own[c]
        pool_ref[c, 20:24, :] = jnp.zeros((4, 128), F32)
    f = store_rows(own, 0, 8, sum_scr, far_scr)
    for n, row in enumerate(near_rows(f)):
        near_scr[n * 8 : n * 8 + 8, :] = row
    above = lax.broadcasted_iota(jnp.int32, (128, 128), 0) < lax.broadcasted_iota(jnp.int32, (128, 128), 1)
    keep_ref[0] = jnp.ones((128, 128), F32)
    keep_ref[1] = jnp.where(above, 1.0, 0.0).astype(F32)
    keep_ref[2] = jnp.zeros((128, 128), F32)
    runs_ref[EVENTS] = jnp.zeros((ACC_GROUPS, 8, 128), F32)
    for b in range(POOL_BLOCKS, ROWS):
        acc_ref[b * 8 * ACC_GROUPS : (b + 1) * 8 * ACC_GROUPS, :] = jnp.zeros((8 * ACC_GROUPS, 128), F32)

    def own_block(b, _):
        far_block(b, sum_scr, far_scr, feat_ref, rhs_ref, place_ref)
        near_block(b, near_scr, lhs_ref, place_ref, wide_ref)
        return 0

    lax.fori_loop(0, OWN_BLOCKS, own_block, 0, unroll=4)
    table_copy.wait()

    for copy in copies:
        copy.wait()
    for c in range(13):
        for k in range(3):
            pool_ref[c, 8 + 4 * k : 12 + 4 * k, :] = import_ref[k, 4 * c : 4 * c + 4, :]
    store_rows([pool_ref[c] for c in range(13)], 8, 24, sum_scr, far_scr)

    def import_block(b, _):
        far_block(b + OWN_BLOCKS, sum_scr, far_scr, feat_ref, rhs_ref, place_ref)
        return 0

    lax.fori_loop(0, POOL_BLOCKS - OWN_BLOCKS, import_block, 0, unroll=4)

    def one(t):
        near, far = pairs_ref[0, 0, 0, t], pairs_ref[0, 0, 1, t]
        keep = jnp.where(t < count_ref[0, 0], jnp.where(near == far, 1, 0), 2)
        return t, near, far, tile_work(near, far, feat_ref, lhs_ref, rhs_ref, place_ref, wide_ref, keep_ref, keep)

    def sums(t, near, far, w):
        before = [smem_ref[0, 2 * t + side] for side in range(2)]

        def add(side, slot, value):
            runs_ref[2 * t + side, slot] = runs_ref[before[side], slot] + value

        tile_sums(w, near, far, feat_ref, add)

    def step(g, _):
        held = None
        for n in range(TILE_STEP):
            current = one(TILE_STEP * g + n)
            if held is not None:
                sums(*held)
            held = current
        sums(*held)
        return 0

    lax.fori_loop(0, EVENTS // 2 // TILE_STEP, step, 0)

    for b in range(POOL_BLOCKS):
        at = smem_ref[1, b]
        for slot in range(ACC_GROUPS):
            row = (b * ACC_GROUPS + slot) * 8
            acc_ref[row : row + 8, :] = runs_ref[at, slot]

    def load(slot, row):
        return acc_ref[pl.ds(8 * slot + row, ROWS, stride=8 * ACC_GROUPS), :]

    force, torque = finish_sums(load, pool_features([pool_ref[c] for c in range(13)]))
    for c, rows in enumerate(force + torque):
        for k in range(3):
            halo_ref[k, 4 * c : 4 * c + 4, :] = rows[8 + 4 * k : 12 + 4 * k]
    copies = send_sets(halo_ref, back_ref, back_send, back_recv, up)

    blocks, lanes = face_masks([face_ref[k, j : j + 1, :] for k in range(3) for j in range(4)])
    index = [frame_ref[8 * m : 8 * m + 8, :] for m in range(3)]
    low = [i & 127 for i in index]
    high = [i >> 7 for i in index]
    spots = [[jnp.zeros((8, 128), F32) for _ in range(3)] for _ in range(3)]
    for b in range(POOL_BLOCKS):
        for c in range(3):
            row = pool_ref[c, b : b + 1, :]
            for m in range(3):
                spots[m][c] = jnp.where(high[m] == b, lane_gather(row, low[m]), spots[m][c])
    levers, scales = [], []
    for m in range(3):
        lever = [spots[m][c] - own[c] for c in range(3)]
        levers.append(lever)
        scales.append(1.0 / (3.0 * (dot3(lever, lever) + LEVER_SOFT)))
    sub24 = lax.broadcasted_iota(jnp.int32, (ROWS, 128), 0)
    sub128 = lax.broadcasted_iota(jnp.int32, (128, 128), 0)
    hits, hot = [], []
    for m in range(3):
        for b in range(OWN_BLOCKS):
            hits.append(jnp.broadcast_to(high[m][b : b + 1], (ROWS, 128)) == sub24)
            lane = jnp.broadcast_to(low[m][b : b + 1], (128, 128)) == sub128
            hot.append(jnp.where(lane, 1.0, 0.0).astype(BF16))

    for copy in copies:
        copy.wait()
    added = scatter_faces(returned_rows(back_ref, 6), blocks, lanes)
    owned = [rows[0:8] + more for rows, more in zip(force + torque, added)]
    torque = owned[3:6]
    kept = [jnp.zeros((8, 128), F32) for _ in range(3)]
    columns = []
    for m in range(3):
        push = [w * scales[m] for w in cross3(torque, levers[m])]
        kept = [kept[c] + push[c] for c in range(3)]
        halves = [split2(w) for w in push]
        for b in range(OWN_BLOCKS):
            hit = hits[8 * m + b]
            parts = []
            for c in range(3):
                for half in halves[c]:
                    parts.append(jnp.where(hit, jnp.broadcast_to(half[b : b + 1], (ROWS, 128)), 0.0))
            columns.append(jnp.concatenate(parts, axis=0).astype(BF16))
    out = nt_dot(jnp.concatenate(columns, axis=1), jnp.concatenate(hot, axis=1))
    forces = []
    for c in range(3):
        rows = out[48 * c : 48 * c + 24] + out[48 * c + 24 : 48 * c + 48]
        forces.append(owned[c] + rows[0:8] - kept[c])
        for k in range(3):
            spread_ref[k, 4 * c : 4 * c + 4, :] = rows[8 + 4 * k : 12 + 4 * k]
    spread_ref[:, 12:16, :] = jnp.zeros((3, 4, 128), F32)
    for copy in send_sets(spread_ref, last_ref, last_send, last_recv, up):
        copy.wait()
    added = scatter_faces(returned_rows(last_ref, 3), blocks, lanes)
    for c in range(3):
        out_ref[8 * c : 8 * c + 8, :] = forces[c] + added[c]


def domain_forces(sizes, coords, multipoles, face_atoms, frame_atoms, tile_pairs, tile_count):
    vmem = pl.BlockSpec(memory_space=pltpu.VMEM)
    hbm = pl.BlockSpec(memory_space=pltpu.HBM)
    return pl.pallas_call(
        functools.partial(kernel_body, sizes),
        out_shape=jax.ShapeDtypeStruct((24, 128), F32),
        in_specs=[hbm] * 6,
        out_specs=vmem,
        scratch_shapes=[
            pltpu.VMEM((24, 128), F32),
            pltpu.VMEM((80, 128), F32),
            pltpu.VMEM((3, 4, 128), jnp.int32),
            pltpu.VMEM((24, 128), jnp.int32),
            pltpu.SMEM((1, 1, 2, 32), jnp.int32),
            pltpu.SMEM((1, 1), jnp.int32),
            pltpu.SemaphoreType.DMA((6,)),
            pltpu.VMEM((3, 56, 128), F32),
            pltpu.VMEM((3, 56, 128), F32),
            pltpu.VMEM((3, 24, 128), F32),
            pltpu.VMEM((3, 24, 128), F32),
            pltpu.VMEM((3, 16, 128), F32),
            pltpu.VMEM((3, 16, 128), F32),
            pltpu.VMEM((8, 128), jnp.int32),
            pltpu.SMEM((8, 128), jnp.int32),
            pltpu.VMEM((13, ROWS, 128), F32),
            pltpu.VMEM((64 * ROWS, 128), F32),
            pltpu.VMEM((88 * 8, 128), F32),
            pltpu.VMEM((184 * ROWS, 128), F32),
            pltpu.VMEM((POOL_BLOCKS, 128, 128), BF16),
            pltpu.VMEM((OWN_BLOCKS, 128, 384), BF16),
            pltpu.VMEM((POOL_BLOCKS, 128, 896), BF16),
            pltpu.VMEM((POOL_BLOCKS, 8, 128), F32),
            pltpu.VMEM((OWN_BLOCKS, 3, 128, 128), F32),
            pltpu.VMEM((3, 128, 128), F32),
            pltpu.VMEM((EVENTS + 1, ACC_GROUPS, 8, 128), F32),
            pltpu.VMEM((ROWS * 8 * ACC_GROUPS, 128), F32),
        ]
        + [pltpu.SemaphoreType.DMA((3,))] * 6
        + [pltpu.SemaphoreType.DMA],
        compiler_params=pltpu.CompilerParams(collective_id=0, has_side_effects=True, vmem_limit_bytes=52 << 20),
    )(coords, multipoles, face_atoms, frame_atoms, tile_pairs, tile_count)


def solution(mesh):
    sizes = (mesh.shape["gx"], mesh.shape["gy"])

    def shards(coords, multipoles, face_atoms, tile_pairs, tile_count, frame_atoms, send_list, send_count):
        coords = coords.reshape(24, 128)
        multipoles = multipoles.reshape(80, 128)
        face_atoms = face_atoms.reshape(3, 4, 128)
        frame_atoms = frame_atoms.reshape(24, 128)
        forces = domain_forces(sizes, coords, multipoles, face_atoms, frame_atoms, tile_pairs, tile_count)
        return forces.reshape(1, 1, 3, 1024)

    four = P("gx", "gy", None, None)
    placed = (four, four, four, four, P("gx", "gy"), four, four, P("gx", "gy", None))
    return jax.shard_map(shards, mesh=mesh, in_specs=placed, out_specs=four, check_vma=False)
```

```python
import functools

import jax
import jax.numpy as jnp
from jax import lax
from jax.experimental import pallas as pl
from jax.experimental.pallas import tpu as pltpu
from jax.sharding import PartitionSpec as P

SOFTENING = 0.5
LEVER_SOFT = 0.04
OWN_BLOCKS = 8
POOL_BLOCKS = 20
ROWS = 24
ENTRIES = ((0, 0), (1, 1), (2, 2), (0, 1), (0, 2), (1, 2))
ENTRY_AT = {(0, 0): 0, (1, 1): 1, (2, 2): 2, (0, 1): 3, (1, 0): 3, (0, 2): 4, (2, 0): 4, (1, 2): 5, (2, 1): 5}
MULT = (1.0, 1.0, 1.0, 2.0, 2.0, 2.0)
F32 = jnp.float32
BF16 = jnp.bfloat16
ACC_GROUPS = 18
EVENTS = 64
TILE_STEP = 16
MESH = pl.DeviceIdType.MESH


def cross3(a, b):
    return (a[1] * b[2] - a[2] * b[1], a[2] * b[0] - a[0] * b[2], a[0] * b[1] - a[1] * b[0])


def dot3(a, b):
    return a[0] * b[0] + a[1] * b[1] + a[2] * b[2]


def mat_vec(m, v):
    return [sum_list([m[ENTRY_AT[(r, c)]] * v[c] for c in range(3)]) for r in range(3)]


def sum_list(items):
    total = items[0]
    for item in items[1:]:
        total = total + item
    return total


def sym_outer(a, b):
    out = []
    for r, c in ENTRIES:
        if r == c:
            out.append(a[r] * b[r])
        else:
            out.append(0.5 * (a[r] * b[c] + a[c] * b[r]))
    return out


def split2(value):
    hi = value.astype(BF16).astype(F32)
    lo = (value - hi).astype(BF16).astype(F32)
    return hi, lo


def nt_dot(a, b):
    return lax.dot_general(a, b, (((1,), (1,)), ((), ())), preferred_element_type=F32)


def mm(a, b):
    return lax.dot_general(a, b, (((1,), (0,)), ((), ())), preferred_element_type=F32)


def lane_gather(row, index):
    table = jnp.broadcast_to(row, (8, 128))
    return jnp.take_along_axis(table, index, axis=1)


def face_masks(face_rows):
    sub8 = lax.broadcasted_iota(jnp.int32, (8, 128), 0)
    sub128 = lax.broadcasted_iota(jnp.int32, (128, 128), 0)
    blocks, lanes = [], []
    for row in face_rows:
        blocks.append(jnp.broadcast_to(row >> 7, (8, 128)) == sub8)
        hit = jnp.broadcast_to(row & 127, (128, 128)) == sub128
        lanes.append(jnp.where(hit, 1.0, 0.0).astype(BF16))
    return blocks, lanes


def scatter_faces(values, blocks, lanes):
    comps = len(values)
    columns = []
    for j in range(len(blocks)):
        parts = []
        for c in range(comps):
            hi, lo = split2(values[c][j])
            parts.append(jnp.where(blocks[j], jnp.broadcast_to(hi, (8, 128)), 0.0))
            parts.append(jnp.where(blocks[j], jnp.broadcast_to(lo, (8, 128)), 0.0))
        columns.append(jnp.concatenate(parts, axis=0).astype(BF16))
    lhs = jnp.concatenate(columns, axis=1)
    rhs = jnp.concatenate(lanes, axis=1)
    out = nt_dot(lhs, rhs)
    return [out[16 * c : 16 * c + 8] + out[16 * c + 8 : 16 * c + 16] for c in range(comps)]


def neighbours(sizes):
    gx, gy = lax.axis_index("gx"), lax.axis_index("gy")
    nx, ny = sizes
    up = (lax.rem(gx + 1, nx), lax.rem(gy + 1, ny))
    down = (lax.rem(gx + nx - 1, nx), lax.rem(gy + ny - 1, ny))
    return [[(to[0], gy), (gx, to[1]), (to[0], to[1])] for to in (up, down)]


def greet(senders):
    for peer in senders:
        pl.semaphore_signal(pltpu.get_barrier_semaphore(), inc=1, device_id=peer, device_id_type=MESH)


def send_sets(send_ref, recv_ref, send_sem, recv_sem, targets):
    copies = []
    for k, peer in enumerate(targets):
        copy = pltpu.make_async_remote_copy(
            src_ref=send_ref.at[k],
            dst_ref=recv_ref.at[k],
            send_sem=send_sem.at[k],
            recv_sem=recv_sem.at[k],
            device_id=peer,
            device_id_type=MESH,
        )
        copy.start()
        copies.append(copy)
    return copies


def pool_features(pool):
    x = [pool[0] - 1.0, pool[1] - 1.0, pool[2] - 0.5]
    q = pool[3]
    d = [pool[4], pool[5], pool[6]]
    quad = [pool[7], pool[8], pool[9], pool[10], pool[11], pool[12]]
    one = jnp.ones_like(q)
    xx = [x[r] * x[c] for r, c in ENTRIES]
    qx = [q * x[r] for r in range(3)]
    m = [qx[r] + d[r] for r in range(3)]
    turned = mat_vec(quad, x)
    dx = dot3(d, x)
    xqx = dot3(x, turned)
    sdx = sym_outer(d, x)
    h = [q * xx[e] + 2.0 * sdx[e] for e in range(6)]
    tx = sym_outer(turned, x)
    outer = [[quad[e] * x[c] for c in range(3)] for e in range(6)]
    return dict(one=one, x=x, q=q, d=d, quad=quad, xx=xx, qx=qx, m=m, turned=turned, dx=dx, xqx=xqx, h=h, tx=tx, outer=outer)


def sum_rows(f):
    zero = jnp.zeros_like(f["one"])
    rows = [*f["xx"], zero, zero]
    rows += [f["one"], *f["x"], f["q"], *f["d"]]
    rows += [*f["qx"], *f["m"], zero, zero]
    rows += [*f["quad"], *f["turned"], *f["h"], zero]
    rows += [*f["tx"]] + [f["outer"][e][c] for e in range(6) for c in range(3)]
    return rows


def near_rows(f):
    zero = jnp.zeros_like(f["one"])
    first = [*f["d"], f["dx"], *f["quad"], *f["turned"], f["xqx"], f["one"], *f["x"], *f["xx"]]
    second = [*f["d"], f["dx"], f["q"], *f["qx"], *f["quad"], *f["turned"], f["xqx"], *f["h"]]
    third = [*f["quad"], *f["turned"], *f["tx"]] + [f["outer"][e][c] for e in range(6) for c in range(3)]
    return first + second + third + [zero] * 7


def far_rows(f):
    zero = jnp.zeros_like(f["one"])
    one = f["one"]
    x, d, q, xx = f["x"], f["d"], f["q"], f["xx"]
    quad, turned = f["quad"], f["turned"]
    z = lambda n: [zero] * n
    u = [3.0 * x[r] for r in range(3)] + [-3.0 * one] + z(20)
    v = z(14) + [3.0 * f["dx"]] + [-3.0 * d[r] for r in range(3)] + z(6)
    p = z(4) + [15.0 * MULT[e] * xx[e] for e in range(6)] + [-30.0 * x[r] for r in range(3)] + [15.0 * one] + z(10)
    r_ = (
        z(14)
        + [15.0 * f["xqx"]]
        + [-30.0 * turned[r] for r in range(3)]
        + [15.0 * MULT[e] * quad[e] for e in range(6)]
    )
    l1 = [1.8 * f["m"][r] for r in range(3)] + [-1.8 * q, -1.8 * f["dx"]] + [1.8 * d[r] for r in range(3)]
    l1 += z(16)
    l2 = (
        [-18.0 * turned[r] for r in range(3)]
        + z(1)
        + [9.0 * f["xqx"]]
        + [-18.0 * turned[r] for r in range(3)]
        + [9.0 * MULT[e] * (f["h"][e] + 2.0 * quad[e]) for e in range(6)]
        + [-18.0 * f["m"][r] for r in range(3)]
        + [9.0 * q]
        + [9.0 * MULT[e] * quad[e] for e in range(6)]
    )
    l3 = [-252.0 * MULT[e] * f["tx"][e] for e in range(6)] + [252.0 * turned[r] for r in range(3)]
    l3 += [-252.0 * MULT[e] * quad[e] for e in range(6)]
    for a, b in ENTRIES:
        for c in range(3):
            term = quad[ENTRY_AT[(a, c)]] * x[b]
            if a != b:
                term = term + quad[ENTRY_AT[(b, c)]] * x[a]
            l3.append(252.0 * term)
    l3 += z(7)
    return [u, v, p, r_, l1, l2, l3]


def far_block(b, sum_scr, far_scr, feat_ref, rhs_ref, place_ref):
    sums = sum_scr[pl.ds(b, 64, stride=ROWS), :]
    place_ref[b] = sums[8:16]
    hi, lo = split2(sums)
    parts = []
    for g in range(8):
        parts += [hi[8 * g : 8 * g + 8], lo[8 * g : 8 * g + 8]]
    feat_ref[b] = jnp.concatenate(parts, axis=0).astype(BF16)
    start = 0
    for out_id, count in enumerate((24, 24, 24, 24, 24, 24, 40)):
        rows = far_scr[pl.ds(b + start * ROWS, count, stride=ROWS), :]
        start += count
        hi, lo = split2(rows)
        pad = [jnp.zeros((128 - 3 * count, 128), F32)]
        stacked = jnp.concatenate([hi, lo, hi] + pad, axis=0).astype(BF16)
        rhs_ref[b, :, out_id * 128 : (out_id + 1) * 128] = stacked


def near_block(b, near_scr, lhs_ref, place_ref, wide_ref):
    start = 0
    for group, count in enumerate((24, 24, 40)):
        rows = near_scr[pl.ds(b + start * 8, count, stride=8), :]
        start += count
        hi, lo = split2(rows)
        stacked = jnp.concatenate([hi, hi, lo, jnp.zeros((128 - 3 * count, 128), F32)], axis=0)
        lhs_ref[b, :, group * 128 : (group + 1) * 128] = stacked.T.astype(BF16)
    place = jnp.concatenate([place_ref[b], jnp.zeros((120, 128), F32)], axis=0).T
    for r in range(3):
        wide_ref[b, r] = jnp.broadcast_to(place[:, r + 1 : r + 2], (128, 128))


def store_rows(pool, low, high, sum_scr, far_scr):
    f = pool_features([pool[c][low:high] for c in range(13)])
    for n, row in enumerate(sum_rows(f)):
        sum_scr[n * ROWS + low : n * ROWS + high, :] = row
    at = 0
    for group in far_rows(f):
        for row in group:
            far_scr[at * ROWS + low : at * ROWS + high, :] = row
            at += 1
    return f


def tile_work(near, far, feat_ref, lhs_ref, rhs_ref, place_ref, wide_ref, keep_ref, keep):
    first = mm(lhs_ref[near, :, 0:128], rhs_ref[far, :, 0:512])
    second = mm(lhs_ref[near, :, 128:256], rhs_ref[far, :, 512:768])
    third = mm(lhs_ref[near, :, 256:384], rhs_ref[far, :, 768:896])
    chunk = 32
    names = ("b1", "b2", "b3", "al", "be", "ga", "de", "e1")
    pieces = {name: ([], []) for name in names}
    place = [jnp.broadcast_to(place_ref[far, r + 1 : r + 2, :], (chunk, 128)) for r in range(3)]
    for row in range(0, 128, chunk):
        rows = slice(row, row + chunk)
        diff = [place[r] - wide_ref[near, r, rows, :] for r in range(3)]
        dist = diff[0] * diff[0] + (diff[1] * diff[1] + (diff[2] * diff[2] + SOFTENING))
        root = lax.rsqrt(dist)
        t = root * root
        b0 = root * keep_ref[keep, rows, :]
        b1 = b0 * t
        b2 = b1 * t
        b3 = b2 * t
        u, v = first[rows, 0:128], first[rows, 128:256]
        pt, rt = first[rows, 256:384] * t, first[rows, 384:512] * t
        l1, l2, l3 = second[rows, 0:128], second[rows, 128:256], third[rows, :]
        gr, gp = 1.4 * rt - v, 1.4 * pt + u
        al = b2 * (rt - v)
        be = b2 * (pt + u)
        ga = b3 * gr
        de = b3 * gp
        e1 = b2 * (l1 + t * (l2 + gr * gp + 0.56 * (rt * pt) + t * l3))
        for name, value in zip(names, (b1, b2, b3, al, be, ga, de, e1)):
            hi = value.astype(BF16)
            pieces[name][0].append(hi)
            pieces[name][1].append((value - hi.astype(F32)).astype(BF16))
    return {name: (jnp.concatenate(h, axis=0), jnp.concatenate(l, axis=0)) for name, (h, l) in pieces.items()}


def tile_sums(w, near, far, feat_ref, add):
    slots = {
        "a": ((0, 1),),
        "ap": ((1, 1),),
        "e": ((2, 1),),
        "b1": ((3, 1), (4, 2)),
        "b2": ((5, 1), (6, 2), (7, 3), (8, 4)),
        "cp": ((9, 3), (10, 4)),
        "c": ((11, 1), (12, 0)),
        "b3": ((13, 3), (14, 4), (15, 5), (16, 6), (17, 7)),
    }

    def pairs_for(a, ap, c, cp):
        return (
            (a, ap, 1, 2, slots["a"], slots["ap"]),
            ("e1", c, 0, 2, slots["e"], slots["c"]),
            ("b1", "b2", 1, 5, slots["b1"], slots["b2"]),
            (cp, "b3", 3, 8, slots["cp"], slots["b3"]),
        )

    near_pairs = pairs_for("al", "be", "ga", "de")
    far_pairs = pairs_for("be", "al", "de", "ga")
    for pairs, source, side, transposed in ((near_pairs, far, 0, True), (far_pairs, near, 1, False)):
        for one, two, first, final, slots_one, slots_two in pairs:
            feats = feat_ref[source, 16 * first : 16 * final, :]
            lhs = jnp.concatenate([feats, feats], axis=1)
            if transposed:
                rhs = jnp.concatenate(
                    [jnp.concatenate([w[one][s].T, w[two][s].T], axis=1) for s in range(2)], axis=0
                )
                out = mm(lhs, rhs)
            else:
                rhs = jnp.concatenate(
                    [jnp.concatenate([w[one][s], w[two][s]], axis=1) for s in range(2)], axis=0
                )
                out = mm(lhs, rhs)
            for half, targets in enumerate((slots_one, slots_two)):
                lanes = slice(128 * half, 128 * half + 128)
                for slot, group in targets:
                    at = 16 * (group - first)
                    add(side, slot, out[at : at + 8, lanes] + out[at + 8 : at + 16, lanes])


def finish_sums(load, f):
    x, q, d, quad = f["x"], f["q"], f["d"], f["quad"]
    turned = f["turned"]
    a_one, a_x = load(0, 0), [load(0, 1 + r) for r in range(3)]
    ap_d = [load(1, 5 + r) for r in range(3)]
    e_one, e_x = load(2, 0), [load(2, 1 + r) for r in range(3)]
    b1_q, b1_d = load(3, 4), [load(3, 5 + r) for r in range(3)]
    b1_qx = [load(4, r) for r in range(3)]
    b2_q, b2_m = load(5, 4), [load(6, 3 + r) for r in range(3)]

    def wide(slot):
        flat = lambda n: load(slot + n // 8, n % 8)
        return [flat(e) for e in range(6)], [flat(6 + r) for r in range(3)]

    b2_quad, b2_t = wide(7)
    b2_h = [load(7 + (9 + e) // 8, (9 + e) % 8) for e in range(6)]
    cp_quad, cp_t = wide(9)
    c_one, c_x = load(11, 0), [load(11, 1 + r) for r in range(3)]
    c_xx = [load(12, e) for e in range(6)]
    b3_quad, b3_t = wide(13)
    b3_tx = [load(15, e) for e in range(6)]
    b3_outer = [[load(15 + (6 + 3 * e + c) // 8, (6 + 3 * e + c) % 8) for c in range(3)] for e in range(6)]

    b2_quad_x = mat_vec(b2_quad, x)
    b3_quad_x = mat_vec(b3_quad, x)
    cp_quad_x = mat_vec(cp_quad, x)
    b2_turn = [b2_t[r] - b2_quad_x[r] for r in range(3)]
    b3_turn = [b3_t[r] - b3_quad_x[r] for r in range(3)]
    cp_turn = [cp_t[r] - cp_quad_x[r] for r in range(3)]
    b1_r = [b1_qx[r] - x[r] * b1_q for r in range(3)]
    a_r = [a_x[r] - x[r] * a_one for r in range(3)]
    e_r = [e_x[r] - x[r] * e_one for r in range(3)]
    c_r = [c_x[r] - x[r] * c_one for r in range(3)]
    b2_r = [b2_m[r] - x[r] * b2_q for r in range(3)]

    slope_d = [a_r[r] + b1_r[r] + b1_d[r] - 6.0 * b2_turn[r] for r in range(3)]

    sx_c = sym_outer(c_x, x)
    sx_m = sym_outer(b2_m, x)
    sx_t = sym_outer(b3_t, x)
    sx_q = sym_outer(b3_quad_x, x)
    mixed = [
        [sum_list([b3_outer[ENTRY_AT[(a, c)]][b] * x[c] for c in range(3)]) for b in range(3)] for a in range(3)
    ]
    slope_q = []
    for e, (a, b) in enumerate(ENTRIES):
        ym = mixed[a][b] if a == b else 0.5 * (mixed[a][b] + mixed[b][a])
        slope_q.append(
            5.0 * (c_xx[e] - 2.0 * sx_c[e] + c_one * f["xx"][e])
            + 3.0 * (b2_h[e] - 2.0 * sx_m[e] + b2_q * f["xx"][e])
            + 6.0 * b2_quad[e]
            - 60.0 * (b3_tx[e] - sx_t[e] - ym + sx_q[e])
        )

    inner = [10.0 * c_r[r] + 6.0 * b2_r[r] - 60.0 * b3_turn[r] for r in range(3)]
    inner = mat_vec(quad, inner)
    b2_quad_d = mat_vec(b2_quad, d)
    b3_quad_t = mat_vec(b3_quad, turned)
    force = []
    for a in range(3):
        spun = sum_list(
            [
                b3_outer[ENTRY_AT[(a, b)]][c] * quad[ENTRY_AT[(b, c)]]
                for b in range(3)
                for c in range(3)
            ]
        )
        force.append(
            -q * (b1_r[a] + b1_d[a])
            - (5.0 / 3.0) * e_r[a]
            + d[a] * (a_one + b1_q)
            - ap_d[a]
            + inner[a]
            + 10.0 * cp_turn[a]
            + 6.0 * q * b2_turn[a]
            - 6.0 * b2_quad_d[a]
            - 60.0 * (spun - b3_quad_t[a])
        )

    full = lambda m, r, c: m[ENTRY_AT[(r, c)]]

    def commutator(r, c):
        return sum_list(
            [full(quad, r, k) * full(slope_q, k, c) - full(slope_q, r, k) * full(quad, k, c) for k in range(3)]
        )

    twist = cross3(d, slope_d)
    torque = [
        2.0 * commutator(2, 1) - twist[0],
        2.0 * commutator(0, 2) - twist[1],
        2.0 * commutator(1, 0) - twist[2],
    ]
    return force, torque


def gather_exports(coords_ref, mult_ref, face_ref, send_ref):
    face = jnp.concatenate([face_ref[k] for k in range(3)] + [jnp.zeros((4, 128), jnp.int32)], axis=0)
    shift = lax.broadcasted_iota(jnp.int32, (16, 128), 0)
    shift_x = jnp.where((shift < 4) | (shift >= 8), 1.0, 0.0).astype(F32)
    shift_y = jnp.where(shift >= 4, 1.0, 0.0).astype(F32)
    halves = [face[0:8], face[8:16]]
    lows = [h & 127 for h in halves]
    highs = [h >> 7 for h in halves]
    for c in range(13):
        src, at = (coords_ref, 8 * c) if c < 3 else (mult_ref, 8 * (c - 3))
        got = []
        for part in range(2):
            total = jnp.zeros((8, 128), F32)
            for b in range(OWN_BLOCKS):
                picked = lane_gather(src[at + b : at + b + 1, :], lows[part])
                total = jnp.where(highs[part] == b, picked, total)
            got.append(total)
        rows = jnp.concatenate(got, axis=0)
        if c == 0:
            rows = rows + shift_x
        if c == 1:
            rows = rows + shift_y
        for k in range(3):
            send_ref[k, 4 * c : 4 * c + 4, :] = rows[4 * k : 4 * k + 4]
    for k in range(3):
        send_ref[k, 52:56, :] = jnp.zeros((4, 128), F32)


def event_tables(pairs_ref, table_ref):
    lane = lax.broadcasted_iota(jnp.int32, (8, 128), 1)
    blocks = [pairs_ref[0, 0, e % 2, e // 2] for e in range(EVENTS)]
    row = jnp.zeros((8, 128), jnp.int32)
    for e, block in enumerate(blocks):
        row = jnp.where(lane == e, block, row)
    before = jnp.full((8, 128), EVENTS, jnp.int32)
    last = jnp.full((8, 128), EVENTS, jnp.int32)
    for e, block in enumerate(blocks):
        before = jnp.where((row == block) & (lane > e), e, before)
        last = jnp.where(lane == block, e, last)
    sub = lax.broadcasted_iota(jnp.int32, (8, 128), 0)
    table_ref[...] = jnp.where(sub == 0, before, last)


def scatter_sets(back_ref, comps, sets, blocks, lanes):
    chosen = [(k, j) for k in sets for j in range(4)]
    values = [[back_ref[k, 4 * c + j : 4 * c + j + 1, :] for k, j in chosen] for c in range(comps)]
    return scatter_faces(values, [blocks[4 * k + j] for k, j in chosen], [lanes[4 * k + j] for k, j in chosen])


def kernel_body(
    sizes, coords_hbm, mult_hbm, face_hbm, frame_hbm, pairs_hbm, count_hbm, out_ref,
    coords_ref, mult_ref, face_ref, frame_ref, pairs_ref, count_ref, load_sem, send_ref, import_ref, halo_ref, back_ref, spread_ref, last_ref, table_ref, smem_ref,
    pool_ref, sum_scr, near_scr, far_scr, feat_ref, lhs_ref, rhs_ref, place_ref, wide_ref, keep_ref, runs_ref, acc_ref,
    send_sem, recv_sem, back_send, back_recv, last_send, last_recv, local_sem,
):
    up, down = neighbours(sizes)
    greet(up)
    loads = [
        pltpu.make_async_copy(source, target, load_sem.at[n])
        for n, (source, target) in enumerate(
            (
                (coords_hbm, coords_ref),
                (mult_hbm, mult_ref),
                (face_hbm, face_ref),
                (frame_hbm, frame_ref),
                (pairs_hbm, pairs_ref),
                (count_hbm, count_ref),
            )
        )
    ]
    for copy in loads:
        copy.start()
    for copy in loads:
        copy.wait()
    gather_exports(coords_ref, mult_ref, face_ref, send_ref)
    pl.semaphore_wait(pltpu.get_barrier_semaphore(), 3)
    copies = send_sets(send_ref, import_ref, send_sem, recv_sem, down)

    event_tables(pairs_ref, table_ref)
    table_copy = pltpu.make_async_copy(table_ref, smem_ref, local_sem)
    table_copy.start()
    own = [coords_ref[8 * c : 8 * c + 8, :] for c in range(3)] + [mult_ref[8 * c : 8 * c + 8, :] for c in range(10)]
    for c in range(13):
        pool_ref[c, 0:8, :] = own[c]
        pool_ref[c, 20:24, :] = jnp.zeros((4, 128), F32)
    f = store_rows(own, 0, 8, sum_scr, far_scr)
    for n, row in enumerate(near_rows(f)):
        near_scr[n * 8 : n * 8 + 8, :] = row
    above = lax.broadcasted_iota(jnp.int32, (128, 128), 0) < lax.broadcasted_iota(jnp.int32, (128, 128), 1)
    keep_ref[0] = jnp.ones((128, 128), F32)
    keep_ref[1] = jnp.where(above, 1.0, 0.0).astype(F32)
    keep_ref[2] = jnp.zeros((128, 128), F32)
    runs_ref[EVENTS] = jnp.zeros((ACC_GROUPS, 8, 128), F32)
    for b in range(POOL_BLOCKS, ROWS):
        acc_ref[b * 8 * ACC_GROUPS : (b + 1) * 8 * ACC_GROUPS, :] = jnp.zeros((8 * ACC_GROUPS, 128), F32)

    def own_block(b, _):
        far_block(b, sum_scr, far_scr, feat_ref, rhs_ref, place_ref)
        near_block(b, near_scr, lhs_ref, place_ref, wide_ref)
        return 0

    lax.fori_loop(0, OWN_BLOCKS, own_block, 0, unroll=4)
    table_copy.wait()

    def import_block(b, _):
        far_block(b, sum_scr, far_scr, feat_ref, rhs_ref, place_ref)
        return 0

    for sets, rows, blocks in (((0, 1), (8, 16), (8, 16)), ((2,), (16, 24), (16, 20))):
        for k in sets:
            copies[k].wait()
        for c in range(13):
            for k in sets:
                pool_ref[c, 8 + 4 * k : 12 + 4 * k, :] = import_ref[k, 4 * c : 4 * c + 4, :]
        store_rows([pool_ref[c] for c in range(13)], *rows, sum_scr, far_scr)
        lax.fori_loop(*blocks, import_block, 0, unroll=4)

    def one(t):
        near, far = pairs_ref[0, 0, 0, t], pairs_ref[0, 0, 1, t]
        keep = jnp.where(t < count_ref[0, 0], jnp.where(near == far, 1, 0), 2)
        return t, near, far, tile_work(near, far, feat_ref, lhs_ref, rhs_ref, place_ref, wide_ref, keep_ref, keep)

    def sums(t, near, far, w):
        before = [smem_ref[0, 2 * t + side] for side in range(2)]

        def add(side, slot, value):
            runs_ref[2 * t + side, slot] = runs_ref[before[side], slot] + value

        tile_sums(w, near, far, feat_ref, add)

    def step(g, _):
        held = None
        for n in range(TILE_STEP):
            current = one(TILE_STEP * g + n)
            if held is not None:
                sums(*held)
            held = current
        sums(*held)
        return 0

    lax.fori_loop(0, EVENTS // 2 // TILE_STEP, step, 0)

    def finish(low, high):
        for b in range(low, min(high, POOL_BLOCKS)):
            at = smem_ref[1, b]
            for slot in range(ACC_GROUPS):
                row = (b * ACC_GROUPS + slot) * 8
                acc_ref[row : row + 8, :] = runs_ref[at, slot]

        def load(slot, row):
            at = low * 8 * ACC_GROUPS + 8 * slot + row
            return acc_ref[pl.ds(at, high - low, stride=8 * ACC_GROUPS), :]

        force, torque = finish_sums(load, pool_features([pool_ref[c, low:high, :] for c in range(13)]))
        return force + torque

    for c, rows in enumerate(finish(8, 24)):
        for k in range(3):
            halo_ref[k, 4 * c : 4 * c + 4, :] = rows[4 * k : 4 * k + 4]
    copies = send_sets(halo_ref, back_ref, back_send, back_recv, up)
    partial = finish(0, 8)

    blocks, lanes = face_masks([face_ref[k, j : j + 1, :] for k in range(3) for j in range(4)])
    index = [frame_ref[8 * m : 8 * m + 8, :] for m in range(3)]
    low = [i & 127 for i in index]
    high = [i >> 7 for i in index]
    spots = [[jnp.zeros((8, 128), F32) for _ in range(3)] for _ in range(3)]
    for b in range(POOL_BLOCKS):
        for c in range(3):
            row = pool_ref[c, b : b + 1, :]
            for m in range(3):
                spots[m][c] = jnp.where(high[m] == b, lane_gather(row, low[m]), spots[m][c])
    levers, scales = [], []
    for m in range(3):
        lever = [spots[m][c] - own[c] for c in range(3)]
        levers.append(lever)
        scales.append(1.0 / (3.0 * (dot3(lever, lever) + LEVER_SOFT)))
    sub24 = lax.broadcasted_iota(jnp.int32, (ROWS, 128), 0)
    sub128 = lax.broadcasted_iota(jnp.int32, (128, 128), 0)
    hits, hot = [], []
    for m in range(3):
        for b in range(OWN_BLOCKS):
            hits.append(jnp.broadcast_to(high[m][b : b + 1], (ROWS, 128)) == sub24)
            lane = jnp.broadcast_to(low[m][b : b + 1], (128, 128)) == sub128
            hot.append(jnp.where(lane, 1.0, 0.0).astype(BF16))

    owned = partial
    for sets in ((0, 1), (2,)):
        for k in sets:
            copies[k].wait()
        added = scatter_sets(back_ref, 6, sets, blocks, lanes)
        owned = [rows + more for rows, more in zip(owned, added)]
    torque = owned[3:6]
    kept = [jnp.zeros((8, 128), F32) for _ in range(3)]
    columns = []
    for m in range(3):
        push = [w * scales[m] for w in cross3(torque, levers[m])]
        kept = [kept[c] + push[c] for c in range(3)]
        halves = [split2(w) for w in push]
        for b in range(OWN_BLOCKS):
            hit = hits[8 * m + b]
            parts = []
            for c in range(3):
                for half in halves[c]:
                    parts.append(jnp.where(hit, jnp.broadcast_to(half[b : b + 1], (ROWS, 128)), 0.0))
            columns.append(jnp.concatenate(parts, axis=0).astype(BF16))
    out = nt_dot(jnp.concatenate(columns, axis=1), jnp.concatenate(hot, axis=1))
    forces = []
    for c in range(3):
        rows = out[48 * c : 48 * c + 24] + out[48 * c + 24 : 48 * c + 48]
        forces.append(owned[c] + rows[0:8] - kept[c])
        for k in range(3):
            spread_ref[k, 4 * c : 4 * c + 4, :] = rows[8 + 4 * k : 12 + 4 * k]
    spread_ref[:, 12:16, :] = jnp.zeros((3, 4, 128), F32)
    copies = send_sets(spread_ref, last_ref, last_send, last_recv, up)
    for sets in ((0, 1), (2,)):
        for k in sets:
            copies[k].wait()
        added = scatter_sets(last_ref, 3, sets, blocks, lanes)
        forces = [rows + more for rows, more in zip(forces, added)]
    for c in range(3):
        out_ref[8 * c : 8 * c + 8, :] = forces[c]


def domain_forces(sizes, coords, multipoles, face_atoms, frame_atoms, tile_pairs, tile_count):
    vmem = pl.BlockSpec(memory_space=pltpu.VMEM)
    hbm = pl.BlockSpec(memory_space=pltpu.HBM)
    return pl.pallas_call(
        functools.partial(kernel_body, sizes),
        out_shape=jax.ShapeDtypeStruct((24, 128), F32),
        in_specs=[hbm] * 6,
        out_specs=vmem,
        scratch_shapes=[
            pltpu.VMEM((24, 128), F32),
            pltpu.VMEM((80, 128), F32),
            pltpu.VMEM((3, 4, 128), jnp.int32),
            pltpu.VMEM((24, 128), jnp.int32),
            pltpu.SMEM((1, 1, 2, 32), jnp.int32),
            pltpu.SMEM((1, 1), jnp.int32),
            pltpu.SemaphoreType.DMA((6,)),
            pltpu.VMEM((3, 56, 128), F32),
            pltpu.VMEM((3, 56, 128), F32),
            pltpu.VMEM((3, 24, 128), F32),
            pltpu.VMEM((3, 24, 128), F32),
            pltpu.VMEM((3, 16, 128), F32),
            pltpu.VMEM((3, 16, 128), F32),
            pltpu.VMEM((8, 128), jnp.int32),
            pltpu.SMEM((8, 128), jnp.int32),
            pltpu.VMEM((13, ROWS, 128), F32),
            pltpu.VMEM((64 * ROWS, 128), F32),
            pltpu.VMEM((88 * 8, 128), F32),
            pltpu.VMEM((184 * ROWS, 128), F32),
            pltpu.VMEM((POOL_BLOCKS, 128, 128), BF16),
            pltpu.VMEM((OWN_BLOCKS, 128, 384), BF16),
            pltpu.VMEM((POOL_BLOCKS, 128, 896), BF16),
            pltpu.VMEM((POOL_BLOCKS, 8, 128), F32),
            pltpu.VMEM((OWN_BLOCKS, 3, 128, 128), F32),
            pltpu.VMEM((3, 128, 128), F32),
            pltpu.VMEM((EVENTS + 1, ACC_GROUPS, 8, 128), F32),
            pltpu.VMEM((ROWS * 8 * ACC_GROUPS, 128), F32),
        ]
        + [pltpu.SemaphoreType.DMA((3,))] * 6
        + [pltpu.SemaphoreType.DMA],
        compiler_params=pltpu.CompilerParams(collective_id=0, has_side_effects=True, vmem_limit_bytes=60 << 20),
    )(coords, multipoles, face_atoms, frame_atoms, tile_pairs, tile_count)


def solution(mesh):
    sizes = (mesh.shape["gx"], mesh.shape["gy"])

    def shards(coords, multipoles, face_atoms, tile_pairs, tile_count, frame_atoms, send_list, send_count):
        coords = coords.reshape(24, 128)
        multipoles = multipoles.reshape(80, 128)
        face_atoms = face_atoms.reshape(3, 4, 128)
        frame_atoms = frame_atoms.reshape(24, 128)
        forces = domain_forces(sizes, coords, multipoles, face_atoms, frame_atoms, tile_pairs, tile_count)
        return forces.reshape(1, 1, 3, 1024)

    four = P("gx", "gy", None, None)
    placed = (four, four, four, four, P("gx", "gy"), four, four, P("gx", "gy", None))
    return jax.shard_map(shards, mesh=mesh, in_specs=placed, out_specs=four, check_vma=False)
```

```python
import functools

import jax
import jax.numpy as jnp
from jax import lax
from jax.experimental import pallas as pl
from jax.experimental.pallas import tpu as pltpu
from jax.sharding import PartitionSpec as P

SOFTENING = 0.5
LEVER_SOFT = 0.04
OWN_BLOCKS = 8
POOL_BLOCKS = 20
ROWS = 24
ENTRIES = ((0, 0), (1, 1), (2, 2), (0, 1), (0, 2), (1, 2))
ENTRY_AT = {(0, 0): 0, (1, 1): 1, (2, 2): 2, (0, 1): 3, (1, 0): 3, (0, 2): 4, (2, 0): 4, (1, 2): 5, (2, 1): 5}
MULT = (1.0, 1.0, 1.0, 2.0, 2.0, 2.0)
F32 = jnp.float32
BF16 = jnp.bfloat16
ACC_GROUPS = 18
EVENTS = 64
TILE_STEP = 16
MESH = pl.DeviceIdType.MESH


def cross3(a, b):
    return (a[1] * b[2] - a[2] * b[1], a[2] * b[0] - a[0] * b[2], a[0] * b[1] - a[1] * b[0])


def dot3(a, b):
    return a[0] * b[0] + a[1] * b[1] + a[2] * b[2]


def mat_vec(m, v):
    return [sum_list([m[ENTRY_AT[(r, c)]] * v[c] for c in range(3)]) for r in range(3)]


def sum_list(items):
    total = items[0]
    for item in items[1:]:
        total = total + item
    return total


def sym_outer(a, b):
    out = []
    for r, c in ENTRIES:
        if r == c:
            out.append(a[r] * b[r])
        else:
            out.append(0.5 * (a[r] * b[c] + a[c] * b[r]))
    return out


def split2(value):
    hi = value.astype(BF16).astype(F32)
    lo = (value - hi).astype(BF16).astype(F32)
    return hi, lo


def nt_dot(a, b):
    return lax.dot_general(a, b, (((1,), (1,)), ((), ())), preferred_element_type=F32)


def mm(a, b):
    return lax.dot_general(a, b, (((1,), (0,)), ((), ())), preferred_element_type=F32)


def lane_gather(row, index):
    table = jnp.broadcast_to(row, (8, 128))
    return jnp.take_along_axis(table, index, axis=1)


def face_masks(face_rows):
    sub8 = lax.broadcasted_iota(jnp.int32, (8, 128), 0)
    sub128 = lax.broadcasted_iota(jnp.int32, (128, 128), 0)
    blocks, lanes = [], []
    for row in face_rows:
        blocks.append(jnp.broadcast_to(row >> 7, (8, 128)) == sub8)
        hit = jnp.broadcast_to(row & 127, (128, 128)) == sub128
        lanes.append(jnp.where(hit, 1.0, 0.0).astype(BF16))
    return blocks, lanes


def scatter_faces(values, blocks, lanes):
    comps = len(values)
    columns = []
    for j in range(len(blocks)):
        parts = []
        for c in range(comps):
            hi, lo = split2(values[c][j])
            parts.append(jnp.where(blocks[j], jnp.broadcast_to(hi, (8, 128)), 0.0))
            parts.append(jnp.where(blocks[j], jnp.broadcast_to(lo, (8, 128)), 0.0))
        columns.append(jnp.concatenate(parts, axis=0).astype(BF16))
    lhs = jnp.concatenate(columns, axis=1)
    rhs = jnp.concatenate(lanes, axis=1)
    out = nt_dot(lhs, rhs)
    return [out[16 * c : 16 * c + 8] + out[16 * c + 8 : 16 * c + 16] for c in range(comps)]


def neighbours(sizes):
    gx, gy = lax.axis_index("gx"), lax.axis_index("gy")
    nx, ny = sizes
    up = (lax.rem(gx + 1, nx), lax.rem(gy + 1, ny))
    down = (lax.rem(gx + nx - 1, nx), lax.rem(gy + ny - 1, ny))
    return [[(to[0], gy), (gx, to[1]), (to[0], to[1])] for to in (up, down)]


def greet(senders):
    for peer in senders:
        pl.semaphore_signal(pltpu.get_barrier_semaphore(), inc=1, device_id=peer, device_id_type=MESH)


def send_sets(send_ref, recv_ref, send_sem, recv_sem, targets):
    copies = []
    for k, peer in enumerate(targets):
        copy = pltpu.make_async_remote_copy(
            src_ref=send_ref.at[k],
            dst_ref=recv_ref.at[k],
            send_sem=send_sem.at[k],
            recv_sem=recv_sem.at[k],
            device_id=peer,
            device_id_type=MESH,
        )
        copy.start()
        copies.append(copy)
    return copies


def pool_features(pool):
    x = [pool[0] - 1.0, pool[1] - 1.0, pool[2] - 0.5]
    q = pool[3]
    d = [pool[4], pool[5], pool[6]]
    quad = [pool[7], pool[8], pool[9], pool[10], pool[11], pool[12]]
    one = jnp.ones_like(q)
    xx = [x[r] * x[c] for r, c in ENTRIES]
    qx = [q * x[r] for r in range(3)]
    m = [qx[r] + d[r] for r in range(3)]
    turned = mat_vec(quad, x)
    dx = dot3(d, x)
    xqx = dot3(x, turned)
    sdx = sym_outer(d, x)
    h = [q * xx[e] + 2.0 * sdx[e] for e in range(6)]
    tx = sym_outer(turned, x)
    outer = [[quad[e] * x[c] for c in range(3)] for e in range(6)]
    return dict(one=one, x=x, q=q, d=d, quad=quad, xx=xx, qx=qx, m=m, turned=turned, dx=dx, xqx=xqx, h=h, tx=tx, outer=outer)


def sum_rows(f):
    zero = jnp.zeros_like(f["one"])
    rows = [*f["xx"], zero, zero]
    rows += [f["one"], *f["x"], f["q"], *f["d"]]
    rows += [*f["qx"], *f["m"], zero, zero]
    rows += [*f["quad"], *f["turned"], *f["h"], zero]
    rows += [*f["tx"]] + [f["outer"][e][c] for e in range(6) for c in range(3)]
    return rows


def column_rows(f):
    zero = jnp.zeros_like(f["one"])
    first = [*f["d"], f["dx"], *f["quad"], *f["turned"], f["xqx"], f["one"], *f["x"], *f["xx"]]
    second = [*f["d"], f["dx"], f["q"], *f["qx"], *f["quad"], *f["turned"], f["xqx"], *f["h"]]
    third = [*f["quad"], *f["turned"], *f["tx"]] + [f["outer"][e][c] for e in range(6) for c in range(3)]
    return first + second + third + [zero] * 7


def coefficient_rows(f):
    zero = jnp.zeros_like(f["one"])
    one = f["one"]
    x, d, q, xx = f["x"], f["d"], f["q"], f["xx"]
    quad, turned = f["quad"], f["turned"]
    z = lambda n: [zero] * n
    u = [-3.0 * x[r] for r in range(3)] + [3.0 * one] + z(20)
    v = z(14) + [-3.0 * f["dx"]] + [3.0 * d[r] for r in range(3)] + z(6)
    p = z(4) + [15.0 * MULT[e] * xx[e] for e in range(6)] + [-30.0 * x[r] for r in range(3)] + [15.0 * one] + z(10)
    r_ = (
        z(14)
        + [15.0 * f["xqx"]]
        + [-30.0 * turned[r] for r in range(3)]
        + [15.0 * MULT[e] * quad[e] for e in range(6)]
    )
    l1 = [1.8 * f["m"][r] for r in range(3)] + [-1.8 * q, -1.8 * f["dx"]] + [1.8 * d[r] for r in range(3)]
    l1 += z(16)
    l2 = (
        [-18.0 * turned[r] for r in range(3)]
        + z(1)
        + [9.0 * f["xqx"]]
        + [-18.0 * turned[r] for r in range(3)]
        + [9.0 * MULT[e] * (f["h"][e] + 2.0 * quad[e]) for e in range(6)]
        + [-18.0 * f["m"][r] for r in range(3)]
        + [9.0 * q]
        + [9.0 * MULT[e] * quad[e] for e in range(6)]
    )
    l3 = [-252.0 * MULT[e] * f["tx"][e] for e in range(6)] + [252.0 * turned[r] for r in range(3)]
    l3 += [-252.0 * MULT[e] * quad[e] for e in range(6)]
    for a, b in ENTRIES:
        for c in range(3):
            term = quad[ENTRY_AT[(a, c)]] * x[b]
            if a != b:
                term = term + quad[ENTRY_AT[(b, c)]] * x[a]
            l3.append(252.0 * term)
    l3 += z(7)
    return [u, v, p, r_, l1, l2, l3]


def pool_block(b, sum_scr, col_scr, feat_ref, col_ref, place_ref):
    sums = sum_scr[pl.ds(b, 64, stride=ROWS), :]
    place_ref[b] = sums[8:16]
    hi, lo = split2(sums)
    parts = []
    for g in range(8):
        parts += [hi[8 * g : 8 * g + 8], lo[8 * g : 8 * g + 8]]
    feat_ref[b] = jnp.concatenate(parts, axis=0).astype(BF16)
    start = 0
    for group, count in enumerate((24, 24, 40)):
        rows = col_scr[pl.ds(b + start * ROWS, count, stride=ROWS), :]
        start += count
        hi, lo = split2(rows)
        stacked = jnp.concatenate([hi, hi, lo, jnp.zeros((128 - 3 * count, 128), F32)], axis=0)
        col_ref[b, group] = stacked.astype(BF16)


def own_rows(b, row_scr, row_ref, place_ref, wide_ref):
    start = 0
    for out_id, count in enumerate((24, 24, 24, 24, 24, 24, 40)):
        rows = row_scr[pl.ds(b + start * 8, count, stride=8), :]
        start += count
        hi, lo = split2(rows)
        pad = [jnp.zeros((128 - 3 * count, 128), F32)]
        stacked = jnp.concatenate([hi, lo, hi] + pad, axis=0).astype(BF16)
        row_ref[b, out_id * 128 : (out_id + 1) * 128, :] = stacked.T
    place = jnp.concatenate([place_ref[b], jnp.zeros((120, 128), F32)], axis=0).T
    for r in range(3):
        wide_ref[b, r] = jnp.broadcast_to(place[:, r + 1 : r + 2], (128, 128))


def store_rows(pool, low, high, sum_scr, col_scr):
    f = pool_features([pool[c][low:high] for c in range(13)])
    for n, row in enumerate(sum_rows(f)):
        sum_scr[n * ROWS + low : n * ROWS + high, :] = row
    for n, row in enumerate(column_rows(f)):
        col_scr[n * ROWS + low : n * ROWS + high, :] = row
    return f


def tile_work(near, far, row_ref, col_ref, place_ref, wide_ref, keep_ref, keep):
    first = mm(row_ref[near, 0:512, :], col_ref[far, 0])
    second = mm(row_ref[near, 512:768, :], col_ref[far, 1])
    third = mm(row_ref[near, 768:896, :], col_ref[far, 2])
    chunk = 32
    names = ("b1", "b2", "b3", "al", "be", "ga", "de", "e1")
    pieces = {name: ([], []) for name in names}
    place = [jnp.broadcast_to(place_ref[far, r + 1 : r + 2, :], (chunk, 128)) for r in range(3)]
    for row in range(0, 128, chunk):
        rows = slice(row, row + chunk)
        diff = [place[r] - wide_ref[near, r, rows, :] for r in range(3)]
        dist = diff[0] * diff[0] + (diff[1] * diff[1] + (diff[2] * diff[2] + SOFTENING))
        root = lax.rsqrt(dist)
        t = root * root
        b0 = root * keep_ref[keep, rows, :]
        b1 = b0 * t
        b2 = b1 * t
        b3 = b2 * t
        v, u, r_, p = [first[n * 128 + row : n * 128 + row + chunk] for n in range(4)]
        rt, pt = r_ * t, p * t
        l1, l2 = [second[n * 128 + row : n * 128 + row + chunk] for n in range(2)]
        l3 = third[rows]
        gr, gp = 1.4 * rt - v, 1.4 * pt + u
        al = b2 * (rt - v)
        be = b2 * (pt + u)
        ga = b3 * gr
        de = b3 * gp
        e1 = b2 * (l1 + t * (l2 + gr * gp + 0.56 * (rt * pt) + t * l3))
        for name, value in zip(names, (b1, b2, b3, al, be, ga, de, e1)):
            hi = value.astype(BF16)
            pieces[name][0].append(hi)
            pieces[name][1].append((value - hi.astype(F32)).astype(BF16))
    return {name: (jnp.concatenate(h, axis=0), jnp.concatenate(l, axis=0)) for name, (h, l) in pieces.items()}


def tile_sums(w, near, far, feat_ref, add):
    slots = {
        "a": ((0, 1),),
        "ap": ((1, 1),),
        "e": ((2, 1),),
        "b1": ((3, 1), (4, 2)),
        "b2": ((5, 1), (6, 2), (7, 3), (8, 4)),
        "cp": ((9, 3), (10, 4)),
        "c": ((11, 1), (12, 0)),
        "b3": ((13, 3), (14, 4), (15, 5), (16, 6), (17, 7)),
    }

    def pairs_for(a, ap, c, cp):
        return (
            (a, ap, 1, 2, slots["a"], slots["ap"]),
            ("e1", c, 0, 2, slots["e"], slots["c"]),
            ("b1", "b2", 1, 5, slots["b1"], slots["b2"]),
            (cp, "b3", 3, 8, slots["cp"], slots["b3"]),
        )

    near_pairs = pairs_for("al", "be", "ga", "de")
    far_pairs = pairs_for("be", "al", "de", "ga")
    for pairs, source, side, transposed in ((near_pairs, far, 0, True), (far_pairs, near, 1, False)):
        for one, two, first, final, slots_one, slots_two in pairs:
            feats = feat_ref[source, 16 * first : 16 * final, :]
            lhs = jnp.concatenate([feats, feats], axis=1)
            if transposed:
                rhs = jnp.concatenate(
                    [jnp.concatenate([w[one][s].T, w[two][s].T], axis=1) for s in range(2)], axis=0
                )
                out = mm(lhs, rhs)
            else:
                rhs = jnp.concatenate(
                    [jnp.concatenate([w[one][s], w[two][s]], axis=1) for s in range(2)], axis=0
                )
                out = mm(lhs, rhs)
            for half, targets in enumerate((slots_one, slots_two)):
                lanes = slice(128 * half, 128 * half + 128)
                for slot, group in targets:
                    at = 16 * (group - first)
                    add(side, slot, out[at : at + 8, lanes] + out[at + 8 : at + 16, lanes])


def finish_sums(load, f):
    x, q, d, quad = f["x"], f["q"], f["d"], f["quad"]
    turned = f["turned"]
    a_one, a_x = load(0, 0), [load(0, 1 + r) for r in range(3)]
    ap_d = [load(1, 5 + r) for r in range(3)]
    e_one, e_x = load(2, 0), [load(2, 1 + r) for r in range(3)]
    b1_q, b1_d = load(3, 4), [load(3, 5 + r) for r in range(3)]
    b1_qx = [load(4, r) for r in range(3)]
    b2_q, b2_m = load(5, 4), [load(6, 3 + r) for r in range(3)]

    def wide(slot):
        flat = lambda n: load(slot + n // 8, n % 8)
        return [flat(e) for e in range(6)], [flat(6 + r) for r in range(3)]

    b2_quad, b2_t = wide(7)
    b2_h = [load(7 + (9 + e) // 8, (9 + e) % 8) for e in range(6)]
    cp_quad, cp_t = wide(9)
    c_one, c_x = load(11, 0), [load(11, 1 + r) for r in range(3)]
    c_xx = [load(12, e) for e in range(6)]
    b3_quad, b3_t = wide(13)
    b3_tx = [load(15, e) for e in range(6)]
    b3_outer = [[load(15 + (6 + 3 * e + c) // 8, (6 + 3 * e + c) % 8) for c in range(3)] for e in range(6)]

    b2_quad_x = mat_vec(b2_quad, x)
    b3_quad_x = mat_vec(b3_quad, x)
    cp_quad_x = mat_vec(cp_quad, x)
    b2_turn = [b2_t[r] - b2_quad_x[r] for r in range(3)]
    b3_turn = [b3_t[r] - b3_quad_x[r] for r in range(3)]
    cp_turn = [cp_t[r] - cp_quad_x[r] for r in range(3)]
    b1_r = [b1_qx[r] - x[r] * b1_q for r in range(3)]
    a_r = [a_x[r] - x[r] * a_one for r in range(3)]
    e_r = [e_x[r] - x[r] * e_one for r in range(3)]
    c_r = [c_x[r] - x[r] * c_one for r in range(3)]
    b2_r = [b2_m[r] - x[r] * b2_q for r in range(3)]

    slope_d = [a_r[r] + b1_r[r] + b1_d[r] - 6.0 * b2_turn[r] for r in range(3)]

    sx_c = sym_outer(c_x, x)
    sx_m = sym_outer(b2_m, x)
    sx_t = sym_outer(b3_t, x)
    sx_q = sym_outer(b3_quad_x, x)
    mixed = [
        [sum_list([b3_outer[ENTRY_AT[(a, c)]][b] * x[c] for c in range(3)]) for b in range(3)] for a in range(3)
    ]
    slope_q = []
    for e, (a, b) in enumerate(ENTRIES):
        ym = mixed[a][b] if a == b else 0.5 * (mixed[a][b] + mixed[b][a])
        slope_q.append(
            5.0 * (c_xx[e] - 2.0 * sx_c[e] + c_one * f["xx"][e])
            + 3.0 * (b2_h[e] - 2.0 * sx_m[e] + b2_q * f["xx"][e])
            + 6.0 * b2_quad[e]
            - 60.0 * (b3_tx[e] - sx_t[e] - ym + sx_q[e])
        )

    inner = [10.0 * c_r[r] + 6.0 * b2_r[r] - 60.0 * b3_turn[r] for r in range(3)]
    inner = mat_vec(quad, inner)
    b2_quad_d = mat_vec(b2_quad, d)
    b3_quad_t = mat_vec(b3_quad, turned)
    force = []
    for a in range(3):
        spun = sum_list(
            [
                b3_outer[ENTRY_AT[(a, b)]][c] * quad[ENTRY_AT[(b, c)]]
                for b in range(3)
                for c in range(3)
            ]
        )
        force.append(
            -q * (b1_r[a] + b1_d[a])
            - (5.0 / 3.0) * e_r[a]
            + d[a] * (a_one + b1_q)
            - ap_d[a]
            + inner[a]
            + 10.0 * cp_turn[a]
            + 6.0 * q * b2_turn[a]
            - 6.0 * b2_quad_d[a]
            - 60.0 * (spun - b3_quad_t[a])
        )

    full = lambda m, r, c: m[ENTRY_AT[(r, c)]]

    def commutator(r, c):
        return sum_list(
            [full(quad, r, k) * full(slope_q, k, c) - full(slope_q, r, k) * full(quad, k, c) for k in range(3)]
        )

    twist = cross3(d, slope_d)
    torque = [
        2.0 * commutator(2, 1) - twist[0],
        2.0 * commutator(0, 2) - twist[1],
        2.0 * commutator(1, 0) - twist[2],
    ]
    return force, torque


def gather_exports(coords_ref, mult_ref, face_ref, send_ref):
    face = jnp.concatenate([face_ref[k] for k in range(3)] + [jnp.zeros((4, 128), jnp.int32)], axis=0)
    shift = lax.broadcasted_iota(jnp.int32, (16, 128), 0)
    shift_x = jnp.where((shift < 4) | (shift >= 8), 1.0, 0.0).astype(F32)
    shift_y = jnp.where(shift >= 4, 1.0, 0.0).astype(F32)
    halves = [face[0:8], face[8:16]]
    lows = [h & 127 for h in halves]
    highs = [h >> 7 for h in halves]
    for c in range(13):
        src, at = (coords_ref, 8 * c) if c < 3 else (mult_ref, 8 * (c - 3))
        got = []
        for part in range(2):
            total = jnp.zeros((8, 128), F32)
            for b in range(OWN_BLOCKS):
                picked = lane_gather(src[at + b : at + b + 1, :], lows[part])
                total = jnp.where(highs[part] == b, picked, total)
            got.append(total)
        rows = jnp.concatenate(got, axis=0)
        if c == 0:
            rows = rows + shift_x
        if c == 1:
            rows = rows + shift_y
        for k in range(3):
            send_ref[k, 4 * c : 4 * c + 4, :] = rows[4 * k : 4 * k + 4]
    for k in range(3):
        send_ref[k, 52:56, :] = jnp.zeros((4, 128), F32)


def event_tables(pairs_ref, table_ref):
    lane = lax.broadcasted_iota(jnp.int32, (8, 128), 1)
    blocks = [pairs_ref[0, 0, e % 2, e // 2] for e in range(EVENTS)]
    row = jnp.zeros((8, 128), jnp.int32)
    for e, block in enumerate(blocks):
        row = jnp.where(lane == e, block, row)
    before = jnp.full((8, 128), EVENTS, jnp.int32)
    last = jnp.full((8, 128), EVENTS, jnp.int32)
    for e, block in enumerate(blocks):
        before = jnp.where((row == block) & (lane > e), e, before)
        last = jnp.where(lane == block, e, last)
    sub = lax.broadcasted_iota(jnp.int32, (8, 128), 0)
    table_ref[...] = jnp.where(sub == 0, before, last)


def scatter_sets(back_ref, comps, sets, blocks, lanes):
    chosen = [(k, j) for k in sets for j in range(4)]
    values = [[back_ref[k, 4 * c + j : 4 * c + j + 1, :] for k, j in chosen] for c in range(comps)]
    return scatter_faces(values, [blocks[4 * k + j] for k, j in chosen], [lanes[4 * k + j] for k, j in chosen])


def kernel_body(
    sizes, coords_hbm, mult_hbm, face_hbm, frame_hbm, pairs_hbm, count_hbm, out_ref,
    coords_ref, mult_ref, face_ref, frame_ref, pairs_ref, count_ref, load_sem, send_ref, import_ref, halo_ref, back_ref, spread_ref, last_ref, table_ref, smem_ref,
    pool_ref, sum_scr, row_scr, col_scr, feat_ref, row_ref, col_ref, place_ref, wide_ref, keep_ref, runs_ref, acc_ref,
    send_sem, recv_sem, back_send, back_recv, last_send, last_recv, local_sem,
):
    up, down = neighbours(sizes)
    greet(up)
    loads = [
        pltpu.make_async_copy(source, target, load_sem.at[n])
        for n, (source, target) in enumerate(
            (
                (coords_hbm, coords_ref),
                (mult_hbm, mult_ref),
                (face_hbm, face_ref),
                (frame_hbm, frame_ref),
                (pairs_hbm, pairs_ref),
                (count_hbm, count_ref),
            )
        )
    ]
    for copy in loads:
        copy.start()
    for copy in loads:
        copy.wait()
    gather_exports(coords_ref, mult_ref, face_ref, send_ref)
    pl.semaphore_wait(pltpu.get_barrier_semaphore(), 3)
    copies = send_sets(send_ref, import_ref, send_sem, recv_sem, down)

    event_tables(pairs_ref, table_ref)
    table_copy = pltpu.make_async_copy(table_ref, smem_ref, local_sem)
    table_copy.start()
    own = [coords_ref[8 * c : 8 * c + 8, :] for c in range(3)] + [mult_ref[8 * c : 8 * c + 8, :] for c in range(10)]
    for c in range(13):
        pool_ref[c, 0:8, :] = own[c]
        pool_ref[c, 20:24, :] = jnp.zeros((4, 128), F32)
    f = store_rows(own, 0, 8, sum_scr, col_scr)
    for n, row in enumerate([row for group in coefficient_rows(f) for row in group]):
        row_scr[n * 8 : n * 8 + 8, :] = row
    above = lax.broadcasted_iota(jnp.int32, (128, 128), 0) < lax.broadcasted_iota(jnp.int32, (128, 128), 1)
    keep_ref[0] = jnp.ones((128, 128), F32)
    keep_ref[1] = jnp.where(above, 1.0, 0.0).astype(F32)
    keep_ref[2] = jnp.zeros((128, 128), F32)
    runs_ref[EVENTS] = jnp.zeros((ACC_GROUPS, 8, 128), F32)
    for b in range(POOL_BLOCKS, ROWS):
        acc_ref[b * 8 * ACC_GROUPS : (b + 1) * 8 * ACC_GROUPS, :] = jnp.zeros((8 * ACC_GROUPS, 128), F32)

    def own_block(b, _):
        pool_block(b, sum_scr, col_scr, feat_ref, col_ref, place_ref)
        own_rows(b, row_scr, row_ref, place_ref, wide_ref)
        return 0

    lax.fori_loop(0, OWN_BLOCKS, own_block, 0, unroll=4)
    table_copy.wait()

    def import_block(b, _):
        pool_block(b, sum_scr, col_scr, feat_ref, col_ref, place_ref)
        return 0

    for sets, rows, blocks in (((0, 1), (8, 16), (8, 16)), ((2,), (16, 24), (16, 20))):
        for k in sets:
            copies[k].wait()
        for c in range(13):
            for k in sets:
                pool_ref[c, 8 + 4 * k : 12 + 4 * k, :] = import_ref[k, 4 * c : 4 * c + 4, :]
        store_rows([pool_ref[c] for c in range(13)], *rows, sum_scr, col_scr)
        lax.fori_loop(*blocks, import_block, 0, unroll=4)

    def one(t):
        near, far = pairs_ref[0, 0, 0, t], pairs_ref[0, 0, 1, t]
        keep = jnp.where(t < count_ref[0, 0], jnp.where(near == far, 1, 0), 2)
        return t, near, far, tile_work(near, far, row_ref, col_ref, place_ref, wide_ref, keep_ref, keep)

    def sums(t, near, far, w):
        before = [smem_ref[0, 2 * t + side] for side in range(2)]

        def add(side, slot, value):
            runs_ref[2 * t + side, slot] = runs_ref[before[side], slot] + value

        tile_sums(w, near, far, feat_ref, add)

    def step(g, _):
        held = None
        for n in range(TILE_STEP):
            current = one(TILE_STEP * g + n)
            if held is not None:
                sums(*held)
            held = current
        sums(*held)
        return 0

    lax.fori_loop(0, EVENTS // 2 // TILE_STEP, step, 0)

    def finish(low, high):
        for b in range(low, min(high, POOL_BLOCKS)):
            at = smem_ref[1, b]
            for slot in range(ACC_GROUPS):
                row = (b * ACC_GROUPS + slot) * 8
                acc_ref[row : row + 8, :] = runs_ref[at, slot]

        def load(slot, row):
            at = low * 8 * ACC_GROUPS + 8 * slot + row
            return acc_ref[pl.ds(at, high - low, stride=8 * ACC_GROUPS), :]

        force, torque = finish_sums(load, pool_features([pool_ref[c, low:high, :] for c in range(13)]))
        return force + torque

    for c, rows in enumerate(finish(8, 24)):
        for k in range(3):
            halo_ref[k, 4 * c : 4 * c + 4, :] = rows[4 * k : 4 * k + 4]
    copies = send_sets(halo_ref, back_ref, back_send, back_recv, up)
    partial = finish(0, 8)

    blocks, lanes = face_masks([face_ref[k, j : j + 1, :] for k in range(3) for j in range(4)])
    index = [frame_ref[8 * m : 8 * m + 8, :] for m in range(3)]
    low = [i & 127 for i in index]
    high = [i >> 7 for i in index]
    spots = [[jnp.zeros((8, 128), F32) for _ in range(3)] for _ in range(3)]
    for b in range(POOL_BLOCKS):
        for c in range(3):
            row = pool_ref[c, b : b + 1, :]
            for m in range(3):
                spots[m][c] = jnp.where(high[m] == b, lane_gather(row, low[m]), spots[m][c])
    levers, scales = [], []
    for m in range(3):
        lever = [spots[m][c] - own[c] for c in range(3)]
        levers.append(lever)
        scales.append(1.0 / (3.0 * (dot3(lever, lever) + LEVER_SOFT)))
    sub24 = lax.broadcasted_iota(jnp.int32, (ROWS, 128), 0)
    sub128 = lax.broadcasted_iota(jnp.int32, (128, 128), 0)
    hits, hot = [], []
    for m in range(3):
        for b in range(OWN_BLOCKS):
            hits.append(jnp.broadcast_to(high[m][b : b + 1], (ROWS, 128)) == sub24)
            lane = jnp.broadcast_to(low[m][b : b + 1], (128, 128)) == sub128
            hot.append(jnp.where(lane, 1.0, 0.0).astype(BF16))

    owned = partial
    for sets in ((0, 1), (2,)):
        for k in sets:
            copies[k].wait()
        added = scatter_sets(back_ref, 6, sets, blocks, lanes)
        owned = [rows + more for rows, more in zip(owned, added)]
    torque = owned[3:6]
    kept = [jnp.zeros((8, 128), F32) for _ in range(3)]
    columns = []
    for m in range(3):
        push = [w * scales[m] for w in cross3(torque, levers[m])]
        kept = [kept[c] + push[c] for c in range(3)]
        halves = [split2(w) for w in push]
        for b in range(OWN_BLOCKS):
            hit = hits[8 * m + b]
            parts = []
            for c in range(3):
                for half in halves[c]:
                    parts.append(jnp.where(hit, jnp.broadcast_to(half[b : b + 1], (ROWS, 128)), 0.0))
            columns.append(jnp.concatenate(parts, axis=0).astype(BF16))
    out = nt_dot(jnp.concatenate(columns, axis=1), jnp.concatenate(hot, axis=1))
    forces = []
    for c in range(3):
        rows = out[48 * c : 48 * c + 24] + out[48 * c + 24 : 48 * c + 48]
        forces.append(owned[c] + rows[0:8] - kept[c])
        for k in range(3):
            spread_ref[k, 4 * c : 4 * c + 4, :] = rows[8 + 4 * k : 12 + 4 * k]
    spread_ref[:, 12:16, :] = jnp.zeros((3, 4, 128), F32)
    copies = send_sets(spread_ref, last_ref, last_send, last_recv, up)
    for sets in ((0, 1), (2,)):
        for k in sets:
            copies[k].wait()
        added = scatter_sets(last_ref, 3, sets, blocks, lanes)
        forces = [rows + more for rows, more in zip(forces, added)]
    for c in range(3):
        out_ref[8 * c : 8 * c + 8, :] = forces[c]


def domain_forces(sizes, coords, multipoles, face_atoms, frame_atoms, tile_pairs, tile_count):
    vmem = pl.BlockSpec(memory_space=pltpu.VMEM)
    hbm = pl.BlockSpec(memory_space=pltpu.HBM)
    return pl.pallas_call(
        functools.partial(kernel_body, sizes),
        out_shape=jax.ShapeDtypeStruct((24, 128), F32),
        in_specs=[hbm] * 6,
        out_specs=vmem,
        scratch_shapes=[
            pltpu.VMEM((24, 128), F32),
            pltpu.VMEM((80, 128), F32),
            pltpu.VMEM((3, 4, 128), jnp.int32),
            pltpu.VMEM((24, 128), jnp.int32),
            pltpu.SMEM((1, 1, 2, 32), jnp.int32),
            pltpu.SMEM((1, 1), jnp.int32),
            pltpu.SemaphoreType.DMA((6,)),
            pltpu.VMEM((3, 56, 128), F32),
            pltpu.VMEM((3, 56, 128), F32),
            pltpu.VMEM((3, 24, 128), F32),
            pltpu.VMEM((3, 24, 128), F32),
            pltpu.VMEM((3, 16, 128), F32),
            pltpu.VMEM((3, 16, 128), F32),
            pltpu.VMEM((8, 128), jnp.int32),
            pltpu.SMEM((8, 128), jnp.int32),
            pltpu.VMEM((13, ROWS, 128), F32),
            pltpu.VMEM((64 * ROWS, 128), F32),
            pltpu.VMEM((184 * 8, 128), F32),
            pltpu.VMEM((88 * ROWS, 128), F32),
            pltpu.VMEM((POOL_BLOCKS, 128, 128), BF16),
            pltpu.VMEM((OWN_BLOCKS, 896, 128), BF16),
            pltpu.VMEM((POOL_BLOCKS, 3, 128, 128), BF16),
            pltpu.VMEM((POOL_BLOCKS, 8, 128), F32),
            pltpu.VMEM((OWN_BLOCKS, 3, 128, 128), F32),
            pltpu.VMEM((3, 128, 128), F32),
            pltpu.VMEM((EVENTS + 1, ACC_GROUPS, 8, 128), F32),
            pltpu.VMEM((ROWS * 8 * ACC_GROUPS, 128), F32),
        ]
        + [pltpu.SemaphoreType.DMA((3,))] * 6
        + [pltpu.SemaphoreType.DMA],
        compiler_params=pltpu.CompilerParams(collective_id=0, has_side_effects=True, vmem_limit_bytes=52 << 20),
    )(*[pltpu.with_memory_space_constraint(a, pltpu.HBM) for a in (coords, multipoles, face_atoms, frame_atoms, tile_pairs)], tile_count)


def solution(mesh):
    sizes = (mesh.shape["gx"], mesh.shape["gy"])

    def shards(coords, multipoles, face_atoms, tile_pairs, tile_count, frame_atoms, send_list, send_count):
        coords = coords.reshape(24, 128)
        multipoles = multipoles.reshape(80, 128)
        face_atoms = face_atoms.reshape(3, 4, 128)
        frame_atoms = frame_atoms.reshape(24, 128)
        forces = domain_forces(sizes, coords, multipoles, face_atoms, frame_atoms, tile_pairs, tile_count)
        return forces.reshape(1, 1, 3, 1024)

    four = P("gx", "gy", None, None)
    placed = (four, four, four, four, P("gx", "gy"), four, four, P("gx", "gy", None))
    return jax.shard_map(shards, mesh=mesh, in_specs=placed, out_specs=four, check_vma=False)
```

```python
import functools

import jax
import jax.numpy as jnp
from jax import lax
from jax.experimental import pallas as pl
from jax.experimental.pallas import tpu as pltpu
from jax.sharding import PartitionSpec as P

SOFTENING = 0.5
LEVER_SOFT = 0.04
OWN_BLOCKS = 8
POOL_BLOCKS = 20
ROWS = 24
ENTRIES = ((0, 0), (1, 1), (2, 2), (0, 1), (0, 2), (1, 2))
ENTRY_AT = {(0, 0): 0, (1, 1): 1, (2, 2): 2, (0, 1): 3, (1, 0): 3, (0, 2): 4, (2, 0): 4, (1, 2): 5, (2, 1): 5}
MULT = (1.0, 1.0, 1.0, 2.0, 2.0, 2.0)
F32 = jnp.float32
BF16 = jnp.bfloat16
ACC_GROUPS = 18
EVENTS = 64
TILE_STEP = 32
MESH = pl.DeviceIdType.MESH


def cross3(a, b):
    return (a[1] * b[2] - a[2] * b[1], a[2] * b[0] - a[0] * b[2], a[0] * b[1] - a[1] * b[0])


def dot3(a, b):
    return a[0] * b[0] + a[1] * b[1] + a[2] * b[2]


def mat_vec(m, v):
    return [sum_list([m[ENTRY_AT[(r, c)]] * v[c] for c in range(3)]) for r in range(3)]


def sum_list(items):
    total = items[0]
    for item in items[1:]:
        total = total + item
    return total


def sym_outer(a, b):
    out = []
    for r, c in ENTRIES:
        if r == c:
            out.append(a[r] * b[r])
        else:
            out.append(0.5 * (a[r] * b[c] + a[c] * b[r]))
    return out


def split2(value):
    hi = value.astype(BF16).astype(F32)
    lo = (value - hi).astype(BF16).astype(F32)
    return hi, lo


def nt_dot(a, b):
    return lax.dot_general(a, b, (((1,), (1,)), ((), ())), preferred_element_type=F32)


def mm(a, b):
    return lax.dot_general(a, b, (((1,), (0,)), ((), ())), preferred_element_type=F32)


def lane_gather(row, index):
    table = jnp.broadcast_to(row, (8, 128))
    return jnp.take_along_axis(table, index, axis=1)


def face_masks(face_rows):
    sub8 = lax.broadcasted_iota(jnp.int32, (8, 128), 0)
    sub128 = lax.broadcasted_iota(jnp.int32, (128, 128), 0)
    blocks, lanes = [], []
    for row in face_rows:
        blocks.append(jnp.broadcast_to(row >> 7, (8, 128)) == sub8)
        hit = jnp.broadcast_to(row & 127, (128, 128)) == sub128
        lanes.append(jnp.where(hit, 1.0, 0.0).astype(BF16))
    return blocks, lanes


def scatter_faces(values, blocks, lanes):
    comps = len(values)
    columns = []
    for j in range(len(blocks)):
        parts = []
        for c in range(comps):
            hi, lo = split2(values[c][j])
            parts.append(jnp.where(blocks[j], jnp.broadcast_to(hi, (8, 128)), 0.0))
            parts.append(jnp.where(blocks[j], jnp.broadcast_to(lo, (8, 128)), 0.0))
        columns.append(jnp.concatenate(parts, axis=0).astype(BF16))
    lhs = jnp.concatenate(columns, axis=1)
    rhs = jnp.concatenate(lanes, axis=1)
    out = nt_dot(lhs, rhs)
    return [out[16 * c : 16 * c + 8] + out[16 * c + 8 : 16 * c + 16] for c in range(comps)]


def neighbours(sizes):
    gx, gy = lax.axis_index("gx"), lax.axis_index("gy")
    nx, ny = sizes
    up = (lax.rem(gx + 1, nx), lax.rem(gy + 1, ny))
    down = (lax.rem(gx + nx - 1, nx), lax.rem(gy + ny - 1, ny))
    return [[(to[0], gy), (gx, to[1]), (to[0], to[1])] for to in (up, down)]


def greet(senders):
    for peer in senders:
        pl.semaphore_signal(pltpu.get_barrier_semaphore(), inc=1, device_id=peer, device_id_type=MESH)


def send_sets(send_ref, recv_ref, send_sem, recv_sem, targets, sets=(2, 0, 1)):
    copies = {}
    for k in sets:
        copy = pltpu.make_async_remote_copy(
            src_ref=send_ref.at[k],
            dst_ref=recv_ref.at[k],
            send_sem=send_sem.at[k],
            recv_sem=recv_sem.at[k],
            device_id=targets[k],
            device_id_type=MESH,
        )
        copy.start()
        copies[k] = copy
    return copies


def pool_features(pool):
    x = [pool[0] - 1.0, pool[1] - 1.0, pool[2] - 0.5]
    q = pool[3]
    d = [pool[4], pool[5], pool[6]]
    quad = [pool[7], pool[8], pool[9], pool[10], pool[11], pool[12]]
    one = jnp.ones_like(q)
    xx = [x[r] * x[c] for r, c in ENTRIES]
    qx = [q * x[r] for r in range(3)]
    m = [qx[r] + d[r] for r in range(3)]
    turned = mat_vec(quad, x)
    dx = dot3(d, x)
    xqx = dot3(x, turned)
    sdx = sym_outer(d, x)
    h = [q * xx[e] + 2.0 * sdx[e] for e in range(6)]
    tx = sym_outer(turned, x)
    outer = [[quad[e] * x[c] for c in range(3)] for e in range(6)]
    return dict(one=one, x=x, q=q, d=d, quad=quad, xx=xx, qx=qx, m=m, turned=turned, dx=dx, xqx=xqx, h=h, tx=tx, outer=outer)


def sum_rows(f):
    zero = jnp.zeros_like(f["one"])
    rows = [*f["xx"], zero, zero]
    rows += [f["one"], *f["x"], f["q"], *f["d"]]
    rows += [*f["qx"], *f["m"], zero, zero]
    rows += [*f["quad"], *f["turned"], *f["h"], zero]
    rows += [*f["tx"]] + [f["outer"][e][c] for e in range(6) for c in range(3)]
    return rows


def column_rows(f):
    zero = jnp.zeros_like(f["one"])
    first = [*f["d"], f["dx"], *f["quad"], *f["turned"], f["xqx"], f["one"], *f["x"], *f["xx"]]
    second = [*f["d"], f["dx"], f["q"], *f["qx"], *f["quad"], *f["turned"], f["xqx"], *f["h"]]
    third = [*f["quad"], *f["turned"], *f["tx"]] + [f["outer"][e][c] for e in range(6) for c in range(3)]
    return first + second + third + [zero] * 7


def coefficient_rows(f):
    zero = jnp.zeros_like(f["one"])
    one = f["one"]
    x, d, q, xx = f["x"], f["d"], f["q"], f["xx"]
    quad, turned = f["quad"], f["turned"]
    z = lambda n: [zero] * n
    u = [-3.0 * x[r] for r in range(3)] + [3.0 * one] + z(20)
    v = z(14) + [-3.0 * f["dx"]] + [3.0 * d[r] for r in range(3)] + z(6)
    p = z(4) + [15.0 * MULT[e] * xx[e] for e in range(6)] + [-30.0 * x[r] for r in range(3)] + [15.0 * one] + z(10)
    r_ = (
        z(14)
        + [15.0 * f["xqx"]]
        + [-30.0 * turned[r] for r in range(3)]
        + [15.0 * MULT[e] * quad[e] for e in range(6)]
    )
    l1 = [1.8 * f["m"][r] for r in range(3)] + [-1.8 * q, -1.8 * f["dx"]] + [1.8 * d[r] for r in range(3)]
    l1 += z(16)
    l2 = (
        [-18.0 * turned[r] for r in range(3)]
        + z(1)
        + [9.0 * f["xqx"]]
        + [-18.0 * turned[r] for r in range(3)]
        + [9.0 * MULT[e] * (f["h"][e] + 2.0 * quad[e]) for e in range(6)]
        + [-18.0 * f["m"][r] for r in range(3)]
        + [9.0 * q]
        + [9.0 * MULT[e] * quad[e] for e in range(6)]
    )
    l3 = [-252.0 * MULT[e] * f["tx"][e] for e in range(6)] + [252.0 * turned[r] for r in range(3)]
    l3 += [-252.0 * MULT[e] * quad[e] for e in range(6)]
    for a, b in ENTRIES:
        for c in range(3):
            term = quad[ENTRY_AT[(a, c)]] * x[b]
            if a != b:
                term = term + quad[ENTRY_AT[(b, c)]] * x[a]
            l3.append(252.0 * term)
    l3 += z(7)
    return [u, v, p, r_, l1, l2, l3]


def pool_block(b, sum_scr, col_scr, feat_ref, col_ref, place_ref):
    sums = sum_scr[pl.ds(b, 64, stride=ROWS), :]
    place_ref[b] = sums[8:16]
    hi, lo = split2(sums)
    parts = []
    for g in range(8):
        parts += [hi[8 * g : 8 * g + 8], lo[8 * g : 8 * g + 8]]
    feat_ref[b] = jnp.concatenate(parts, axis=0).astype(BF16)
    start = 0
    for group, count in enumerate((24, 24, 40)):
        rows = col_scr[pl.ds(b + start * ROWS, count, stride=ROWS), :]
        start += count
        hi, lo = split2(rows)
        stacked = jnp.concatenate([hi, hi, lo, jnp.zeros((128 - 3 * count, 128), F32)], axis=0)
        col_ref[b, group] = stacked.astype(BF16)


def own_rows(b, row_scr, row_ref, place_ref, wide_ref):
    start = 0
    for out_id, count in enumerate((24, 24, 24, 24, 24, 24, 40)):
        rows = row_scr[pl.ds(b + start * 8, count, stride=8), :]
        start += count
        hi, lo = split2(rows)
        pad = [jnp.zeros((128 - 3 * count, 128), F32)]
        stacked = jnp.concatenate([hi, lo, hi] + pad, axis=0).astype(BF16)
        row_ref[b, out_id * 128 : (out_id + 1) * 128, :] = stacked.T
    place = jnp.concatenate([place_ref[b], jnp.zeros((120, 128), F32)], axis=0).T
    for r in range(3):
        wide_ref[b, r] = jnp.broadcast_to(place[:, r + 1 : r + 2], (128, 128))


def store_rows(pool, low, high, sum_scr, col_scr):
    f = pool_features([pool[c][low:high] for c in range(13)])
    for n, row in enumerate(sum_rows(f)):
        sum_scr[n * ROWS + low : n * ROWS + high, :] = row
    for n, row in enumerate(column_rows(f)):
        col_scr[n * ROWS + low : n * ROWS + high, :] = row
    return f


def tile_work(near, far, row_ref, col_ref, place_ref, wide_ref, keep_ref, keep):
    first = mm(row_ref[near, 0:512, :], col_ref[far, 0])
    second = mm(row_ref[near, 512:768, :], col_ref[far, 1])
    third = mm(row_ref[near, 768:896, :], col_ref[far, 2])
    chunk = 32
    names = ("b1", "b2", "b3", "al", "be", "ga", "de", "e1")
    pieces = {name: ([], []) for name in names}
    place = [jnp.broadcast_to(place_ref[far, r + 1 : r + 2, :], (chunk, 128)) for r in range(3)]
    for row in range(0, 128, chunk):
        rows = slice(row, row + chunk)
        diff = [place[r] - wide_ref[near, r, rows, :] for r in range(3)]
        dist = diff[0] * diff[0] + (diff[1] * diff[1] + (diff[2] * diff[2] + SOFTENING))
        root = lax.rsqrt(dist)
        t = root * root
        b0 = root * keep_ref[keep, rows, :]
        b1 = b0 * t
        b2 = b1 * t
        b3 = b2 * t
        v, u, r_, p = [first[n * 128 + row : n * 128 + row + chunk] for n in range(4)]
        rt, pt = r_ * t, p * t
        l1, l2 = [second[n * 128 + row : n * 128 + row + chunk] for n in range(2)]
        l3 = third[rows]
        gr, gp = 1.4 * rt - v, 1.4 * pt + u
        al = b2 * (rt - v)
        be = b2 * (pt + u)
        ga = b3 * gr
        de = b3 * gp
        e1 = b2 * (l1 + t * (l2 + gr * gp + 0.56 * (rt * pt) + t * l3))
        for name, value in zip(names, (b1, b2, b3, al, be, ga, de, e1)):
            hi = value.astype(BF16)
            pieces[name][0].append(hi)
            pieces[name][1].append((value - hi.astype(F32)).astype(BF16))
    return {name: (jnp.concatenate(h, axis=0), jnp.concatenate(l, axis=0)) for name, (h, l) in pieces.items()}


def tile_sums(w, near, far, feat_ref, add):
    slots = {
        "a": ((0, 1),),
        "ap": ((1, 1),),
        "e": ((2, 1),),
        "b1": ((3, 1), (4, 2)),
        "b2": ((5, 1), (6, 2), (7, 3), (8, 4)),
        "cp": ((9, 3), (10, 4)),
        "c": ((11, 1), (12, 0)),
        "b3": ((13, 3), (14, 4), (15, 5), (16, 6), (17, 7)),
    }

    def pairs_for(a, ap, c, cp):
        return (
            (a, ap, 1, 2, slots["a"], slots["ap"]),
            ("e1", c, 0, 2, slots["e"], slots["c"]),
            ("b1", "b2", 1, 5, slots["b1"], slots["b2"]),
            (cp, "b3", 3, 8, slots["cp"], slots["b3"]),
        )

    near_pairs = pairs_for("al", "be", "ga", "de")
    far_pairs = pairs_for("be", "al", "de", "ga")
    for pairs, source, side, transposed in ((near_pairs, far, 0, True), (far_pairs, near, 1, False)):
        for one, two, first, final, slots_one, slots_two in pairs:
            feats = feat_ref[source, 16 * first : 16 * final, :]
            lhs = jnp.concatenate([feats, feats], axis=1)
            if transposed:
                rhs = jnp.concatenate(
                    [jnp.concatenate([w[one][s].T, w[two][s].T], axis=1) for s in range(2)], axis=0
                )
                out = mm(lhs, rhs)
            else:
                rhs = jnp.concatenate(
                    [jnp.concatenate([w[one][s], w[two][s]], axis=1) for s in range(2)], axis=0
                )
                out = mm(lhs, rhs)
            for half, targets in enumerate((slots_one, slots_two)):
                lanes = slice(128 * half, 128 * half + 128)
                for slot, group in targets:
                    at = 16 * (group - first)
                    add(side, slot, out[at : at + 8, lanes] + out[at + 8 : at + 16, lanes])


def finish_sums(load, f):
    x, q, d, quad = f["x"], f["q"], f["d"], f["quad"]
    turned = f["turned"]
    a_one, a_x = load(0, 0), [load(0, 1 + r) for r in range(3)]
    ap_d = [load(1, 5 + r) for r in range(3)]
    e_one, e_x = load(2, 0), [load(2, 1 + r) for r in range(3)]
    b1_q, b1_d = load(3, 4), [load(3, 5 + r) for r in range(3)]
    b1_qx = [load(4, r) for r in range(3)]
    b2_q, b2_m = load(5, 4), [load(6, 3 + r) for r in range(3)]

    def wide(slot):
        flat = lambda n: load(slot + n // 8, n % 8)
        return [flat(e) for e in range(6)], [flat(6 + r) for r in range(3)]

    b2_quad, b2_t = wide(7)
    b2_h = [load(7 + (9 + e) // 8, (9 + e) % 8) for e in range(6)]
    cp_quad, cp_t = wide(9)
    c_one, c_x = load(11, 0), [load(11, 1 + r) for r in range(3)]
    c_xx = [load(12, e) for e in range(6)]
    b3_quad, b3_t = wide(13)
    b3_tx = [load(15, e) for e in range(6)]
    b3_outer = [[load(15 + (6 + 3 * e + c) // 8, (6 + 3 * e + c) % 8) for c in range(3)] for e in range(6)]

    b2_quad_x = mat_vec(b2_quad, x)
    b3_quad_x = mat_vec(b3_quad, x)
    cp_quad_x = mat_vec(cp_quad, x)
    b2_turn = [b2_t[r] - b2_quad_x[r] for r in range(3)]
    b3_turn = [b3_t[r] - b3_quad_x[r] for r in range(3)]
    cp_turn = [cp_t[r] - cp_quad_x[r] for r in range(3)]
    b1_r = [b1_qx[r] - x[r] * b1_q for r in range(3)]
    a_r = [a_x[r] - x[r] * a_one for r in range(3)]
    e_r = [e_x[r] - x[r] * e_one for r in range(3)]
    c_r = [c_x[r] - x[r] * c_one for r in range(3)]
    b2_r = [b2_m[r] - x[r] * b2_q for r in range(3)]

    slope_d = [a_r[r] + b1_r[r] + b1_d[r] - 6.0 * b2_turn[r] for r in range(3)]

    sx_c = sym_outer(c_x, x)
    sx_m = sym_outer(b2_m, x)
    sx_t = sym_outer(b3_t, x)
    sx_q = sym_outer(b3_quad_x, x)
    mixed = [
        [sum_list([b3_outer[ENTRY_AT[(a, c)]][b] * x[c] for c in range(3)]) for b in range(3)] for a in range(3)
    ]
    slope_q = []
    for e, (a, b) in enumerate(ENTRIES):
        ym = mixed[a][b] if a == b else 0.5 * (mixed[a][b] + mixed[b][a])
        slope_q.append(
            5.0 * (c_xx[e] - 2.0 * sx_c[e] + c_one * f["xx"][e])
            + 3.0 * (b2_h[e] - 2.0 * sx_m[e] + b2_q * f["xx"][e])
            + 6.0 * b2_quad[e]
            - 60.0 * (b3_tx[e] - sx_t[e] - ym + sx_q[e])
        )

    inner = [10.0 * c_r[r] + 6.0 * b2_r[r] - 60.0 * b3_turn[r] for r in range(3)]
    inner = mat_vec(quad, inner)
    b2_quad_d = mat_vec(b2_quad, d)
    b3_quad_t = mat_vec(b3_quad, turned)
    force = []
    for a in range(3):
        spun = sum_list(
            [
                b3_outer[ENTRY_AT[(a, b)]][c] * quad[ENTRY_AT[(b, c)]]
                for b in range(3)
                for c in range(3)
            ]
        )
        force.append(
            -q * (b1_r[a] + b1_d[a])
            - (5.0 / 3.0) * e_r[a]
            + d[a] * (a_one + b1_q)
            - ap_d[a]
            + inner[a]
            + 10.0 * cp_turn[a]
            + 6.0 * q * b2_turn[a]
            - 6.0 * b2_quad_d[a]
            - 60.0 * (spun - b3_quad_t[a])
        )

    full = lambda m, r, c: m[ENTRY_AT[(r, c)]]

    def commutator(r, c):
        return sum_list(
            [full(quad, r, k) * full(slope_q, k, c) - full(slope_q, r, k) * full(quad, k, c) for k in range(3)]
        )

    twist = cross3(d, slope_d)
    torque = [
        2.0 * commutator(2, 1) - twist[0],
        2.0 * commutator(0, 2) - twist[1],
        2.0 * commutator(1, 0) - twist[2],
    ]
    return force, torque


def gather_exports(coords_ref, mult_ref, face_ref, send_ref):
    face = jnp.concatenate([face_ref[k] for k in range(3)] + [jnp.zeros((4, 128), jnp.int32)], axis=0)
    shift = lax.broadcasted_iota(jnp.int32, (16, 128), 0)
    shift_x = jnp.where((shift < 4) | (shift >= 8), 1.0, 0.0).astype(F32)
    shift_y = jnp.where(shift >= 4, 1.0, 0.0).astype(F32)
    halves = [face[0:8], face[8:16]]
    lows = [h & 127 for h in halves]
    highs = [h >> 7 for h in halves]
    for c in range(13):
        src, at = (coords_ref, 8 * c) if c < 3 else (mult_ref, 8 * (c - 3))
        got = []
        for part in range(2):
            total = jnp.zeros((8, 128), F32)
            for b in range(OWN_BLOCKS):
                picked = lane_gather(src[at + b : at + b + 1, :], lows[part])
                total = jnp.where(highs[part] == b, picked, total)
            got.append(total)
        rows = jnp.concatenate(got, axis=0)
        if c == 0:
            rows = rows + shift_x
        if c == 1:
            rows = rows + shift_y
        for k in range(3):
            send_ref[k, 4 * c : 4 * c + 4, :] = rows[4 * k : 4 * k + 4]
    for k in range(3):
        send_ref[k, 52:56, :] = jnp.zeros((4, 128), F32)


def event_tables(pairs_ref, table_ref):
    lane = lax.broadcasted_iota(jnp.int32, (8, 128), 1)
    blocks = [pairs_ref[0, 0, e % 2, e // 2] for e in range(EVENTS)]
    row = jnp.zeros((8, 128), jnp.int32)
    for e, block in enumerate(blocks):
        row = jnp.where(lane == e, block, row)
    before = jnp.full((8, 128), EVENTS, jnp.int32)
    last = jnp.full((8, 128), EVENTS, jnp.int32)
    for e, block in enumerate(blocks):
        before = jnp.where((row == block) & (lane > e), e, before)
        last = jnp.where(lane == block, e, last)
    sub = lax.broadcasted_iota(jnp.int32, (8, 128), 0)
    table_ref[...] = jnp.where(sub == 0, before, last)


def scatter_sets(back_ref, comps, sets, blocks, lanes):
    chosen = [(k, j) for k in sets for j in range(4)]
    values = [[back_ref[k, 4 * c + j : 4 * c + j + 1, :] for k, j in chosen] for c in range(comps)]
    return scatter_faces(values, [blocks[4 * k + j] for k, j in chosen], [lanes[4 * k + j] for k, j in chosen])


def kernel_body(
    sizes, coords_hbm, mult_hbm, face_hbm, frame_hbm, pairs_hbm, count_hbm, out_ref,
    coords_ref, mult_ref, face_ref, frame_ref, pairs_ref, count_ref, load_sem, send_ref, import_ref, halo_ref, back_ref, spread_ref, last_ref, table_ref, smem_ref,
    pool_ref, sum_scr, row_scr, col_scr, feat_ref, row_ref, col_ref, place_ref, wide_ref, keep_ref, runs_ref, acc_ref,
    send_sem, recv_sem, back_send, back_recv, last_send, last_recv, local_sem,
):
    up, down = neighbours(sizes)
    greet(up)
    loads = [
        pltpu.make_async_copy(source, target, load_sem.at[n])
        for n, (source, target) in enumerate(
            (
                (coords_hbm, coords_ref),
                (mult_hbm, mult_ref),
                (face_hbm, face_ref),
                (frame_hbm, frame_ref),
                (pairs_hbm, pairs_ref),
                (count_hbm, count_ref),
            )
        )
    ]
    for copy in loads:
        copy.start()
    for copy in loads[:3]:
        copy.wait()
    gather_exports(coords_ref, mult_ref, face_ref, send_ref)
    pl.semaphore_wait(pltpu.get_barrier_semaphore(), 3)
    copies = send_sets(send_ref, import_ref, send_sem, recv_sem, down)

    for copy in loads[3:]:
        copy.wait()
    event_tables(pairs_ref, table_ref)
    table_copy = pltpu.make_async_copy(table_ref, smem_ref, local_sem)
    table_copy.start()
    own = [coords_ref[8 * c : 8 * c + 8, :] for c in range(3)] + [mult_ref[8 * c : 8 * c + 8, :] for c in range(10)]
    for c in range(13):
        pool_ref[c, 0:8, :] = own[c]
        pool_ref[c, 20:24, :] = jnp.zeros((4, 128), F32)
    f = store_rows(own, 0, 8, sum_scr, col_scr)
    for n, row in enumerate([row for group in coefficient_rows(f) for row in group]):
        row_scr[n * 8 : n * 8 + 8, :] = row
    above = lax.broadcasted_iota(jnp.int32, (128, 128), 0) < lax.broadcasted_iota(jnp.int32, (128, 128), 1)
    keep_ref[0] = jnp.ones((128, 128), F32)
    keep_ref[1] = jnp.where(above, 1.0, 0.0).astype(F32)
    keep_ref[2] = jnp.zeros((128, 128), F32)
    runs_ref[EVENTS] = jnp.zeros((ACC_GROUPS, 8, 128), F32)
    for b in range(POOL_BLOCKS, ROWS):
        acc_ref[b * 8 * ACC_GROUPS : (b + 1) * 8 * ACC_GROUPS, :] = jnp.zeros((8 * ACC_GROUPS, 128), F32)

    def own_block(b, _):
        pool_block(b, sum_scr, col_scr, feat_ref, col_ref, place_ref)
        own_rows(b, row_scr, row_ref, place_ref, wide_ref)
        return 0

    lax.fori_loop(0, OWN_BLOCKS, own_block, 0, unroll=4)
    table_copy.wait()

    def import_block(b, _):
        pool_block(b, sum_scr, col_scr, feat_ref, col_ref, place_ref)
        return 0

    for sets, rows, blocks in (((0, 1), (8, 16), (8, 16)), ((2,), (16, 24), (16, 20))):
        for k in sets:
            copies[k].wait()
        for c in range(13):
            for k in sets:
                pool_ref[c, 8 + 4 * k : 12 + 4 * k, :] = import_ref[k, 4 * c : 4 * c + 4, :]
        store_rows([pool_ref[c] for c in range(13)], *rows, sum_scr, col_scr)
        lax.fori_loop(*blocks, import_block, 0, unroll=4)

    def one(t):
        near, far = pairs_ref[0, 0, 0, t], pairs_ref[0, 0, 1, t]
        keep = jnp.where(t < count_ref[0, 0], jnp.where(near == far, 1, 0), 2)
        return t, near, far, tile_work(near, far, row_ref, col_ref, place_ref, wide_ref, keep_ref, keep)

    def sums(t, near, far, w):
        before = [smem_ref[0, 2 * t + side] for side in range(2)]

        def add(side, slot, value):
            runs_ref[2 * t + side, slot] = runs_ref[before[side], slot] + value

        tile_sums(w, near, far, feat_ref, add)

    def step(g, _):
        held = None
        for n in range(TILE_STEP):
            current = one(TILE_STEP * g + n)
            if held is not None:
                sums(*held)
            held = current
        sums(*held)
        return 0

    lax.fori_loop(0, EVENTS // 2 // TILE_STEP, step, 0)

    def finish(low, high):
        for b in range(low, min(high, POOL_BLOCKS)):
            at = smem_ref[1, b]
            for slot in range(ACC_GROUPS):
                row = (b * ACC_GROUPS + slot) * 8
                acc_ref[row : row + 8, :] = runs_ref[at, slot]

        def load(slot, row):
            at = low * 8 * ACC_GROUPS + 8 * slot + row
            return acc_ref[pl.ds(at, high - low, stride=8 * ACC_GROUPS), :]

        force, torque = finish_sums(load, pool_features([pool_ref[c, low:high, :] for c in range(13)]))
        return force + torque

    copies = {}
    for sets, low in (((2,), 16), ((0, 1), 8)):
        for c, rows in enumerate(finish(low, low + 8)):
            for n, k in enumerate(sets):
                halo_ref[k, 4 * c : 4 * c + 4, :] = rows[4 * n : 4 * n + 4]
        copies.update(send_sets(halo_ref, back_ref, back_send, back_recv, up, sets))
    partial = finish(0, 8)

    blocks, lanes = face_masks([face_ref[k, j : j + 1, :] for k in range(3) for j in range(4)])
    index = [frame_ref[8 * m : 8 * m + 8, :] for m in range(3)]
    low = [i & 127 for i in index]
    high = [i >> 7 for i in index]
    spots = [[jnp.zeros((8, 128), F32) for _ in range(3)] for _ in range(3)]
    for b in range(POOL_BLOCKS):
        for c in range(3):
            row = pool_ref[c, b : b + 1, :]
            for m in range(3):
                spots[m][c] = jnp.where(high[m] == b, lane_gather(row, low[m]), spots[m][c])
    levers, scales = [], []
    for m in range(3):
        lever = [spots[m][c] - own[c] for c in range(3)]
        levers.append(lever)
        scales.append(1.0 / (3.0 * (dot3(lever, lever) + LEVER_SOFT)))
    sub24 = lax.broadcasted_iota(jnp.int32, (ROWS, 128), 0)
    sub128 = lax.broadcasted_iota(jnp.int32, (128, 128), 0)
    hits, hot = [], []
    for m in range(3):
        for b in range(OWN_BLOCKS):
            hits.append(jnp.broadcast_to(high[m][b : b + 1], (ROWS, 128)) == sub24)
            lane = jnp.broadcast_to(low[m][b : b + 1], (128, 128)) == sub128
            hot.append(jnp.where(lane, 1.0, 0.0).astype(BF16))

    owned = partial
    for sets in ((0, 1), (2,)):
        for k in sets:
            copies[k].wait()
        added = scatter_sets(back_ref, 6, sets, blocks, lanes)
        owned = [rows + more for rows, more in zip(owned, added)]
    torque = owned[3:6]
    kept = [jnp.zeros((8, 128), F32) for _ in range(3)]
    columns = []
    for m in range(3):
        push = [w * scales[m] for w in cross3(torque, levers[m])]
        kept = [kept[c] + push[c] for c in range(3)]
        halves = [split2(w) for w in push]
        for b in range(OWN_BLOCKS):
            hit = hits[8 * m + b]
            parts = []
            for c in range(3):
                for half in halves[c]:
                    parts.append(jnp.where(hit, jnp.broadcast_to(half[b : b + 1], (ROWS, 128)), 0.0))
            columns.append(jnp.concatenate(parts, axis=0).astype(BF16))
    out = nt_dot(jnp.concatenate(columns, axis=1), jnp.concatenate(hot, axis=1))
    forces = []
    for c in range(3):
        rows = out[48 * c : 48 * c + 24] + out[48 * c + 24 : 48 * c + 48]
        forces.append(owned[c] + rows[0:8] - kept[c])
        for k in range(3):
            spread_ref[k, 4 * c : 4 * c + 4, :] = rows[8 + 4 * k : 12 + 4 * k]
    spread_ref[:, 12:16, :] = jnp.zeros((3, 4, 128), F32)
    copies = send_sets(spread_ref, last_ref, last_send, last_recv, up)
    for sets in ((0, 1), (2,)):
        for k in sets:
            copies[k].wait()
        added = scatter_sets(last_ref, 3, sets, blocks, lanes)
        forces = [rows + more for rows, more in zip(forces, added)]
    for c in range(3):
        out_ref[8 * c : 8 * c + 8, :] = forces[c]


def domain_forces(sizes, coords, multipoles, face_atoms, frame_atoms, tile_pairs, tile_count):
    vmem = pl.BlockSpec(memory_space=pltpu.VMEM)
    hbm = pl.BlockSpec(memory_space=pltpu.HBM)
    return pl.pallas_call(
        functools.partial(kernel_body, sizes),
        out_shape=jax.ShapeDtypeStruct((24, 128), F32),
        in_specs=[hbm] * 6,
        out_specs=vmem,
        scratch_shapes=[
            pltpu.VMEM((24, 128), F32),
            pltpu.VMEM((80, 128), F32),
            pltpu.VMEM((3, 4, 128), jnp.int32),
            pltpu.VMEM((24, 128), jnp.int32),
            pltpu.SMEM((1, 1, 2, 32), jnp.int32),
            pltpu.SMEM((1, 1), jnp.int32),
            pltpu.SemaphoreType.DMA((6,)),
            pltpu.VMEM((3, 56, 128), F32),
            pltpu.VMEM((3, 56, 128), F32),
            pltpu.VMEM((3, 24, 128), F32),
            pltpu.VMEM((3, 24, 128), F32),
            pltpu.VMEM((3, 16, 128), F32),
            pltpu.VMEM((3, 16, 128), F32),
            pltpu.VMEM((8, 128), jnp.int32),
            pltpu.SMEM((8, 128), jnp.int32),
            pltpu.VMEM((13, ROWS, 128), F32),
            pltpu.VMEM((64 * ROWS, 128), F32),
            pltpu.VMEM((184 * 8, 128), F32),
            pltpu.VMEM((88 * ROWS, 128), F32),
            pltpu.VMEM((POOL_BLOCKS, 128, 128), BF16),
            pltpu.VMEM((OWN_BLOCKS, 896, 128), BF16),
            pltpu.VMEM((POOL_BLOCKS, 3, 128, 128), BF16),
            pltpu.VMEM((POOL_BLOCKS, 8, 128), F32),
            pltpu.VMEM((OWN_BLOCKS, 3, 128, 128), F32),
            pltpu.VMEM((3, 128, 128), F32),
            pltpu.VMEM((EVENTS + 1, ACC_GROUPS, 8, 128), F32),
            pltpu.VMEM((ROWS * 8 * ACC_GROUPS, 128), F32),
        ]
        + [pltpu.SemaphoreType.DMA((3,))] * 6
        + [pltpu.SemaphoreType.DMA],
        compiler_params=pltpu.CompilerParams(collective_id=0, has_side_effects=True, vmem_limit_bytes=52 << 20),
    )(*[pltpu.with_memory_space_constraint(a, pltpu.HBM) for a in (coords, multipoles, face_atoms, frame_atoms, tile_pairs)], tile_count)


def solution(mesh):
    sizes = (mesh.shape["gx"], mesh.shape["gy"])

    def shards(coords, multipoles, face_atoms, tile_pairs, tile_count, frame_atoms, send_list, send_count):
        coords = coords.reshape(24, 128)
        multipoles = multipoles.reshape(80, 128)
        face_atoms = face_atoms.reshape(3, 4, 128)
        frame_atoms = frame_atoms.reshape(24, 128)
        forces = domain_forces(sizes, coords, multipoles, face_atoms, frame_atoms, tile_pairs, tile_count)
        return forces.reshape(1, 1, 3, 1024)

    four = P("gx", "gy", None, None)
    placed = (four, four, four, four, P("gx", "gy"), four, four, P("gx", "gy", None))
    return jax.shard_map(shards, mesh=mesh, in_specs=placed, out_specs=four, check_vma=False)
```

```python
import functools

import jax
import jax.numpy as jnp
from jax import lax
from jax.experimental import pallas as pl
from jax.experimental.pallas import tpu as pltpu
from jax.sharding import PartitionSpec as P

SOFTENING = 0.5
LEVER_SOFT = 0.04
OWN_BLOCKS = 8
POOL_BLOCKS = 20
ROWS = 24
ENTRIES = ((0, 0), (1, 1), (2, 2), (0, 1), (0, 2), (1, 2))
ENTRY_AT = {(0, 0): 0, (1, 1): 1, (2, 2): 2, (0, 1): 3, (1, 0): 3, (0, 2): 4, (2, 0): 4, (1, 2): 5, (2, 1): 5}
MULT = (1.0, 1.0, 1.0, 2.0, 2.0, 2.0)
F32 = jnp.float32
BF16 = jnp.bfloat16
ACC_GROUPS = 18
EVENTS = 64
TILE_STEP = 32
MESH = pl.DeviceIdType.MESH


def cross3(a, b):
    return (a[1] * b[2] - a[2] * b[1], a[2] * b[0] - a[0] * b[2], a[0] * b[1] - a[1] * b[0])


def dot3(a, b):
    return a[0] * b[0] + a[1] * b[1] + a[2] * b[2]


def mat_vec(m, v):
    return [sum_list([m[ENTRY_AT[(r, c)]] * v[c] for c in range(3)]) for r in range(3)]


def sum_list(items):
    total = items[0]
    for item in items[1:]:
        total = total + item
    return total


def sym_outer(a, b):
    out = []
    for r, c in ENTRIES:
        if r == c:
            out.append(a[r] * b[r])
        else:
            out.append(0.5 * (a[r] * b[c] + a[c] * b[r]))
    return out


def split2(value):
    hi = value.astype(BF16).astype(F32)
    lo = (value - hi).astype(BF16).astype(F32)
    return hi, lo


def nt_dot(a, b):
    return lax.dot_general(a, b, (((1,), (1,)), ((), ())), preferred_element_type=F32)


def mm(a, b):
    return lax.dot_general(a, b, (((1,), (0,)), ((), ())), preferred_element_type=F32)


def lane_gather(row, index):
    table = jnp.broadcast_to(row, (8, 128))
    return jnp.take_along_axis(table, index, axis=1)


def face_masks(face_rows):
    sub8 = lax.broadcasted_iota(jnp.int32, (8, 128), 0)
    sub128 = lax.broadcasted_iota(jnp.int32, (128, 128), 0)
    blocks, lanes = [], []
    for row in face_rows:
        blocks.append(jnp.broadcast_to(row >> 7, (8, 128)) == sub8)
        hit = jnp.broadcast_to(row & 127, (128, 128)) == sub128
        lanes.append(jnp.where(hit, 1.0, 0.0).astype(BF16))
    return blocks, lanes


def scatter_faces(values, blocks, lanes):
    comps = len(values)
    columns = []
    for j in range(len(blocks)):
        parts = []
        for c in range(comps):
            hi, lo = split2(values[c][j])
            parts.append(jnp.where(blocks[j], jnp.broadcast_to(hi, (8, 128)), 0.0))
            parts.append(jnp.where(blocks[j], jnp.broadcast_to(lo, (8, 128)), 0.0))
        columns.append(jnp.concatenate(parts, axis=0).astype(BF16))
    lhs = jnp.concatenate(columns, axis=1)
    rhs = jnp.concatenate(lanes, axis=1)
    out = nt_dot(lhs, rhs)
    return [out[16 * c : 16 * c + 8] + out[16 * c + 8 : 16 * c + 16] for c in range(comps)]


def neighbours(sizes):
    gx, gy = lax.axis_index("gx"), lax.axis_index("gy")
    nx, ny = sizes
    up = (lax.rem(gx + 1, nx), lax.rem(gy + 1, ny))
    down = (lax.rem(gx + nx - 1, nx), lax.rem(gy + ny - 1, ny))
    return [[(to[0], gy), (gx, to[1]), (to[0], to[1])] for to in (up, down)]


def greet(senders):
    for peer in senders:
        pl.semaphore_signal(pltpu.get_barrier_semaphore(), inc=1, device_id=peer, device_id_type=MESH)


def send_sets(send_ref, recv_ref, send_sem, recv_sem, targets, sets=(2, 0, 1)):
    copies = {}
    for k in sets:
        copy = pltpu.make_async_remote_copy(
            src_ref=send_ref.at[k],
            dst_ref=recv_ref.at[k],
            send_sem=send_sem.at[k],
            recv_sem=recv_sem.at[k],
            device_id=targets[k],
            device_id_type=MESH,
        )
        copy.start()
        copies[k] = copy
    return copies


def pool_features(pool):
    x = [pool[0] - 1.0, pool[1] - 1.0, pool[2] - 0.5]
    q = pool[3]
    d = [pool[4], pool[5], pool[6]]
    quad = [pool[7], pool[8], pool[9], pool[10], pool[11], pool[12]]
    one = jnp.ones_like(q)
    xx = [x[r] * x[c] for r, c in ENTRIES]
    qx = [q * x[r] for r in range(3)]
    m = [qx[r] + d[r] for r in range(3)]
    turned = mat_vec(quad, x)
    dx = dot3(d, x)
    xqx = dot3(x, turned)
    sdx = sym_outer(d, x)
    h = [q * xx[e] + 2.0 * sdx[e] for e in range(6)]
    tx = sym_outer(turned, x)
    outer = [[quad[e] * x[c] for c in range(3)] for e in range(6)]
    return dict(one=one, x=x, q=q, d=d, quad=quad, xx=xx, qx=qx, m=m, turned=turned, dx=dx, xqx=xqx, h=h, tx=tx, outer=outer)


def sum_rows(f):
    zero = jnp.zeros_like(f["one"])
    rows = [*f["xx"], zero, zero]
    rows += [f["one"], *f["x"], f["q"], *f["d"]]
    rows += [*f["qx"], *f["m"], zero, zero]
    rows += [*f["quad"], *f["turned"], *f["h"], zero]
    rows += [*f["tx"]] + [f["outer"][e][c] for e in range(6) for c in range(3)]
    return rows


def column_rows(f):
    zero = jnp.zeros_like(f["one"])
    first = [*f["d"], f["dx"], *f["quad"], *f["turned"], f["xqx"], f["one"], *f["x"], *f["xx"]]
    second = [*f["d"], f["dx"], f["q"], *f["qx"], *f["quad"], *f["turned"], f["xqx"], *f["h"]]
    third = [*f["quad"], *f["turned"], *f["tx"]] + [f["outer"][e][c] for e in range(6) for c in range(3)]
    return first + second + third + [zero] * 7


def coefficient_rows(f):
    zero = jnp.zeros_like(f["one"])
    one = f["one"]
    x, d, q, xx = f["x"], f["d"], f["q"], f["xx"]
    quad, turned = f["quad"], f["turned"]
    z = lambda n: [zero] * n
    u = [-3.0 * x[r] for r in range(3)] + [3.0 * one] + z(20)
    v = z(14) + [-3.0 * f["dx"]] + [3.0 * d[r] for r in range(3)] + z(6)
    p = z(4) + [15.0 * MULT[e] * xx[e] for e in range(6)] + [-30.0 * x[r] for r in range(3)] + [15.0 * one] + z(10)
    r_ = (
        z(14)
        + [15.0 * f["xqx"]]
        + [-30.0 * turned[r] for r in range(3)]
        + [15.0 * MULT[e] * quad[e] for e in range(6)]
    )
    l1 = [1.8 * f["m"][r] for r in range(3)] + [-1.8 * q, -1.8 * f["dx"]] + [1.8 * d[r] for r in range(3)]
    l1 += z(16)
    l2 = (
        [-18.0 * turned[r] for r in range(3)]
        + z(1)
        + [9.0 * f["xqx"]]
        + [-18.0 * turned[r] for r in range(3)]
        + [9.0 * MULT[e] * (f["h"][e] + 2.0 * quad[e]) for e in range(6)]
        + [-18.0 * f["m"][r] for r in range(3)]
        + [9.0 * q]
        + [9.0 * MULT[e] * quad[e] for e in range(6)]
    )
    l3 = [-252.0 * MULT[e] * f["tx"][e] for e in range(6)] + [252.0 * turned[r] for r in range(3)]
    l3 += [-252.0 * MULT[e] * quad[e] for e in range(6)]
    for a, b in ENTRIES:
        for c in range(3):
            term = quad[ENTRY_AT[(a, c)]] * x[b]
            if a != b:
                term = term + quad[ENTRY_AT[(b, c)]] * x[a]
            l3.append(252.0 * term)
    l3 += z(7)
    return [u, v, p, r_, l1, l2, l3]


def pool_block(b, sum_scr, col_scr, feat_ref, col_ref, place_ref):
    sums = sum_scr[pl.ds(b, 64, stride=ROWS), :]
    place_ref[b] = sums[8:16]
    hi, lo = split2(sums)
    parts = []
    for g in range(8):
        parts += [hi[8 * g : 8 * g + 8], lo[8 * g : 8 * g + 8]]
    feat_ref[b] = jnp.concatenate(parts, axis=0).astype(BF16)
    start = 0
    for group, count in enumerate((24, 24, 40)):
        rows = col_scr[pl.ds(b + start * ROWS, count, stride=ROWS), :]
        start += count
        hi, lo = split2(rows)
        stacked = jnp.concatenate([hi, hi, lo, jnp.zeros((128 - 3 * count, 128), F32)], axis=0)
        col_ref[b, group] = stacked.astype(BF16)


def own_rows(b, row_scr, row_ref, place_ref, wide_ref):
    start = 0
    for out_id, count in enumerate((24, 24, 24, 24, 24, 24, 40)):
        rows = row_scr[pl.ds(b + start * 8, count, stride=8), :]
        start += count
        hi, lo = split2(rows)
        pad = [jnp.zeros((128 - 3 * count, 128), F32)]
        stacked = jnp.concatenate([hi, lo, hi] + pad, axis=0).astype(BF16)
        row_ref[b, out_id * 128 : (out_id + 1) * 128, :] = stacked.T
    place = jnp.concatenate([place_ref[b], jnp.zeros((120, 128), F32)], axis=0).T
    for r in range(3):
        wide_ref[b, r] = jnp.broadcast_to(place[:, r + 1 : r + 2], (128, 128))


def store_rows(pool, low, high, sum_scr, col_scr):
    f = pool_features([pool[c][low:high] for c in range(13)])
    for n, row in enumerate(sum_rows(f)):
        sum_scr[n * ROWS + low : n * ROWS + high, :] = row
    for n, row in enumerate(column_rows(f)):
        col_scr[n * ROWS + low : n * ROWS + high, :] = row
    return f


def tile_work(near, far, row_ref, col_ref, place_ref, wide_ref, keep_ref, keep):
    first = mm(row_ref[near, 0:512, :], col_ref[far, 0])
    second = mm(row_ref[near, 512:768, :], col_ref[far, 1])
    third = mm(row_ref[near, 768:896, :], col_ref[far, 2])
    chunk = 32
    names = ("b1", "b2", "b3", "al", "be", "ga", "de", "e1")
    pieces = {name: ([], []) for name in names}
    place = [jnp.broadcast_to(place_ref[far, r + 1 : r + 2, :], (chunk, 128)) for r in range(3)]
    for row in range(0, 128, chunk):
        rows = slice(row, row + chunk)
        diff = [place[r] - wide_ref[near, r, rows, :] for r in range(3)]
        dist = diff[0] * diff[0] + (diff[1] * diff[1] + (diff[2] * diff[2] + SOFTENING))
        root = lax.rsqrt(dist)
        t = root * root
        b0 = root * keep_ref[keep, rows, :]
        b1 = b0 * t
        b2 = b1 * t
        b3 = b2 * t
        v, u, r_, p = [first[n * 128 + row : n * 128 + row + chunk] for n in range(4)]
        rt, pt = r_ * t, p * t
        l1, l2 = [second[n * 128 + row : n * 128 + row + chunk] for n in range(2)]
        l3 = third[rows]
        gr, gp = 1.4 * rt - v, 1.4 * pt + u
        al = b2 * (rt - v)
        be = b2 * (pt + u)
        ga = b3 * gr
        de = b3 * gp
        e1 = b2 * (l1 + t * (l2 + gr * gp + 0.56 * (rt * pt) + t * l3))
        for name, value in zip(names, (b1, b2, b3, al, be, ga, de, e1)):
            hi = value.astype(BF16)
            pieces[name][0].append(hi)
            pieces[name][1].append((value - hi.astype(F32)).astype(BF16))
    return {name: (jnp.concatenate(h, axis=0), jnp.concatenate(l, axis=0)) for name, (h, l) in pieces.items()}


def tile_sums(w, near, far, feat_ref, add):
    slots = {
        "a": ((0, 1),),
        "ap": ((1, 1),),
        "e": ((2, 1),),
        "b1": ((3, 1), (4, 2)),
        "b2": ((5, 1), (6, 2), (7, 3), (8, 4)),
        "cp": ((9, 3), (10, 4)),
        "c": ((11, 1), (12, 0)),
        "b3": ((13, 3), (14, 4), (15, 5), (16, 6), (17, 7)),
    }

    def pairs_for(a, ap, c, cp):
        return (
            (a, ap, 1, 2, slots["a"], slots["ap"]),
            ("e1", c, 0, 2, slots["e"], slots["c"]),
            ("b1", "b2", 1, 5, slots["b1"], slots["b2"]),
            (cp, "b3", 3, 8, slots["cp"], slots["b3"]),
        )

    near_pairs = pairs_for("al", "be", "ga", "de")
    far_pairs = pairs_for("be", "al", "de", "ga")
    for pairs, source, side, transposed in ((near_pairs, far, 0, True), (far_pairs, near, 1, False)):
        for one, two, first, final, slots_one, slots_two in pairs:
            feats = feat_ref[source, 16 * first : 16 * final, :]
            lhs = jnp.concatenate([feats, feats], axis=1)
            if transposed:
                rhs = jnp.concatenate(
                    [jnp.concatenate([w[one][s].T, w[two][s].T], axis=1) for s in range(2)], axis=0
                )
                out = mm(lhs, rhs)
            else:
                rhs = jnp.concatenate(
                    [jnp.concatenate([w[one][s], w[two][s]], axis=1) for s in range(2)], axis=0
                )
                out = mm(lhs, rhs)
            for half, targets in enumerate((slots_one, slots_two)):
                lanes = slice(128 * half, 128 * half + 128)
                for slot, group in targets:
                    at = 16 * (group - first)
                    add(side, slot, out[at : at + 8, lanes] + out[at + 8 : at + 16, lanes])


def finish_sums(load, f):
    x, q, d, quad = f["x"], f["q"], f["d"], f["quad"]
    turned = f["turned"]
    a_one, a_x = load(0, 0), [load(0, 1 + r) for r in range(3)]
    ap_d = [load(1, 5 + r) for r in range(3)]
    e_one, e_x = load(2, 0), [load(2, 1 + r) for r in range(3)]
    b1_q, b1_d = load(3, 4), [load(3, 5 + r) for r in range(3)]
    b1_qx = [load(4, r) for r in range(3)]
    b2_q, b2_m = load(5, 4), [load(6, 3 + r) for r in range(3)]

    def wide(slot):
        flat = lambda n: load(slot + n // 8, n % 8)
        return [flat(e) for e in range(6)], [flat(6 + r) for r in range(3)]

    b2_quad, b2_t = wide(7)
    b2_h = [load(7 + (9 + e) // 8, (9 + e) % 8) for e in range(6)]
    cp_quad, cp_t = wide(9)
    c_one, c_x = load(11, 0), [load(11, 1 + r) for r in range(3)]
    c_xx = [load(12, e) for e in range(6)]
    b3_quad, b3_t = wide(13)
    b3_tx = [load(15, e) for e in range(6)]
    b3_outer = [[load(15 + (6 + 3 * e + c) // 8, (6 + 3 * e + c) % 8) for c in range(3)] for e in range(6)]

    b2_quad_x = mat_vec(b2_quad, x)
    b3_quad_x = mat_vec(b3_quad, x)
    cp_quad_x = mat_vec(cp_quad, x)
    b2_turn = [b2_t[r] - b2_quad_x[r] for r in range(3)]
    b3_turn = [b3_t[r] - b3_quad_x[r] for r in range(3)]
    cp_turn = [cp_t[r] - cp_quad_x[r] for r in range(3)]
    b1_r = [b1_qx[r] - x[r] * b1_q for r in range(3)]
    a_r = [a_x[r] - x[r] * a_one for r in range(3)]
    e_r = [e_x[r] - x[r] * e_one for r in range(3)]
    c_r = [c_x[r] - x[r] * c_one for r in range(3)]
    b2_r = [b2_m[r] - x[r] * b2_q for r in range(3)]

    slope_d = [a_r[r] + b1_r[r] + b1_d[r] - 6.0 * b2_turn[r] for r in range(3)]

    sx_c = sym_outer(c_x, x)
    sx_m = sym_outer(b2_m, x)
    sx_t = sym_outer(b3_t, x)
    sx_q = sym_outer(b3_quad_x, x)
    mixed = [
        [sum_list([b3_outer[ENTRY_AT[(a, c)]][b] * x[c] for c in range(3)]) for b in range(3)] for a in range(3)
    ]
    slope_q = []
    for e, (a, b) in enumerate(ENTRIES):
        ym = mixed[a][b] if a == b else 0.5 * (mixed[a][b] + mixed[b][a])
        slope_q.append(
            5.0 * (c_xx[e] - 2.0 * sx_c[e] + c_one * f["xx"][e])
            + 3.0 * (b2_h[e] - 2.0 * sx_m[e] + b2_q * f["xx"][e])
            + 6.0 * b2_quad[e]
            - 60.0 * (b3_tx[e] - sx_t[e] - ym + sx_q[e])
        )

    inner = [10.0 * c_r[r] + 6.0 * b2_r[r] - 60.0 * b3_turn[r] for r in range(3)]
    inner = mat_vec(quad, inner)
    b2_quad_d = mat_vec(b2_quad, d)
    b3_quad_t = mat_vec(b3_quad, turned)
    force = []
    for a in range(3):
        spun = sum_list(
            [
                b3_outer[ENTRY_AT[(a, b)]][c] * quad[ENTRY_AT[(b, c)]]
                for b in range(3)
                for c in range(3)
            ]
        )
        force.append(
            -q * (b1_r[a] + b1_d[a])
            - (5.0 / 3.0) * e_r[a]
            + d[a] * (a_one + b1_q)
            - ap_d[a]
            + inner[a]
            + 10.0 * cp_turn[a]
            + 6.0 * q * b2_turn[a]
            - 6.0 * b2_quad_d[a]
            - 60.0 * (spun - b3_quad_t[a])
        )

    full = lambda m, r, c: m[ENTRY_AT[(r, c)]]

    def commutator(r, c):
        return sum_list(
            [full(quad, r, k) * full(slope_q, k, c) - full(slope_q, r, k) * full(quad, k, c) for k in range(3)]
        )

    twist = cross3(d, slope_d)
    torque = [
        2.0 * commutator(2, 1) - twist[0],
        2.0 * commutator(0, 2) - twist[1],
        2.0 * commutator(1, 0) - twist[2],
    ]
    return force, torque


def gather_exports(coords_ref, mult_ref, face_ref, send_ref):
    face = jnp.concatenate([face_ref[k] for k in range(3)] + [jnp.zeros((4, 128), jnp.int32)], axis=0)
    shift = lax.broadcasted_iota(jnp.int32, (16, 128), 0)
    shift_x = jnp.where((shift < 4) | (shift >= 8), 1.0, 0.0).astype(F32)
    shift_y = jnp.where(shift >= 4, 1.0, 0.0).astype(F32)
    halves = [face[0:8], face[8:16]]
    lows = [h & 127 for h in halves]
    highs = [h >> 7 for h in halves]
    for c in range(13):
        src, at = (coords_ref, 8 * c) if c < 3 else (mult_ref, 8 * (c - 3))
        got = []
        for part in range(2):
            total = jnp.zeros((8, 128), F32)
            for b in range(OWN_BLOCKS):
                picked = lane_gather(src[at + b : at + b + 1, :], lows[part])
                total = jnp.where(highs[part] == b, picked, total)
            got.append(total)
        rows = jnp.concatenate(got, axis=0)
        if c == 0:
            rows = rows + shift_x
        if c == 1:
            rows = rows + shift_y
        for k in range(3):
            send_ref[k, 4 * c : 4 * c + 4, :] = rows[4 * k : 4 * k + 4]
    for k in range(3):
        send_ref[k, 52:56, :] = jnp.zeros((4, 128), F32)


def event_tables(pairs_ref, table_ref):
    lane = lax.broadcasted_iota(jnp.int32, (8, 128), 1)
    blocks = [pairs_ref[0, 0, e % 2, e // 2] for e in range(EVENTS)]
    row = jnp.zeros((8, 128), jnp.int32)
    for e, block in enumerate(blocks):
        row = jnp.where(lane == e, block, row)
    before = jnp.full((8, 128), EVENTS, jnp.int32)
    last = jnp.full((8, 128), EVENTS, jnp.int32)
    for e, block in enumerate(blocks):
        before = jnp.where((row == block) & (lane > e), e, before)
        last = jnp.where(lane == block, e, last)
    sub = lax.broadcasted_iota(jnp.int32, (8, 128), 0)
    table_ref[...] = jnp.where(sub == 0, before, last)


def scatter_sets(back_ref, comps, sets, blocks, lanes):
    chosen = [(k, j) for k in sets for j in range(4)]
    values = [[back_ref[k, 4 * c + j : 4 * c + j + 1, :] for k, j in chosen] for c in range(comps)]
    return scatter_faces(values, [blocks[4 * k + j] for k, j in chosen], [lanes[4 * k + j] for k, j in chosen])


def kernel_body(
    sizes, coords_hbm, mult_hbm, face_hbm, frame_hbm, pairs_hbm, count_hbm, out_ref,
    coords_ref, mult_ref, face_ref, frame_ref, pairs_ref, count_ref, load_sem, send_ref, import_ref, halo_ref, back_ref, spread_ref, last_ref, table_ref, smem_ref,
    pool_ref, sum_scr, row_scr, col_scr, feat_ref, row_ref, col_ref, place_ref, wide_ref, keep_ref, runs_ref, acc_ref,
    send_sem, recv_sem, back_send, back_recv, last_send, last_recv, local_sem,
):
    up, down = neighbours(sizes)
    greet(up)
    loads = [
        pltpu.make_async_copy(source, target, load_sem.at[n])
        for n, (source, target) in enumerate(
            (
                (coords_hbm, coords_ref),
                (mult_hbm, mult_ref),
                (face_hbm, face_ref),
                (frame_hbm, frame_ref),
                (pairs_hbm, pairs_ref),
                (count_hbm, count_ref),
            )
        )
    ]
    for copy in loads:
        copy.start()
    for copy in loads[:3]:
        copy.wait()
    gather_exports(coords_ref, mult_ref, face_ref, send_ref)
    pl.semaphore_wait(pltpu.get_barrier_semaphore(), 3)
    copies = send_sets(send_ref, import_ref, send_sem, recv_sem, down)

    for copy in loads[3:]:
        copy.wait()
    event_tables(pairs_ref, table_ref)
    table_copy = pltpu.make_async_copy(table_ref, smem_ref, local_sem)
    table_copy.start()
    own = [coords_ref[8 * c : 8 * c + 8, :] for c in range(3)] + [mult_ref[8 * c : 8 * c + 8, :] for c in range(10)]
    for c in range(13):
        pool_ref[c, 0:8, :] = own[c]
        pool_ref[c, 20:24, :] = jnp.zeros((4, 128), F32)
    f = store_rows(own, 0, 8, sum_scr, col_scr)
    for n, row in enumerate([row for group in coefficient_rows(f) for row in group]):
        row_scr[n * 8 : n * 8 + 8, :] = row
    above = lax.broadcasted_iota(jnp.int32, (128, 128), 0) < lax.broadcasted_iota(jnp.int32, (128, 128), 1)
    keep_ref[0] = jnp.ones((128, 128), F32)
    keep_ref[1] = jnp.where(above, 1.0, 0.0).astype(F32)
    keep_ref[2] = jnp.zeros((128, 128), F32)
    runs_ref[EVENTS] = jnp.zeros((ACC_GROUPS, 8, 128), F32)
    for b in range(POOL_BLOCKS, ROWS):
        acc_ref[b * 8 * ACC_GROUPS : (b + 1) * 8 * ACC_GROUPS, :] = jnp.zeros((8 * ACC_GROUPS, 128), F32)

    def own_block(b, _):
        pool_block(b, sum_scr, col_scr, feat_ref, col_ref, place_ref)
        own_rows(b, row_scr, row_ref, place_ref, wide_ref)
        return 0

    lax.fori_loop(0, OWN_BLOCKS, own_block, 0, unroll=8)
    table_copy.wait()

    def import_block(b, _):
        pool_block(b, sum_scr, col_scr, feat_ref, col_ref, place_ref)
        return 0

    for sets, rows, blocks in (((0, 1), (8, 16), (8, 16)), ((2,), (16, 24), (16, 20))):
        for k in sets:
            copies[k].wait()
        for c in range(13):
            for k in sets:
                pool_ref[c, 8 + 4 * k : 12 + 4 * k, :] = import_ref[k, 4 * c : 4 * c + 4, :]
        store_rows([pool_ref[c] for c in range(13)], *rows, sum_scr, col_scr)
        lax.fori_loop(*blocks, import_block, 0, unroll=blocks[1] - blocks[0])

    def one(t):
        near, far = pairs_ref[0, 0, 0, t], pairs_ref[0, 0, 1, t]
        keep = jnp.where(t < count_ref[0, 0], jnp.where(near == far, 1, 0), 2)
        return t, near, far, tile_work(near, far, row_ref, col_ref, place_ref, wide_ref, keep_ref, keep)

    def sums(t, near, far, w):
        before = [smem_ref[0, 2 * t + side] for side in range(2)]

        def add(side, slot, value):
            runs_ref[2 * t + side, slot] = runs_ref[before[side], slot] + value

        tile_sums(w, near, far, feat_ref, add)

    def step(g, _):
        held = None
        for n in range(TILE_STEP):
            current = one(TILE_STEP * g + n)
            if held is not None:
                sums(*held)
            held = current
        sums(*held)
        return 0

    lax.fori_loop(0, EVENTS // 2 // TILE_STEP, step, 0)

    def finish(low, high):
        for b in range(low, min(high, POOL_BLOCKS)):
            at = smem_ref[1, b]
            for slot in range(ACC_GROUPS):
                row = (b * ACC_GROUPS + slot) * 8
                acc_ref[row : row + 8, :] = runs_ref[at, slot]

        def load(slot, row):
            at = low * 8 * ACC_GROUPS + 8 * slot + row
            return acc_ref[pl.ds(at, high - low, stride=8 * ACC_GROUPS), :]

        force, torque = finish_sums(load, pool_features([pool_ref[c, low:high, :] for c in range(13)]))
        return force + torque

    copies = {}
    for sets, low in (((2,), 16), ((0, 1), 8)):
        for c, rows in enumerate(finish(low, low + 8)):
            for n, k in enumerate(sets):
                halo_ref[k, 4 * c : 4 * c + 4, :] = rows[4 * n : 4 * n + 4]
        copies.update(send_sets(halo_ref, back_ref, back_send, back_recv, up, sets))
    partial = finish(0, 8)

    blocks, lanes = face_masks([face_ref[k, j : j + 1, :] for k in range(3) for j in range(4)])
    index = [frame_ref[8 * m : 8 * m + 8, :] for m in range(3)]
    low = [i & 127 for i in index]
    high = [i >> 7 for i in index]
    spots = [[jnp.zeros((8, 128), F32) for _ in range(3)] for _ in range(3)]
    for b in range(POOL_BLOCKS):
        for c in range(3):
            row = pool_ref[c, b : b + 1, :]
            for m in range(3):
                spots[m][c] = jnp.where(high[m] == b, lane_gather(row, low[m]), spots[m][c])
    levers, scales = [], []
    for m in range(3):
        lever = [spots[m][c] - own[c] for c in range(3)]
        levers.append(lever)
        scales.append(1.0 / (3.0 * (dot3(lever, lever) + LEVER_SOFT)))
    sub24 = lax.broadcasted_iota(jnp.int32, (ROWS, 128), 0)
    sub128 = lax.broadcasted_iota(jnp.int32, (128, 128), 0)
    hits, hot = [], []
    for m in range(3):
        for b in range(OWN_BLOCKS):
            hits.append(jnp.broadcast_to(high[m][b : b + 1], (ROWS, 128)) == sub24)
            lane = jnp.broadcast_to(low[m][b : b + 1], (128, 128)) == sub128
            hot.append(jnp.where(lane, 1.0, 0.0).astype(BF16))

    owned = partial
    for sets in ((0, 1), (2,)):
        for k in sets:
            copies[k].wait()
        added = scatter_sets(back_ref, 6, sets, blocks, lanes)
        owned = [rows + more for rows, more in zip(owned, added)]
    torque = owned[3:6]
    kept = [jnp.zeros((8, 128), F32) for _ in range(3)]
    columns = []
    for m in range(3):
        push = [w * scales[m] for w in cross3(torque, levers[m])]
        kept = [kept[c] + push[c] for c in range(3)]
        halves = [split2(w) for w in push]
        for b in range(OWN_BLOCKS):
            hit = hits[8 * m + b]
            parts = []
            for c in range(3):
                for half in halves[c]:
                    parts.append(jnp.where(hit, jnp.broadcast_to(half[b : b + 1], (ROWS, 128)), 0.0))
            columns.append(jnp.concatenate(parts, axis=0).astype(BF16))
    out = nt_dot(jnp.concatenate(columns, axis=1), jnp.concatenate(hot, axis=1))
    forces = []
    for c in range(3):
        rows = out[48 * c : 48 * c + 24] + out[48 * c + 24 : 48 * c + 48]
        forces.append(owned[c] + rows[0:8] - kept[c])
        for k in range(3):
            spread_ref[k, 4 * c : 4 * c + 4, :] = rows[8 + 4 * k : 12 + 4 * k]
    spread_ref[:, 12:16, :] = jnp.zeros((3, 4, 128), F32)
    copies = send_sets(spread_ref, last_ref, last_send, last_recv, up)
    for sets in ((0, 1), (2,)):
        for k in sets:
            copies[k].wait()
        added = scatter_sets(last_ref, 3, sets, blocks, lanes)
        forces = [rows + more for rows, more in zip(forces, added)]
    for c in range(3):
        out_ref[8 * c : 8 * c + 8, :] = forces[c]


def domain_forces(sizes, coords, multipoles, face_atoms, frame_atoms, tile_pairs, tile_count):
    vmem = pl.BlockSpec(memory_space=pltpu.VMEM)
    hbm = pl.BlockSpec(memory_space=pltpu.HBM)
    return pl.pallas_call(
        functools.partial(kernel_body, sizes),
        out_shape=jax.ShapeDtypeStruct((24, 128), F32),
        in_specs=[hbm] * 6,
        out_specs=vmem,
        scratch_shapes=[
            pltpu.VMEM((24, 128), F32),
            pltpu.VMEM((80, 128), F32),
            pltpu.VMEM((3, 4, 128), jnp.int32),
            pltpu.VMEM((24, 128), jnp.int32),
            pltpu.SMEM((1, 1, 2, 32), jnp.int32),
            pltpu.SMEM((1, 1), jnp.int32),
            pltpu.SemaphoreType.DMA((6,)),
            pltpu.VMEM((3, 56, 128), F32),
            pltpu.VMEM((3, 56, 128), F32),
            pltpu.VMEM((3, 24, 128), F32),
            pltpu.VMEM((3, 24, 128), F32),
            pltpu.VMEM((3, 16, 128), F32),
            pltpu.VMEM((3, 16, 128), F32),
            pltpu.VMEM((8, 128), jnp.int32),
            pltpu.SMEM((8, 128), jnp.int32),
            pltpu.VMEM((13, ROWS, 128), F32),
            pltpu.VMEM((64 * ROWS, 128), F32),
            pltpu.VMEM((184 * 8, 128), F32),
            pltpu.VMEM((88 * ROWS, 128), F32),
            pltpu.VMEM((POOL_BLOCKS, 128, 128), BF16),
            pltpu.VMEM((OWN_BLOCKS, 896, 128), BF16),
            pltpu.VMEM((POOL_BLOCKS, 3, 128, 128), BF16),
            pltpu.VMEM((POOL_BLOCKS, 8, 128), F32),
            pltpu.VMEM((OWN_BLOCKS, 3, 128, 128), F32),
            pltpu.VMEM((3, 128, 128), F32),
            pltpu.VMEM((EVENTS + 1, ACC_GROUPS, 8, 128), F32),
            pltpu.VMEM((ROWS * 8 * ACC_GROUPS, 128), F32),
        ]
        + [pltpu.SemaphoreType.DMA((3,))] * 6
        + [pltpu.SemaphoreType.DMA],
        compiler_params=pltpu.CompilerParams(collective_id=0, has_side_effects=True, vmem_limit_bytes=52 << 20),
    )(*[pltpu.with_memory_space_constraint(a, pltpu.HBM) for a in (coords, multipoles, face_atoms, frame_atoms, tile_pairs)], tile_count)


def solution(mesh):
    sizes = (mesh.shape["gx"], mesh.shape["gy"])

    def shards(coords, multipoles, face_atoms, tile_pairs, tile_count, frame_atoms, send_list, send_count):
        coords = coords.reshape(24, 128)
        multipoles = multipoles.reshape(80, 128)
        face_atoms = face_atoms.reshape(3, 4, 128)
        frame_atoms = frame_atoms.reshape(24, 128)
        forces = domain_forces(sizes, coords, multipoles, face_atoms, frame_atoms, tile_pairs, tile_count)
        return forces.reshape(1, 1, 3, 1024)

    four = P("gx", "gy", None, None)
    placed = (four, four, four, four, P("gx", "gy"), four, four, P("gx", "gy", None))
    return jax.shard_map(shards, mesh=mesh, in_specs=placed, out_specs=four, check_vma=False)
```
